32 devices in a mesh: dp: 4 (over y, x), expert: 4 (over z), tensor: 2 (over core).
Axes of the slice: x: 2, y: 2, z: 4, core: 2. Of those that a mesh axis runs over, the one named last changes fastest.
Arguments:
- tokens: bfloat16 [4096, 2048], P(('dp', 'expert'), 'tensor'), may hold values from -6 to 6
- norm_attn: float32 [2048], P('tensor'), may hold values from 0.5 to 1.5
- norm_mlp: float32 [2048], P('tensor'), may hold values from 0.5 to 1.5
- w_kv: float32 [2048, 2, 2048], P(('dp', 'expert'), None, 'tensor'), may hold values from -0.125 to 0.125
- router_attn: float32 [2048, 8], replicated, may hold values from -0.125 to 0.125
- router_mlp: float32 [2048, 8], replicated, may hold values from -0.125 to 0.125
- w_query: float32 [8, 2048, 2048], P('expert', 'dp', 'tensor'), may hold values from -0.125 to 0.125
- w_output: float32 [8, 2048, 2048], P('expert', 'tensor', 'dp'), may hold values from -0.5 to 0.5
- w_gateup: float32 [8, 2048, 2, 5632], P('expert', 'dp', None, 'tensor'), may hold values from -0.125 to 0.125
- w_down: float32 [8, 5632, 2048], P('expert', 'tensor', 'dp'), may hold values from -0.078125 to 0.078125
- segments: int32 [4096], P(('dp', 'expert')), may hold values from 0 to 127, never falling along the last dimension, each value on 1 to 1024 neighbouring positions
- att_routes: int32 [4096, 2], P(('dp', 'expert')), may hold values from 0 to 7, all different within a row; in each aligned block of 256 rows (0 to 255, 256 to 511, ...) at most 96 rows name the same one
- mlp_routes: int32 [4096, 2], P(('dp', 'expert')), may hold values from 0 to 7, all different within a row; in each aligned block of 256 rows (0 to 255, 256 to 511, ...) at most 96 rows name the same one
- cotangent: bfloat16 [4096, 2048], P(('dp', 'expert'), 'tensor'), may hold values from -6 to 6
Outputs:
- out: bfloat16 [4096, 2048], P(('dp', 'expert'), 'tensor')
- grad_tokens: float32 [4096, 2048], P(('dp', 'expert'), 'tensor')
- grad_norm_attn: float32 [2048], P('tensor')
- grad_norm_mlp: float32 [2048], P('tensor')
- grad_w_kv: float32 [2048, 2, 2048], P(('dp', 'expert'), None, 'tensor')
- grad_router_attn: float32 [2048, 8], replicated
- grad_router_mlp: float32 [2048, 8], replicated
- grad_w_query: float32 [8, 2048, 2048], P('expert', 'dp', 'tensor')
- grad_w_output: float32 [8, 2048, 2048], P('expert', 'tensor', 'dp')
- grad_w_gateup: float32 [8, 2048, 2, 5632], P('expert', 'dp', None, 'tensor')
- grad_w_down: float32 [8, 5632, 2048], P('expert', 'tensor', 'dp')
The draws below stay inside these ranges and needn't reach their ends.
Inputs may be any that keep to these rules, and one draw needn't show every extreme that they name: `segments`: document numbers never fall along the tokens; a document holds 1 to 1024 tokens and one holds exactly 1024; a document may continue across the end of a sequence, but attention never does. `att_routes`: each token names 2 different experts; the 256 tokens of one device name no expert more than 96 times, and on some device some expert exactly 96 times. `mlp_routes`: each token names 2 different experts; the 256 tokens of one device name no expert more than 96 times, and on some device some expert exactly 96 times.
All inputs are finite; a program needn't handle non-finite values.
Results may differ from the reference program's by a relative error of at most 0.018.
Values may be sent and summed in bfloat16 or wider, within the bound.
No kernel may reach another device: no remote copies, remote signals or barrier semaphores. Data moves between devices by JAX's collectives and lax.ppermute only.
A program may use at most 384 MiB of HBM per device.

```python
import math
import jax
import jax.numpy as jnp
import numpy as np
from jax import lax

D = 2048
HEADS = 16
HD = 128
E_ATT = 8
E_MLP = 8
TOP = 2
FF = 5632
TOK_DEV = 256
KVW = 2048
SEQ = 1024
TOKENS = 4096
CAP = 96


def shard_levels(key, shape, shards, low, top_value):
    level, own = 1.0, jax.random.fold_in(key, 6)
    for position, shards_of in shards:
        draws = jnp.exp(jax.random.uniform(jax.random.fold_in(own, position), (shards_of,), jnp.float32, low / len(shards), top_value / len(shards)))
        level = level * jnp.repeat(draws, shape[position] // shards_of).reshape([-1 if axis == position else 1 for axis in range(len(shape))])
    return level


def profile(number_of, total, bound, lean):
    portions = [(1 << 20) // math.isqrt(rank ** lean) + 1 for rank in range(2, number_of + 1)]
    rest, holding = total - bound - (number_of - 1), [1] * (number_of - 1)
    while rest > 0:
        movable = [i for i in range(number_of - 1) if holding[i] < bound]
        whole, budget = sum([portions[i] for i in movable]), rest
        for i in movable:
            addition = min(bound - holding[i], max(1, budget * portions[i] // whole), rest)
            holding[i] = holding[i] + addition
            rest = rest - addition
    return np.array([bound] + holding)


def uneven_parts(stream_key, amount, total, bound, slope):
    if amount == 2:
        one = jax.random.randint(stream_key, (), max(1, total - bound), min(bound, total - 1) + 1)
        return jnp.stack([one, total - one])
    tallies = jnp.asarray(profile(amount, total, bound, slope), jnp.int32)
    pairs = (amount - 1) // 2
    source_of, receiver = tallies[1:1 + 2 * pairs:2], tallies[2:2 + 2 * pairs:2]
    margin = jnp.minimum(source_of - 1, bound - receiver)
    passed = jax.random.randint(jax.random.fold_in(stream_key, 1), (pairs,), 0, 1 << 20) % (margin + 1)
    tallies = tallies.at[1:1 + 2 * pairs:2].set(source_of - passed).at[2:2 + 2 * pairs:2].set(receiver + passed)
    return tallies[jax.random.permutation(jax.random.fold_in(stream_key, 2), amount)]


def deal_out(own_key, own, number, rows, count, top, bound, skew):
    order = jax.random.permutation(own_key, count)
    heavy_load, common = load_shares(count, rows * top, bound, skew, True), load_shares(count, rows * top, bound, skew, False)
    places = jnp.arange(count)

    def named(tallies, offset_by):
        used = int((tallies > 0).sum())
        fixed = max(1, used // 4)
        moved = fixed + (places - fixed + offset_by * (used - fixed)) % max(1, count - fixed)
        return jnp.zeros((count,), jnp.int32).at[order[jnp.where(places < fixed, places, moved)]].set(jnp.asarray(tallies, jnp.int32))

    tallies = jnp.where(number % 4 == 0, named(heavy_load, number // 4), named(common, number - number // 4 - 1))
    mixed = jax.random.permutation(jax.random.fold_in(own, 3), count)
    giver, taker = mixed[0:count // 2 * 2:2], mixed[1:count // 2 * 2:2]
    margin = jnp.minimum(tallies[giver] - 1, bound - tallies[taker]) // 2
    margin = jnp.where((giver == order[0]) | (taker == order[0]) | (tallies[taker] == 0), 0, jnp.maximum(margin, 0))
    moved = jax.random.randint(jax.random.fold_in(own, 4), (count // 2,), 0, 1 << 20) % (margin + 1)
    tallies = tallies.at[giver].add(-moved).at[taker].add(moved)
    labels = jnp.searchsorted(jnp.cumsum(tallies), jnp.arange(rows * top), side="right").astype(jnp.int32)
    listing = labels.reshape(top, rows).T
    listing = listing[jax.random.permutation(jax.random.fold_in(own, 1), rows)]
    offset_by = jax.random.randint(jax.random.fold_in(own, 2), (rows, 1), 0, top)
    return jnp.take_along_axis(listing, (jnp.arange(top)[None, :] + offset_by) % top, axis=1)


def load_shares(number_of, total, reach, slope, full):
    weights = [(1 << 20) // math.isqrt(standing ** slope) + 1 for standing in range(1, number_of + 1)]
    largest = reach if full else min(reach, max(-(-total // number_of), total * weights[0] // sum(weights)))
    least = 1 if total - largest >= number_of - 1 else 0
    given, rest = [largest] + [least] * (number_of - 1), total - largest - least * (number_of - 1)
    while rest > 0:
        free = [i for i in range(1, number_of) if given[i] < largest] or [i for i in range(1, number_of) if given[i] < reach]
        pool, left = sum([weights[i] for i in free]), rest
        for i in free:
            extra = min(reach - given[i], max(1, left * weights[i] // pool), rest)
            given[i] = given[i] + extra
            rest = rest - extra
    return np.array(given)


def normal_values(own_key, dims, spread, limit, cuts=(), kind=jnp.bfloat16):
    drawn = jax.random.normal(own_key, dims, jnp.float32) * spread
    if len(cuts) > 0:
        drawn = shard_levels(own_key, dims, cuts, -0.22, 0.18) * drawn
    return jnp.clip(drawn, min=-limit, max=limit).astype(kind)


def setup_inputs(seed: int = 0) -> dict:
    splits = jax.random.split(jax.random.key(seed), 15)
    tokens = normal_values(splits[0], (TOKENS, D), 1.0, 6.0, ((0, 16), (1, 2)))
    norm_attn = jnp.clip(1.0 + 0.1 * jax.random.normal(splits[1], (D,), jnp.float32), 0.5, 1.5)
    norm_mlp = jnp.clip(1.0 + 0.1 * jax.random.normal(splits[2], (D,), jnp.float32), 0.5, 1.5)
    w_kv = normal_values(splits[3], (D, 2, KVW), D ** -0.5, 0.125, ((0, 16), (2, 2)), jnp.float32)
    router_attn = normal_values(splits[4], (D, E_ATT), D ** -0.5, 0.125, (), jnp.float32)
    router_mlp = normal_values(splits[5], (D, E_MLP), D ** -0.5, 0.125, (), jnp.float32)
    w_query = normal_values(splits[6], (E_ATT, D, KVW), D ** -0.5, 0.125, ((0, 4), (1, 4), (2, 2)), jnp.float32)
    w_output = normal_values(splits[7], (E_ATT, KVW, D), (KVW // 16) ** -0.5, 0.5, ((0, 4), (1, 2), (2, 4)), jnp.float32)
    w_gateup = normal_values(splits[8], (E_MLP, D, 2, FF), D ** -0.5, 0.125, ((0, 4), (1, 4), (3, 2)), jnp.float32)
    w_down = normal_values(splits[9], (E_MLP, FF, D), FF ** -0.5, 0.078125, ((0, 4), (1, 2), (2, 4)), jnp.float32)
    segments = jnp.searchsorted(jnp.cumsum(uneven_parts(splits[10], TOKENS // 32, TOKENS, SEQ, 2)), jnp.arange(TOKENS), side="right").astype(jnp.int32)
    att_routes_keys = jax.random.split(jax.random.fold_in(splits[11], 1), TOKENS // TOK_DEV)
    att_routes_turns = jax.random.permutation(jax.random.fold_in(splits[11], 3), TOKENS // TOK_DEV)
    att_routes = jax.vmap(lambda own, number: deal_out(jax.random.fold_in(splits[11], 2), own, number, TOK_DEV, E_ATT, TOP, CAP, 2))(att_routes_keys, att_routes_turns).reshape((TOKENS, TOP))
    mlp_routes_keys = jax.random.split(jax.random.fold_in(splits[12], 1), TOKENS // TOK_DEV)
    mlp_routes_turns = jax.random.permutation(jax.random.fold_in(splits[12], 3), TOKENS // TOK_DEV)
    mlp_routes = jax.vmap(lambda own, number: deal_out(jax.random.fold_in(splits[12], 2), own, number, TOK_DEV, E_MLP, TOP, CAP, 2))(mlp_routes_keys, mlp_routes_turns).reshape((TOKENS, TOP))
    cotangent = normal_values(splits[13], (TOKENS, D), 1.0, 6.0, ((0, 16), (1, 2)))
    return {"tokens": tokens, "norm_attn": norm_attn, "norm_mlp": norm_mlp, "w_kv": w_kv, "router_attn": router_attn, "router_mlp": router_mlp, "w_query": w_query, "w_output": w_output, "w_gateup": w_gateup, "w_down": w_down, "segments": segments, "att_routes": att_routes, "mlp_routes": mlp_routes, "cotangent": cotangent}


EPSILON = 1e-06
MASKED = -1000000000.0
HIGHEST = lax.Precision.HIGHEST

@jax.custom_vjp
def low(v):
    return lax.optimization_barrier(v.astype(jnp.bfloat16)).astype(jnp.float32)

@jax.custom_vjp
def low_back(v):
    return v

def low_keep(v):
    return (low(v), None)

def low_pass(kept, grad):
    return (grad,)

def back_keep(v):
    return (v, None)

def back_low(kept, grad):
    return (low(grad),)
low.defvjp(low_keep, low_pass)
low_back.defvjp(back_keep, back_low)

def rope_angle(positions, head_dim):
    half_dim = head_dim // 2
    frequency = jnp.exp(jnp.arange(half_dim, dtype=jnp.float32) * (-2.0 * math.log(10000.0) / head_dim))
    return positions.astype(jnp.float32)[:, None] * frequency[None, :]

def rotate(values, angles):
    half_dim = values.shape[-1] // 2
    cosine = jnp.cos(angles)[..., None, :]
    sine_part = jnp.sin(angles)[..., None, :]
    first_half = values[..., :half_dim]
    second = values[..., half_dim:]
    return jnp.concatenate([first_half * cosine - second * sine_part, second * cosine + first_half * sine_part], -1)

def rms_norm(values, gain_vector):
    return values * lax.rsqrt(lax.optimization_barrier(jnp.mean(values * values, -1, keepdims=True)) + EPSILON) * gain_vector

def slot_tables(routes, experts, capacity):
    flat_routes = routes.reshape(-1)
    one_hot = (flat_routes[:, None] == jnp.arange(experts, dtype=jnp.int32)[None, :]).astype(jnp.int32)
    slot_rank = lax.optimization_barrier(jnp.sum((jnp.cumsum(one_hot, 0) - one_hot) * one_hot, 1))
    slot_index = flat_routes * capacity + slot_rank
    slot_table = jnp.zeros((experts * capacity,), jnp.int32).at[slot_index].set(jnp.arange(flat_routes.shape[0], dtype=jnp.int32) + 1)
    return (slot_index, slot_table)

def block_size(row_count):
    return max((divisor for divisor in range(1, min(row_count, 512) + 1) if row_count % divisor == 0))

def route_gates(normed, router, routes):
    logits = low_back(jnp.dot(normed, low(router), precision=HIGHEST))
    chosen = jnp.take_along_axis(logits, routes, axis=1)
    return jax.nn.softmax(chosen, axis=1)

def by_expert(inputs, routes, weights, experts, apply):
    span = routes.shape[0] // TOK_DEV * CAP
    slot_index, slot_table = slot_tables(routes, experts, span)

    def one_expert(pieces):
        column, weight = pieces
        live_slot = column > 0
        row_block = jnp.take(inputs, jnp.maximum(column - 1, 0), axis=0)
        row_block = jnp.where(live_slot[:, None], row_block, jnp.zeros((), row_block.dtype))
        return apply(row_block, weight)
    results = lax.map(one_expert, (slot_table.reshape(experts, span), weights))
    return jnp.take(results.reshape(experts * span, -1), slot_index, axis=0)

def attend(query_rows, key_rows, value_rows, segments):
    seq_count = key_rows.shape[0] // SEQ
    block_rows = block_size(SEQ * TOP)
    score_scale = 1.0 / math.sqrt(HD)
    key_pos = jnp.arange(SEQ, dtype=jnp.int32)
    query_pos = jnp.repeat(key_pos, TOP)

    def one_sequence(carried, pieces):
        query_seq, key_seq, value_seq, seg_seq = pieces
        query_seg = jnp.repeat(seg_seq, TOP)

        def one_block(block):
            query_block, pos_block, seg_block = block
            raw_scores = jnp.einsum('qhd,khd->hqk', query_block, key_seq, precision=HIGHEST) * score_scale
            scores = low_back(raw_scores)
            allowed = (seg_block[:, None] == seg_seq[None, :]) & (pos_block[:, None] >= key_pos[None, :])
            scores = jnp.where(allowed[None], scores, MASKED)
            softmax_rows = low(jax.nn.softmax(scores, axis=-1))
            return jnp.einsum('hqk,khd->qhd', softmax_rows, value_seq, precision=HIGHEST)
        mixed_rows = lax.map(jax.checkpoint(one_block), (query_seq.reshape(-1, block_rows, HEADS, HD), query_pos.reshape(-1, block_rows), query_seg.reshape(-1, block_rows)))
        return (carried, mixed_rows.reshape(SEQ * TOP, HEADS, HD))
    pieces = (query_rows.reshape(seq_count, SEQ * TOP, HEADS, HD), key_rows.reshape(seq_count, SEQ, HEADS, HD), value_rows.reshape(seq_count, SEQ, HEADS, HD), segments.reshape(seq_count, SEQ))
    unused, mixed_rows = lax.scan(one_sequence, jnp.zeros((), jnp.float32), pieces)
    return mixed_rows.reshape(-1, HEADS, HD)

def forward(residual, norm_attn, norm_mlp, w_kv, router_attn, router_mlp, w_query, w_output, w_gateup, w_down, segments, att_routes, mlp_routes):
    token_total = residual.shape[0]
    normed_a = low(rms_norm(residual, norm_attn))
    kv_raw = jnp.einsum('td,dgf->tgf', normed_a, low(w_kv), precision=HIGHEST)
    positions = jnp.arange(token_total, dtype=jnp.int32) % SEQ
    angles = rope_angle(positions, HD)
    key_rows = low(rotate(low_back(kv_raw[:, 0].reshape(token_total, HEADS, HD)), angles))
    value_rows = low(low_back(kv_raw[:, 1].reshape(token_total, HEADS, HD)))
    gates_a = route_gates(normed_a, router_attn, att_routes)
    copies_a = low_back(jnp.repeat(normed_a, TOP, axis=0))

    def project(row_block, weight):
        return jnp.dot(row_block, low(weight), precision=HIGHEST)
    query_raw = by_expert(copies_a, att_routes, w_query, E_ATT, project)
    query_angles = rope_angle(jnp.repeat(positions, TOP), HD)
    query_rows = low(rotate(low_back(query_raw.reshape(-1, HEADS, HD)), query_angles))
    mixed_rows = low(low_back(attend(query_rows, key_rows, value_rows, segments)))
    branch_a = low(low_back(by_expert(mixed_rows.reshape(-1, KVW), att_routes, w_output, E_ATT, project)))
    middle = residual + lax.optimization_barrier(jnp.sum(gates_a[:, :, None] * branch_a.reshape(token_total, TOP, D), 1))
    normed_b = low(rms_norm(middle, norm_mlp))
    gates_b = route_gates(normed_b, router_mlp, mlp_routes)
    copies_b = low_back(jnp.repeat(normed_b, TOP, axis=0))

    def feed(row_block, weight_pair):
        gate_up = low_back(jnp.einsum('rd,dgf->rgf', row_block, low(weight_pair[0]), precision=HIGHEST))
        hidden = low(jax.nn.silu(gate_up[:, 0]) * gate_up[:, 1])
        return jnp.dot(hidden, low(weight_pair[1]), precision=HIGHEST)
    branch_b = low(low_back(by_expert(copies_b, mlp_routes, (w_gateup, w_down), E_MLP, feed)))
    return middle + lax.optimization_barrier(jnp.sum(gates_b[:, :, None] * branch_b.reshape(token_total, TOP, D), 1))

def reference(tokens, norm_attn, norm_mlp, w_kv, router_attn, router_mlp, w_query, w_output, w_gateup, w_down, segments, att_routes, mlp_routes, cotangent):

    def tied(residual, gain_a, gain_b, kv_weight, router_a, router_b, query_weight, output_weight, gateup_weight, down_weight):
        return forward(residual, gain_a, gain_b, kv_weight, router_a, router_b, query_weight, output_weight, gateup_weight, down_weight, segments, att_routes, mlp_routes)
    output, pull = jax.vjp(tied, tokens.astype(jnp.float32), norm_attn, norm_mlp, w_kv, router_attn, router_mlp, w_query, w_output, w_gateup, w_down)
    grads = pull(cotangent.astype(jnp.float32))
    return (output.astype(jnp.bfloat16), grads[0], grads[1], grads[2], grads[3], grads[4], grads[5], grads[6], grads[7], grads[8], grads[9])
```

```python
import math

import jax
import jax.numpy as jnp
from jax import lax
from jax.sharding import PartitionSpec as P

HD = 128
EPSILON = 1e-06
MASKED = -1000000000.0
F32 = jnp.float32
BF16 = jnp.bfloat16


def dot(lhs, rhs):
    return jnp.dot(lhs, rhs, preferred_element_type=F32)


def ein(spec, lhs, rhs):
    return jnp.einsum(spec, lhs, rhs, preferred_element_type=F32)


def rope_angle(positions):
    half_dim = HD // 2
    frequency = jnp.exp(
        jnp.arange(half_dim, dtype=F32) * (-2.0 * math.log(10000.0) / HD)
    )
    return positions.astype(F32)[:, None] * frequency[None, :]


def rotate(values, cosine, sine):
    half_dim = values.shape[-1] // 2
    cosine = cosine[..., None, :]
    sine = sine[..., None, :]
    first = values[..., :half_dim]
    second = values[..., half_dim:]
    return jnp.concatenate([first * cosine - second * sine, second * cosine + first * sine], -1)


def block_size(row_count):
    return max(d for d in range(1, min(row_count, 512) + 1) if row_count % d == 0)


def swap(values):
    return lax.ppermute(values, "tensor", [(0, 1), (1, 0)])


def a2a(values, axis):
    return lax.all_to_all(values, axis, split_axis=0, concat_axis=0, tiled=True)


def total_over(values, axis):
    count = lax.axis_size(axis)
    step = 1
    while step < count:
        values = values + lax.ppermute(values, axis, [(i, i ^ step) for i in range(count)])
        step *= 2
    return values


def core_sum(values):
    return values + swap(values)


def both_halves(values, core):
    other = swap(values)
    first = jnp.where(core == 0, values, other)
    second = jnp.where(core == 0, other, values)
    return jnp.concatenate([first, second], -1)


def one_hot_slots(routes, experts, capacity):
    token_count = routes.shape[1]
    member = (routes[:, None, :, 0] == experts[None, :, None]) | (
        routes[:, None, :, 1] == experts[None, :, None]
    )
    tokens = jnp.arange(token_count, dtype=jnp.int32)
    upper = (tokens[:, None] < tokens[None, :]).astype(BF16)
    rank = dot(member.astype(BF16), upper).astype(jnp.int32)
    slots = jnp.arange(capacity, dtype=jnp.int32)
    return member[:, :, None, :] & (rank[:, :, None, :] == slots[None, None, :, None])


def masked_scores(query_block, pos_block, seg_block, key_rows, seq_seg, score_scale):
    key_pos = jnp.arange(key_rows.shape[0], dtype=jnp.int32)
    raw = ein("qhd,khd->hqk", query_block, key_rows) * score_scale
    allowed = (seg_block[:, None] == seq_seg[None, :]) & (pos_block[:, None] >= key_pos[None, :])
    return jnp.where(allowed[None], raw, MASKED)


def attend_forward(query_rows, row_pos, row_seg, key_rows, value_rows, seq_seg):
    row_count, head_count, head_dim = query_rows.shape
    block_rows = block_size(row_count)
    score_scale = 1.0 / math.sqrt(head_dim)

    def one_block(pieces):
        query_block, pos_block, seg_block = pieces
        scores = masked_scores(query_block, pos_block, seg_block, key_rows, seq_seg, score_scale)
        row_peak = jnp.max(scores, -1, keepdims=True)
        row_exp = jnp.exp(scores - row_peak)
        row_mass = jnp.sum(row_exp, -1, keepdims=True)
        softmax_rows = (row_exp / row_mass).astype(BF16)
        mixed = ein("hqk,khd->qhd", softmax_rows, value_rows)
        return (mixed.astype(BF16), (row_peak + jnp.log(row_mass))[..., 0])

    mixed, log_mass = lax.map(
        one_block,
        (
            query_rows.reshape(-1, block_rows, head_count, head_dim),
            row_pos.reshape(-1, block_rows),
            row_seg.reshape(-1, block_rows),
        ),
    )
    return (mixed.reshape(row_count, head_count, head_dim), log_mass)


def attend_backward(
    query_rows, row_pos, row_seg, key_rows, value_rows, seq_seg, log_mass, grad_mixed
):
    row_count, head_count, head_dim = query_rows.shape
    block_rows = block_size(row_count)
    score_scale = 1.0 / math.sqrt(head_dim)

    def one_block(carried, pieces):
        grad_keys, grad_values = carried
        query_block, pos_block, seg_block, mass_block, grad_block = pieces
        scores = masked_scores(query_block, pos_block, seg_block, key_rows, seq_seg, score_scale)
        softmax_rows = jnp.exp(scores - mass_block[..., None])
        grad_soft = ein("qhd,khd->hqk", grad_block, value_rows)
        inner_sum = jnp.sum(softmax_rows * grad_soft, -1, keepdims=True)
        grad_scores = (softmax_rows * (grad_soft - inner_sum)).astype(BF16)
        grad_query = ein("hqk,khd->qhd", grad_scores, key_rows) * score_scale
        grad_keys = grad_keys + ein("hqk,qhd->khd", grad_scores, query_block) * score_scale
        grad_values = grad_values + ein("hqk,qhd->khd", softmax_rows.astype(BF16), grad_block)
        return ((grad_keys, grad_values), grad_query)

    zero_keys = jnp.zeros(key_rows.shape, F32)
    pieces = (
        query_rows.reshape(-1, block_rows, head_count, head_dim),
        row_pos.reshape(-1, block_rows),
        row_seg.reshape(-1, block_rows),
        log_mass,
        grad_mixed.reshape(-1, block_rows, head_count, head_dim),
    )
    (grad_keys, grad_values), grad_query = lax.scan(one_block, (zero_keys, zero_keys), pieces)
    return (grad_query.reshape(row_count, head_count, head_dim), grad_keys, grad_values)


def shards(
    tokens,
    norm_attn,
    norm_mlp,
    w_kv,
    router_attn,
    router_mlp,
    w_query,
    w_output,
    w_gateup,
    w_down,
    segments,
    att_routes,
    mlp_routes,
    cotangent,
):
    count, width = tokens.shape
    full_width = 2 * width
    planes = lax.axis_size("expert")
    columns = lax.axis_size("dp")
    plane = lax.axis_index("expert")
    column = lax.axis_index("dp")
    core = lax.axis_index("tensor")
    n_att = router_attn.shape[1]
    n_mlp = router_mlp.shape[1]
    local_att = w_query.shape[0]
    local_mlp = w_gateup.shape[0]
    ff_parts = columns // local_mlp
    depth = w_gateup.shape[1]
    ff_core = w_gateup.shape[3]
    ff = ff_core // ff_parts
    cap = 3 * count // 8
    seq = planes * count
    feats = w_query.shape[2]
    heads = feats // HD
    kv_part = feats // planes
    part_heads = kv_part // HD
    mlp_expert = plane * local_mlp + column % local_mlp

    ints = jnp.stack(
        [segments, att_routes[:, 0], att_routes[:, 1], mlp_routes[:, 0], mlp_routes[:, 1]]
        + [segments] * 3,
        0,
    )
    all_ints = lax.all_gather(ints, ("dp", "expert"), axis=0, tiled=False).reshape(
        columns, planes, 8, count
    )
    seq_ints = lax.dynamic_index_in_dim(all_ints, column, 0, keepdims=False)
    seq_seg = seq_ints[:, 0].reshape(seq)
    seq_att = jnp.stack([seq_ints[:, 1], seq_ints[:, 2]], -1)
    every_mlp = jnp.stack([all_ints[:, :, 3], all_ints[:, :, 4]], -1).reshape(-1, count, 2)

    seq_tokens = lax.all_gather(tokens, "expert", axis=0, tiled=True)
    residual = tokens.astype(F32)

    def rms_scale(values):
        return lax.rsqrt(
            core_sum(jnp.sum(values * values, 1, keepdims=True)) / full_width + EPSILON
        )

    scale_a = rms_scale(residual)
    rows_a_half = (residual * scale_a * norm_attn).astype(BF16)
    seq_res = seq_tokens.astype(F32)
    seq_scale = rms_scale(seq_res)
    seq_a_half = (seq_res * seq_scale * norm_attn).astype(BF16)
    seq_a = both_halves(seq_a_half, core)

    kv_local = (
        w_kv.astype(BF16).reshape(w_kv.shape[0], 2, planes, kv_part).transpose(2, 0, 1, 3)
    )
    kv_local = a2a(kv_local, "expert")
    w_kv_part = lax.all_gather(kv_local, "dp", axis=0, tiled=True).reshape(
        full_width, 2 * kv_part
    )
    kv_raw = dot(seq_a, w_kv_part)
    angles = rope_angle(jnp.arange(seq, dtype=jnp.int32))
    cos_seq, sin_seq = jnp.cos(angles), jnp.sin(angles)
    key_part = rotate(kv_raw[:, :kv_part].reshape(seq, part_heads, HD), cos_seq, sin_seq)
    kv_part_rows = jnp.stack(
        [key_part.astype(BF16), kv_raw[:, kv_part:].reshape(seq, part_heads, HD).astype(BF16)], 0
    )
    kv_rows = lax.all_gather(kv_part_rows, "expert", axis=2, tiled=True)
    key_rows, value_rows = kv_rows[0], kv_rows[1]

    whole_query = lax.all_gather(w_query.astype(BF16), "dp", axis=1, tiled=True)
    whole_output = lax.all_gather(w_output.astype(BF16), "dp", axis=2, tiled=True)

    gu_send = (
        w_gateup.reshape(local_mlp, depth, 2, ff_parts, ff)
        .transpose(3, 0, 1, 2, 4)
        .astype(BF16)
        .reshape(columns, depth, 2 * ff)
    )
    w_gu = a2a(gu_send, "dp").reshape(full_width, 2 * ff)
    down_send = (
        w_down.reshape(local_mlp, ff_parts, ff, depth)
        .transpose(1, 0, 2, 3)
        .astype(BF16)
        .reshape(columns, ff, depth)
    )
    w_dn = a2a(down_send, "dp")

    own_att = jnp.arange(local_att, dtype=jnp.int32) + plane * local_att
    att_slots = one_hot_slots(seq_att, own_att, cap)
    home_att = one_hot_slots(att_routes[None], jnp.arange(n_att, dtype=jnp.int32), cap)[0]
    home_mlp = one_hot_slots(mlp_routes[None], jnp.arange(n_mlp, dtype=jnp.int32), cap)[0]
    mlp_slots = one_hot_slots(every_mlp, mlp_expert[None], cap)[:, 0]
    other_expert = jnp.sum(every_mlp, -1) - mlp_expert
    row_other = jnp.sum(jnp.where(mlp_slots, other_expert[:, None, :], 0), -1).reshape(-1)

    def by_choice(home, routes):
        experts = home.shape[0]
        named = routes.T[:, None, :] == jnp.arange(experts, dtype=jnp.int32)[None, :, None]
        picks = home[None] & named[:, :, None, :]
        return picks.astype(BF16).reshape(2, experts * cap, count)

    pick_att = by_choice(home_att, att_routes)
    pick_mlp = by_choice(home_mlp, mlp_routes)
    flat_att = home_att.astype(BF16).reshape(n_att * cap, count)
    flat_mlp = home_mlp.astype(BF16).reshape(n_mlp * cap, count)
    seq_pos = jnp.arange(seq, dtype=jnp.int32).reshape(planes, 1, 1, count)
    row_pos = jnp.sum(jnp.where(att_slots, seq_pos, 0), -1).reshape(-1)
    row_seg = jnp.sum(
        jnp.where(att_slots, seq_seg.reshape(planes, 1, 1, count), 0), -1
    ).reshape(-1)
    att_rows = planes * local_att * cap

    def to_expert(rows_half):
        held = a2a(rows_half.reshape(planes, local_mlp * cap, width), "expert")
        held = held.reshape(planes, local_mlp, cap, width).transpose(1, 0, 2, 3)
        sent = jnp.broadcast_to(
            held[None], (ff_parts, local_mlp, planes, cap, width)
        ).reshape(columns, planes * cap, width)
        return both_halves(a2a(sent, "dp").reshape(-1, width), core)

    grad_rows_out = to_expert(dot(flat_mlp, cotangent).astype(BF16))
    grad_hidden_raw = ein("rsd,sfd->rf", grad_rows_out.reshape(-1, columns, depth), w_dn)

    def gates_of(half_rows, router, routes):
        part = lax.dynamic_slice_in_dim(router, core * width, width, 0).astype(BF16)
        logits = core_sum(ein("de,td->et", part, half_rows))
        experts = router.shape[1]
        named = (
            routes.T[:, None, :] == jnp.arange(experts, dtype=jnp.int32)[None, :, None]
        ).astype(F32)
        chosen = jnp.sum(named * logits[None], 1)
        return jax.nn.softmax(chosen, axis=0), named, part

    gates_a, named_a, router_a = gates_of(rows_a_half, router_attn, att_routes)
    held_a = ein(
        "slct,std->lscd", att_slots.astype(BF16), seq_a.reshape(planes, count, full_width)
    ).astype(BF16)
    held_a = held_a.reshape(local_att, planes * cap, full_width)
    pos_rows = row_pos.reshape(planes, local_att, cap).transpose(1, 0, 2).reshape(-1)
    seg_rows = row_seg.reshape(planes, local_att, cap).transpose(1, 0, 2).reshape(-1)
    angle_rows = rope_angle(pos_rows)
    cos_rows, sin_rows = jnp.cos(angle_rows), jnp.sin(angle_rows)
    query_raw = ein("lrd,ldf->lrf", held_a, whole_query)
    query_rows = rotate(query_raw.reshape(att_rows, heads, HD), cos_rows, sin_rows).astype(BF16)
    mixed_rows, log_mass = attend_forward(
        query_rows, pos_rows, seg_rows, key_rows, value_rows, seq_seg
    )
    mixed_owner = mixed_rows.reshape(local_att, planes * cap, feats)

    def halves(values, axis):
        mine = lax.dynamic_slice_in_dim(values, core * width, width, axis)
        theirs = lax.dynamic_slice_in_dim(values, (1 - core) * width, width, axis)
        return mine, theirs

    def att_home(rows):
        sent = rows.astype(BF16).reshape(local_att, planes, cap, width).transpose(1, 0, 2, 3)
        return a2a(sent.reshape(planes, local_att * cap, width), "expert").reshape(-1, width)

    out_mine, out_theirs = halves(whole_output, 2)
    given = swap(ein("lrf,lfd->lrd", mixed_owner, out_theirs).astype(BF16))
    branch_a = ein("lrf,lfd->lrd", mixed_owner, out_mine) + given.astype(F32)
    home_a = att_home(branch_a)
    taken_a = ein("jst,sd->jtd", pick_att, home_a)
    middle = residual + jnp.sum(gates_a[:, :, None] * taken_a, 0)

    scale_b = rms_scale(middle)
    rows_b_half = (middle * scale_b * norm_mlp).astype(BF16)
    gates_b, named_b, router_b = gates_of(rows_b_half, router_mlp, mlp_routes)
    held_b = to_expert(dot(flat_mlp, rows_b_half).astype(BF16))
    gate_up = dot(held_b, w_gu)
    row_logits = dot(held_b, router_mlp.astype(BF16))
    expert_ids = jnp.arange(n_mlp, dtype=jnp.int32)[None, :]
    own_logit = jnp.sum(jnp.where(expert_ids == mlp_expert, row_logits, 0.0), 1, keepdims=True)
    other_logit = jnp.sum(
        jnp.where(expert_ids == row_other[:, None], row_logits, 0.0), 1, keepdims=True
    )
    row_gate = jax.nn.sigmoid(own_logit - other_logit)
    gate_part = gate_up[:, :ff]
    up_part = gate_up[:, ff:]
    sig = jax.nn.sigmoid(gate_part)
    silu = gate_part * sig
    hidden32 = silu * up_part
    hidden = hidden32.astype(BF16)
    hidden_gated = (hidden32 * row_gate).astype(BF16)
    row_dgate = jnp.sum(hidden32 * grad_hidden_raw, 1)
    grad_hidden = grad_hidden_raw * row_gate
    grad_gate = (grad_hidden * up_part * sig * (1.0 + gate_part * (1.0 - sig))).astype(BF16)
    grad_up = (grad_hidden * silu).astype(BF16)
    grad_both = jnp.concatenate([grad_gate, grad_up], 1)

    def mlp_home(rows):
        tail = rows.shape[1:]
        got = a2a(rows.reshape((columns, planes * cap) + tail), "dp")
        got = got.reshape((ff_parts, local_mlp, planes, cap) + tail).astype(F32)
        summed = jnp.sum(got, 0).swapaxes(0, 1).astype(rows.dtype)
        back = a2a(summed.reshape((planes, local_mlp * cap) + tail), "expert")
        return back.reshape((n_mlp * cap,) + tail)

    dgate_home = mlp_home(core_sum(row_dgate))
    gu_mine, gu_theirs = halves(w_gu, 0)
    given = swap(ein("rf,df->rd", grad_both, gu_theirs).astype(BF16))
    copies = (ein("rf,df->rd", grad_both, gu_mine) + given.astype(F32)).astype(BF16)
    home_db = mlp_home(copies)

    def gates_back(gates, grad_gates, named):
        chosen = gates * (grad_gates - jnp.sum(gates * grad_gates, 0, keepdims=True))
        return jnp.sum(chosen[:, None, :] * named, 0).astype(BF16)

    grad_gates_b = jnp.sum(pick_mlp.astype(F32) * dgate_home[None, :, None], 1)
    grad_logit_b = gates_back(gates_b, grad_gates_b, named_b)
    grad_normed_b = ein("st,sd->td", flat_mlp, home_db) + ein("et,de->td", grad_logit_b, router_b)
    grad_router_b = ein("et,td->ed", grad_logit_b, rows_b_half)

    def normalize_back(values, gain, row_scale, grad_normed):
        inner = core_sum(jnp.sum(grad_normed * gain * values, 1, keepdims=True))
        grad_values = (
            row_scale * gain * grad_normed
            - values * (row_scale * row_scale * row_scale) * inner / full_width
        )
        return grad_values, jnp.sum(grad_normed * values * row_scale, 0)

    grad_out = cotangent.astype(F32)
    grad_mid_norm, grad_gain_b = normalize_back(middle, norm_mlp, scale_b, grad_normed_b)
    grad_middle = grad_out + grad_mid_norm

    grad_gates_a = core_sum(jnp.sum(grad_middle[None] * taken_a, 2))
    grad_logit_a = gates_back(gates_a, grad_gates_a, named_a)
    grad_taken_a = (gates_a[:, :, None] * grad_middle[None]).astype(BF16)
    sent_a = ein("jst,jtd->sd", pick_att, grad_taken_a).astype(BF16)
    held_grad_a = both_halves(
        a2a(sent_a.reshape(planes, local_att * cap, width), "expert").reshape(-1, width), core
    )
    held_grad_a = (
        held_grad_a.reshape(planes, local_att, cap, full_width)
        .transpose(1, 0, 2, 3)
        .reshape(local_att, planes * cap, full_width)
    )
    grad_mixed = ein("lrd,lfd->lrf", held_grad_a, whole_output).astype(BF16)
    grad_query_rot, grad_keys, grad_values = attend_backward(
        query_rows,
        pos_rows,
        seg_rows,
        key_rows,
        value_rows,
        seq_seg,
        log_mass,
        grad_mixed.reshape(att_rows, heads, HD),
    )
    grad_query_raw = (
        rotate(grad_query_rot, cos_rows, -sin_rows)
        .astype(BF16)
        .reshape(local_att, planes * cap, feats)
    )
    grad_kv_seq = jnp.stack([grad_keys, grad_values], 0).astype(BF16)
    grad_kv_part = lax.psum_scatter(
        grad_kv_seq, "expert", scatter_dimension=2, tiled=True
    ).astype(F32)
    grad_kv = jnp.concatenate(
        [
            rotate(grad_kv_part[0], cos_seq, -sin_seq).reshape(seq, kv_part),
            grad_kv_part[1].reshape(seq, kv_part),
        ],
        1,
    ).astype(BF16)
    query_mine, query_theirs = halves(whole_query, 1)
    kv_mine, kv_theirs = halves(w_kv_part, 0)

    def grad_seq(query_half, kv_half):
        rows = ein("lrf,ldf->lrd", grad_query_raw, query_half).astype(BF16)
        spread = ein(
            "slct,lscd->std",
            att_slots.astype(BF16),
            rows.reshape(local_att, planes, cap, width),
        )
        return spread.reshape(seq, width) + ein("tf,df->td", grad_kv, kv_half)

    given = swap(grad_seq(query_theirs, kv_theirs).astype(BF16))
    grad_seq_a = (grad_seq(query_mine, kv_mine) + given.astype(F32)).astype(BF16)
    grad_rows_a = lax.psum_scatter(
        grad_seq_a, "expert", scatter_dimension=0, tiled=True
    ).astype(F32)
    grad_normed_a = grad_rows_a + ein("et,de->td", grad_logit_a, router_a)
    grad_router_a = ein("et,td->ed", grad_logit_a, rows_a_half)
    grad_in_norm, grad_gain_a = normalize_back(residual, norm_attn, scale_a, grad_normed_a)
    grad_tokens = grad_middle + grad_in_norm

    grad_gu = ein("rd,rf->df", held_b, grad_both).astype(BF16)
    got_gu = a2a(grad_gu.reshape(columns, depth, 2 * ff), "dp")
    grad_wgateup = (
        got_gu.reshape(ff_parts, local_mlp, depth, 2, ff)
        .transpose(1, 2, 3, 0, 4)
        .astype(F32)
        .reshape(w_gateup.shape)
    )
    grad_dn = ein(
        "rf,rsd->sfd", hidden_gated, grad_rows_out.reshape(-1, columns, depth)
    ).astype(BF16)
    got_dn = a2a(grad_dn, "dp")
    grad_wdown = (
        got_dn.reshape(ff_parts, local_mlp, ff, depth)
        .transpose(1, 0, 2, 3)
        .astype(F32)
        .reshape(w_down.shape)
    )
    grad_woutput = lax.psum_scatter(
        ein("lrf,lrd->lfd", mixed_owner, held_grad_a).astype(BF16),
        "dp",
        scatter_dimension=2,
        tiled=True,
    ).astype(F32)
    grad_wquery = lax.psum_scatter(
        ein("lrd,lrf->ldf", held_a, grad_query_raw).astype(BF16),
        "dp",
        scatter_dimension=1,
        tiled=True,
    ).astype(F32)
    grad_kv_w = lax.psum_scatter(
        ein("td,tf->df", seq_a, grad_kv).astype(BF16), "dp", scatter_dimension=0, tiled=True
    )
    grad_kv_w = a2a(grad_kv_w.reshape(planes, w_kv.shape[0], 2, kv_part), "expert")
    grad_wkv = grad_kv_w.transpose(1, 2, 0, 3).astype(F32).reshape(w_kv.shape)

    dn_lo = w_dn.reshape(2, columns // 2, ff, depth)
    dn_mine = lax.dynamic_index_in_dim(dn_lo, core, 0, keepdims=False)
    dn_theirs = lax.dynamic_index_in_dim(dn_lo, 1 - core, 0, keepdims=False)
    rows_total = held_b.shape[0]

    def branch_half(weights):
        return ein("rf,sfd->rsd", hidden, weights).reshape(rows_total, width)

    given = swap(branch_half(dn_theirs).astype(BF16))
    branch_b = (branch_half(dn_mine) + given.astype(F32)).astype(BF16)
    home_b = mlp_home(branch_b)
    taken_b = ein("jst,sd->jtd", pick_mlp, home_b)
    output = middle + jnp.sum(gates_b[:, :, None] * taken_b, 0)

    small = jnp.concatenate(
        [grad_router_a, grad_router_b, grad_gain_a[None], grad_gain_b[None]], 0
    )
    small = total_over(total_over(small, "dp"), "expert")
    routers = both_halves(small[: n_att + n_mlp], core)
    return (
        output.astype(BF16),
        grad_tokens,
        small[n_att + n_mlp],
        small[n_att + n_mlp + 1],
        grad_wkv,
        routers[:n_att].T,
        routers[n_att:].T,
        grad_wquery,
        grad_woutput,
        grad_wgateup,
        grad_wdown,
    )


def solution(mesh):
    in_specs = (
        P(("dp", "expert"), "tensor"),
        P("tensor"),
        P("tensor"),
        P(("dp", "expert"), None, "tensor"),
        P(),
        P(),
        P("expert", "dp", "tensor"),
        P("expert", "tensor", "dp"),
        P("expert", "dp", None, "tensor"),
        P("expert", "tensor", "dp"),
        P(("dp", "expert")),
        P(("dp", "expert"), None),
        P(("dp", "expert"), None),
        P(("dp", "expert"), "tensor"),
    )
    out_specs = (
        P(("dp", "expert"), "tensor"),
        P(("dp", "expert"), "tensor"),
        P("tensor"),
        P("tensor"),
        P(("dp", "expert"), None, "tensor"),
        P(),
        P(),
        P("expert", "dp", "tensor"),
        P("expert", "tensor", "dp"),
        P("expert", "dp", None, "tensor"),
        P("expert", "tensor", "dp"),
    )
    return jax.shard_map(shards, mesh=mesh, in_specs=in_specs, out_specs=out_specs, check_vma=False)
```

```python
import functools
import math

import jax
import jax.numpy as jnp
from jax import lax
from jax.experimental import pallas as pl
from jax.experimental.pallas import tpu as pltpu
from jax.sharding import PartitionSpec as P

HD = 128
EPSILON = 1e-06
MASKED = -1000000000.0
F32 = jnp.float32
BF16 = jnp.bfloat16
LIMIT = 60 << 20
NT = (((1,), (1,)), ((), ()))
TN = (((0,), (0,)), ((), ()))


def dot(lhs, rhs):
    return jnp.dot(lhs, rhs, preferred_element_type=F32)


def ein(spec, lhs, rhs):
    return jnp.einsum(spec, lhs, rhs, preferred_element_type=F32)


def gdot(lhs, rhs, dims):
    return lax.dot_general(lhs, rhs, dims, preferred_element_type=F32)


def swap(values):
    return lax.ppermute(values, "tensor", [(0, 1), (1, 0)])


def a2a(values, axis):
    return lax.all_to_all(values, axis, split_axis=0, concat_axis=0, tiled=True)


def total_over(values, axis):
    count = lax.axis_size(axis)
    step = 1
    while step < count:
        values = values + lax.ppermute(values, axis, [(i, i ^ step) for i in range(count)])
        step *= 2
    return values


def core_sum(values):
    return values + swap(values)


def relay(values, axis):
    count = lax.axis_size(axis)
    up, down = [values], [values]
    for _ in range(count - 1):
        up.append(lax.ppermute(up[-1], axis, [(i, i + 1) for i in range(count - 1)]))
        down.append(lax.ppermute(down[-1], axis, [(i + 1, i) for i in range(count - 1)]))
    return [values] + [down[j] + up[count - j] for j in range(1, count)]


def shift(blocks, sign):
    count = lax.axis_size("expert")
    return [blocks[0]] + [
        lax.ppermute(blocks[j], "expert", [(i, (i + sign * j) % count) for i in range(count)])
        for j in range(1, count)
    ]


def cross(blocks):
    count = lax.axis_size("dp")
    return [blocks[0]] + [
        lax.ppermute(blocks[k], "dp", [(i, i ^ k) for i in range(count)]) for k in range(1, count)
    ]


def both_halves(values, core):
    other = swap(values)
    first = jnp.where(core == 0, values, other)
    second = jnp.where(core == 0, other, values)
    return jnp.concatenate([first, second], -1)


def one_hot_slots(routes, experts, capacity):
    token_count = routes.shape[2]
    member = (routes[:, None, 0] == experts[None, :, None]) | (
        routes[:, None, 1] == experts[None, :, None]
    )
    tokens = jnp.arange(token_count, dtype=jnp.int32)
    upper = (tokens[:, None] < tokens[None, :]).astype(BF16)
    rank = dot(member.astype(BF16), upper).astype(jnp.int32)
    slots = jnp.arange(capacity, dtype=jnp.int32)
    return member[:, :, None, :] & (rank[:, :, None, :] == slots[None, None, :, None])


def params(*kinds):
    return pltpu.CompilerParams(dimension_semantics=kinds, vmem_limit_bytes=LIMIT)


def pack_kernel(ff, parts, src, out):
    for part in range(parts):
        for half in range(2):
            out[part, 0, :, half * ff : (half + 1) * ff] = src[
                0, :, half, part * ff : (part + 1) * ff
            ].astype(BF16)


def pack_gateup(weights, parts):
    local, depth, _, ff_core = weights.shape
    ff = ff_core // parts
    if ff % 128:
        moved = weights.reshape(local, depth, 2, parts, ff).transpose(3, 0, 1, 2, 4)
        return moved.astype(BF16).reshape(parts, local, depth, 2 * ff)
    rows = min(depth, 128)
    return pl.pallas_call(
        functools.partial(pack_kernel, ff, parts),
        grid=(local, depth // rows),
        in_specs=[pl.BlockSpec((1, rows, 2, ff_core), lambda l, r: (l, r, 0, 0))],
        out_specs=pl.BlockSpec((parts, 1, rows, 2 * ff), lambda l, r: (0, l, r, 0)),
        out_shape=jax.ShapeDtypeStruct((parts, local, depth, 2 * ff), BF16),
        compiler_params=params("parallel", "parallel"),
        name="pack_gateup",
    )(weights)


def unpack_kernel(ff, parts, src, out):
    for part in range(parts):
        for half in range(2):
            out[0, :, half, part * ff : (part + 1) * ff] = src[
                part, 0, :, half * ff : (half + 1) * ff
            ].astype(F32)


def unpack_gateup(grads, parts):
    _, local, depth, ff2 = grads.shape
    ff = ff2 // 2
    if ff % 128:
        moved = grads.reshape(parts, local, depth, 2, ff).transpose(1, 2, 3, 0, 4)
        return moved.astype(F32).reshape(local, depth, 2, parts * ff)
    rows = min(depth, 128)
    return pl.pallas_call(
        functools.partial(unpack_kernel, ff, parts),
        grid=(local, depth // rows),
        in_specs=[pl.BlockSpec((parts, 1, rows, 2 * ff), lambda l, r: (0, l, r, 0))],
        out_specs=pl.BlockSpec((1, rows, 2, parts * ff), lambda l, r: (l, r, 0, 0)),
        out_shape=jax.ShapeDtypeStruct((local, depth, 2, parts * ff), F32),
        compiler_params=params("parallel", "parallel"),
        name="unpack_gateup",
    )(grads)


def cast_kernel(src, out):
    out[...] = src[...].reshape(out.shape).astype(out.dtype)


def pack_down(weights, parts):
    local, ff_core, depth = weights.shape
    ff = ff_core // parts
    return pl.pallas_call(
        cast_kernel,
        grid=(parts, local),
        in_specs=[pl.BlockSpec((1, ff, depth), lambda p, l: (l, p, 0))],
        out_specs=pl.BlockSpec((1, 1, ff, depth), lambda p, l: (p, l, 0, 0)),
        out_shape=jax.ShapeDtypeStruct((parts, local, ff, depth), BF16),
        compiler_params=params("parallel", "parallel"),
        name="pack_down",
    )(weights)


def unpack_down(grads):
    parts, local, ff, depth = grads.shape
    return pl.pallas_call(
        cast_kernel,
        grid=(parts, local),
        in_specs=[pl.BlockSpec((1, 1, ff, depth), lambda p, l: (p, l, 0, 0))],
        out_specs=pl.BlockSpec((1, ff, depth), lambda p, l: (l, p, 0)),
        out_shape=jax.ShapeDtypeStruct((local, parts * ff, depth), F32),
        compiler_params=params("parallel", "parallel"),
        name="unpack_down",
    )(grads)


def turn(values, cosine, sine):
    return values * cosine + pltpu.roll(values, HD // 2, 1) * sine


def att_fwd_kernel(
    place, q_in, kv, cos, sin, row_pos, row_seg, key_seg, *rest
):
    o_out, q_out = rest[-2:]
    query = turn(q_in[...], cos[...], sin[...]).astype(BF16)
    q_out[...] = query
    scores = gdot(query, kv[0, :, :HD], NT) * (1.0 / math.sqrt(HD))
    key_pos = lax.broadcasted_iota(jnp.int32, scores.shape, 1)
    allowed = (row_seg[...] == key_seg[...]) & (row_pos[...] >= key_pos)
    scores = jnp.where(allowed, scores, MASKED)
    peak = jnp.max(scores, 1, keepdims=True)
    weight = jnp.exp(scores - peak)
    mass = jnp.sum(weight, 1, keepdims=True)
    soft = (weight * (1.0 / mass)).astype(BF16)
    o_out[...] = dot(soft, kv[0, :, HD:]).astype(BF16)


def att_forward(place, q_raw, kv, cos, sin, row_pos, row_seg, key_seg, group, before):
    rows, feats = q_raw.shape
    seq, wide = kv.shape[1:]
    group_heads = wide // (2 * HD)
    block = min(256, rows)
    head = lambda h, i, place: (i, place[group] * group_heads + h)
    row = lambda h, i, place: (i, 0)
    in_specs = [
        pl.BlockSpec((block, HD), head),
        pl.BlockSpec((1, seq, 2 * HD), lambda h, i, place: (0, 0, h)),
        pl.BlockSpec((block, HD), row),
        pl.BlockSpec((block, HD), row),
        pl.BlockSpec((block, 1), row),
        pl.BlockSpec((block, 1), row),
        pl.BlockSpec((1, seq), lambda h, i, place: (0, 0)),
    ]
    operands = [place, q_raw, kv, cos, sin, row_pos, row_seg, key_seg]
    aliases = {}
    if before is not None:
        in_specs += [pl.BlockSpec(memory_space=pl.ANY)] * 2
        operands += list(before)
        aliases = {8: 0, 9: 1}
    return pl.pallas_call(
        att_fwd_kernel,
        grid_spec=pltpu.PrefetchScalarGridSpec(
            num_scalar_prefetch=1,
            grid=(group_heads, rows // block),
            in_specs=in_specs,
            out_specs=[pl.BlockSpec((block, HD), head)] * 2,
        ),
        out_shape=[jax.ShapeDtypeStruct((rows, feats), BF16)] * 2,
        input_output_aliases=aliases,
        compiler_params=params("arbitrary", "arbitrary"),
        name="attention_fwd",
    )(*operands)


def att_bwd_kernel(
    place, q_in, do_in, kv, cos, sin, key_cos, key_sin, row_pos, row_seg, key_seg,
    dq_out, dkv_out, dk_sum, dv_sum,
):
    step = pl.program_id(1)
    scale = 1.0 / math.sqrt(HD)
    query, grad_out = q_in[...], do_in[...]
    keys, values = kv[0, :, :HD], kv[0, :, HD:]
    scores = gdot(keys, query, NT) * scale
    key_pos = lax.broadcasted_iota(jnp.int32, scores.shape, 0)
    allowed = (row_seg[...] == key_seg[...]) & (row_pos[...] >= key_pos)
    scores = jnp.where(allowed, scores, MASKED)
    peak = jnp.max(scores, 0, keepdims=True)
    weight = jnp.exp(scores - peak)
    soft = weight * (1.0 / jnp.sum(weight, 0, keepdims=True))
    grad_soft = gdot(values, grad_out, NT)
    inner = jnp.sum(soft * grad_soft, 0, keepdims=True)
    grad_scores = (soft * (grad_soft - inner)).astype(BF16)
    grad_query = gdot(grad_scores, keys, TN) * scale
    dq_out[...] = turn(grad_query, cos[...], -sin[...]).astype(BF16)

    @pl.when(step == 0)
    def _():
        dk_sum[...] = jnp.zeros_like(dk_sum)
        dv_sum[...] = jnp.zeros_like(dv_sum)

    dk_sum[...] += dot(grad_scores, query)
    dv_sum[...] += dot(soft.astype(BF16), grad_out)

    @pl.when(step == pl.num_programs(1) - 1)
    def _():
        grad_keys = turn(dk_sum[...] * scale, key_cos[...], -key_sin[...])
        dkv_out[0, :, :HD] = grad_keys.astype(BF16)
        dkv_out[0, :, HD:] = dv_sum[...].astype(BF16)


def att_backward(
    place, query, grad_mixed, kv, cos, sin, key_cos, key_sin, row_pos, row_seg, key_seg
):
    rows, feats = query.shape
    planes, seq, wide = kv.shape
    group_heads = wide // (2 * HD)
    block = min(256, rows)
    group = lambda h: h // group_heads
    inner = lambda h: lax.rem(h, group_heads)
    head = lambda h, i, place: (i, place[group(h)] * group_heads + inner(h))
    row = lambda h, i, place: (i, 0)
    lane = lambda h, i, place: (0, i)
    whole = lambda h, i, place: (0, 0)
    return pl.pallas_call(
        att_bwd_kernel,
        grid_spec=pltpu.PrefetchScalarGridSpec(
            num_scalar_prefetch=1,
            grid=(planes * group_heads, rows // block),
            in_specs=[
                pl.BlockSpec((block, HD), head),
                pl.BlockSpec((block, HD), head),
                pl.BlockSpec((1, seq, 2 * HD), lambda h, i, place: (group(h), 0, inner(h))),
                pl.BlockSpec((block, HD), row),
                pl.BlockSpec((block, HD), row),
                pl.BlockSpec((seq, HD), whole),
                pl.BlockSpec((seq, HD), whole),
                pl.BlockSpec((1, block), lane),
                pl.BlockSpec((1, block), lane),
                pl.BlockSpec((seq, 1), whole),
            ],
            out_specs=[
                pl.BlockSpec((block, HD), head),
                pl.BlockSpec(
                    (1, seq, 2 * HD), lambda h, i, place: (place[group(h)], 0, inner(h))
                ),
            ],
            scratch_shapes=[pltpu.VMEM((seq, HD), F32)] * 2,
        ),
        out_shape=[
            jax.ShapeDtypeStruct((rows, feats), BF16),
            jax.ShapeDtypeStruct((planes, seq, wide), BF16),
        ],
        compiler_params=params("arbitrary", "arbitrary"),
        name="attention_bwd",
    )(place, query, grad_mixed, kv, cos, sin, key_cos, key_sin, row_pos, row_seg, key_seg)


def raw_kernel(core, g_own, g_other, w_dn, out):
    columns = w_dn.shape[0]
    half, depth = columns // 2, w_dn.shape[2]
    total = jnp.zeros(out.shape, F32)
    for i in range(half):
        part = slice(i * depth, (i + 1) * depth)
        total += gdot(g_own[:, part], w_dn[core[0] * half + i], NT)
        total += gdot(g_other[:, part], w_dn[(1 - core[0]) * half + i], NT)
    out[...] = total


def hidden_raw(core, g_own, g_other, w_dn):
    rows, width = g_own.shape
    columns, ff, depth = w_dn.shape
    block = 256
    return pl.pallas_call(
        raw_kernel,
        grid_spec=pltpu.PrefetchScalarGridSpec(
            num_scalar_prefetch=1,
            grid=(rows // block,),
            in_specs=[
                pl.BlockSpec((block, width), lambda i, c: (i, 0)),
                pl.BlockSpec((block, width), lambda i, c: (i, 0)),
                pl.BlockSpec(
                    (columns, ff, depth), lambda i, c: (0, 0, 0), pipeline_mode=pl.Buffered(1)
                ),
            ],
            out_specs=pl.BlockSpec((block, ff), lambda i, c: (i, 0)),
        ),
        out_shape=jax.ShapeDtypeStruct((rows, ff), F32),
        compiler_params=params("arbitrary"),
        name="hidden_raw",
    )(core, g_own, g_other, w_dn)


def ff_kernel(place, x_own, x_other, w_gu, raw, router, other, hid, hid_gated, duw, dgate):
    core, expert = place[0], place[1]
    width = x_own.shape[1]
    ff = raw.shape[1]
    mine = pl.ds(pl.multiple_of(core * width, width), width)
    theirs = pl.ds(pl.multiple_of((1 - core) * width, width), width)

    def product(weights):
        return dot(x_own[...], weights[mine, :]) + dot(x_other[...], weights[theirs, :])

    logits = product(router)
    lanes = lax.broadcasted_iota(jnp.int32, logits.shape, 1)
    own_logit = jnp.sum(jnp.where(lanes == expert, logits, 0.0), 1, keepdims=True)
    other_logit = jnp.sum(jnp.where(lanes == other[...], logits, 0.0), 1, keepdims=True)
    gate = jax.nn.sigmoid(own_logit - other_logit)
    both = product(w_gu)
    gate_part, up_part = both[:, :ff], both[:, ff:]
    sig = 1.0 / (1.0 + jnp.exp(-gate_part))
    silu = gate_part * sig
    hidden = silu * up_part
    hid[...] = hidden.astype(BF16)
    hid_gated[...] = (hidden * gate).astype(BF16)
    dgate[...] = jnp.sum(hidden * raw[...], 1, keepdims=True)
    grad_hidden = raw[...] * gate
    duw[:, :ff] = (grad_hidden * up_part * (sig * (1.0 + gate_part * (1.0 - sig)))).astype(BF16)
    duw[:, ff:] = (grad_hidden * silu).astype(BF16)


def feed_forward(place, x_own, x_other, w_gu, raw, router, other):
    rows, width = x_own.shape
    ff = raw.shape[1]
    block = 256
    row = lambda i, c: (i, 0)
    whole = lambda i, c: (0, 0)
    return pl.pallas_call(
        ff_kernel,
        grid_spec=pltpu.PrefetchScalarGridSpec(
            num_scalar_prefetch=1,
            grid=(rows // block,),
            in_specs=[
                pl.BlockSpec((block, width), row),
                pl.BlockSpec((block, width), row),
                pl.BlockSpec(w_gu.shape, whole, pipeline_mode=pl.Buffered(1)),
                pl.BlockSpec((block, ff), row),
                pl.BlockSpec(router.shape, whole, pipeline_mode=pl.Buffered(1)),
                pl.BlockSpec((block, 1), row),
            ],
            out_specs=[
                pl.BlockSpec((block, ff), row),
                pl.BlockSpec((block, ff), row),
                pl.BlockSpec((block, 2 * ff), row),
                pl.BlockSpec((block, 1), row),
            ],
        ),
        out_shape=[
            jax.ShapeDtypeStruct((rows, ff), BF16),
            jax.ShapeDtypeStruct((rows, ff), BF16),
            jax.ShapeDtypeStruct((rows, 2 * ff), BF16),
            jax.ShapeDtypeStruct((rows, 1), F32),
        ],
        compiler_params=params("arbitrary"),
        name="feed_forward",
    )(place, x_own, x_other, w_gu, raw, router, other)


def rows_kernel(transposed, which, lhs, weights, *rest):
    out = rest[-1]
    if transposed:
        total = gdot(lhs[...], weights[...], NT)
    else:
        total = jnp.concatenate(
            [dot(lhs[...], weights[i]) for i in range(weights.shape[0])], 1
        )
    if len(rest) > 1:
        total = total + rest[0][...].astype(F32)
    out[...] = total.astype(BF16)


def rows_half(which, lhs, weights, width, add=None):
    rows, inner = lhs.shape
    transposed = weights.ndim == 2
    block = 256
    row = lambda i, c: (i, 0)
    if transposed:
        w_spec = pl.BlockSpec(
            (width, inner), lambda i, c: (c[0], 0), pipeline_mode=pl.Buffered(1)
        )
    else:
        w_spec = pl.BlockSpec(
            (weights.shape[0] // 2,) + weights.shape[1:],
            lambda i, c: (c[0], 0, 0),
            pipeline_mode=pl.Buffered(1),
        )
    in_specs = [pl.BlockSpec((block, inner), row), w_spec]
    operands = [which, lhs, weights]
    if add is not None:
        in_specs.append(pl.BlockSpec((block, width), row))
        operands.append(add)
    return pl.pallas_call(
        functools.partial(rows_kernel, transposed),
        grid_spec=pltpu.PrefetchScalarGridSpec(
            num_scalar_prefetch=1,
            grid=(rows // block,),
            in_specs=in_specs,
            out_specs=pl.BlockSpec((block, width), row),
        ),
        out_shape=jax.ShapeDtypeStruct((rows, width), BF16),
        compiler_params=params("arbitrary"),
        name="rows_half",
    )(*operands)


def shards(
    tokens,
    norm_attn,
    norm_mlp,
    w_kv,
    router_attn,
    router_mlp,
    w_query,
    w_output,
    w_gateup,
    w_down,
    segments,
    att_routes,
    mlp_routes,
    cotangent,
):
    count, width = tokens.shape
    full_width = 2 * width
    planes = lax.axis_size("expert")
    columns = lax.axis_size("dp")
    plane = lax.axis_index("expert")
    column = lax.axis_index("dp")
    core = lax.axis_index("tensor")
    n_att = router_attn.shape[1]
    n_mlp = router_mlp.shape[1]
    local_att = w_query.shape[0]
    local_mlp = w_gateup.shape[0]
    ff_parts = columns // local_mlp
    depth = w_gateup.shape[1]
    ff = w_gateup.shape[3] // ff_parts
    cap = 3 * count // 8
    seq = planes * count
    feats = w_query.shape[2]
    kv_part = feats // planes
    part_heads = kv_part // HD
    own_local = column % local_mlp
    mlp_expert = plane * local_mlp + own_local
    steps = jnp.arange(planes, dtype=jnp.int32)
    source_planes = (plane + steps) % planes
    target_planes = (plane - steps + planes) % planes
    near_local = own_local ^ jnp.arange(local_mlp, dtype=jnp.int32)
    core_at = core.astype(jnp.int32)[None]
    other_at = 1 - core_at

    def absolute(blocks):
        twice = jnp.concatenate([blocks, blocks], 0)
        return lax.dynamic_slice_in_dim(twice, (planes - plane) % planes, planes, 0)

    def relative(blocks):
        twice = jnp.concatenate([blocks, blocks], 0)
        return lax.dynamic_slice_in_dim(twice, plane, planes, 0)

    kv_send = w_kv.astype(BF16).reshape(w_kv.shape[0], 2, planes, part_heads, HD)
    kv_send = a2a(kv_send.transpose(2, 0, 3, 1, 4), "expert")
    w_kv_part = lax.all_gather(kv_send, "dp", axis=0, tiled=True).reshape(
        full_width, 2 * kv_part
    )
    whole_query = lax.all_gather(w_query.astype(BF16), "dp", axis=1, tiled=True)
    whole_output = lax.all_gather(w_output.astype(BF16), "dp", axis=2, tiled=True)
    down_send = pack_down(w_down, ff_parts).reshape(columns, ff, depth)
    w_dn = a2a(down_send, "dp")
    gu_send = pack_gateup(w_gateup, ff_parts).reshape(columns, depth, 2 * ff)
    w_gu = a2a(gu_send, "dp").reshape(full_width, 2 * ff)

    ints = jnp.concatenate(
        [
            segments[None],
            att_routes.T,
            mlp_routes.T,
            jnp.zeros((3, count), jnp.int32),
        ],
        0,
    )
    near_ints = jnp.stack(relay(ints, "expert"), 0)[None]
    step = 1
    while step < columns:
        pairs = [(i, i ^ step) for i in range(columns)]
        near_ints = jnp.concatenate([near_ints, lax.ppermute(near_ints, "dp", pairs)], 0)
        step *= 2

    residual = tokens.astype(F32)
    seq_res = jnp.concatenate(relay(tokens, "expert"), 0).astype(F32)

    def rms_scale(values):
        return lax.rsqrt(
            core_sum(jnp.sum(values * values, 1, keepdims=True)) / full_width + EPSILON
        )

    seq_scale = rms_scale(seq_res)
    seq_a_half = (seq_res * seq_scale * norm_attn).astype(BF16)
    scale_a = seq_scale[:count]
    rows_a_half = seq_a_half[:count]
    seq_a = both_halves(seq_a_half, core)

    def angles_of(positions):
        frequency = jnp.exp(
            jnp.arange(HD // 2, dtype=F32) * (-2.0 * math.log(10000.0) / HD)
        )
        angle = positions.astype(F32)[:, None] * frequency[None, :]
        cosine, sine = jnp.cos(angle), jnp.sin(angle)
        return jnp.concatenate([cosine, cosine], 1), jnp.concatenate([-sine, sine], 1)

    seq_pos = jnp.arange(seq, dtype=jnp.int32)
    cos_seq, sin_seq = angles_of(seq_pos)
    near_pos = source_planes[:, None] * count + jnp.arange(count, dtype=jnp.int32)[None]
    cos_near, sin_near = angles_of(near_pos.reshape(-1))
    kv_raw = dot(seq_a, w_kv_part).reshape(seq, part_heads, 2, HD)
    keys = kv_raw[:, :, 0]
    turned = jnp.concatenate([keys[..., HD // 2 :], keys[..., : HD // 2]], -1)
    keys = keys * cos_near[:, None] + turned * sin_near[:, None]
    kv_mine = jnp.stack([keys.astype(BF16), kv_raw[:, :, 1].astype(BF16)], 2)
    kv_mine = absolute(kv_mine.reshape(planes, count, 2 * kv_part)).reshape(seq, 2 * kv_part)
    kv_near = relay(kv_mine, "expert")

    seq_ints = near_ints[0]
    own_att = jnp.arange(local_att, dtype=jnp.int32) + plane * local_att
    att_ids = (target_planes[:, None] * local_att + jnp.arange(local_att)[None]).reshape(-1)
    mlp_ids = (target_planes[:, None] * local_mlp + near_local[None]).reshape(-1)
    att_slots = one_hot_slots(seq_ints[:, 1:3], own_att, cap)
    home_att = one_hot_slots(ints[None, 1:3], att_ids, cap)[0]
    home_mlp = one_hot_slots(ints[None, 3:5], mlp_ids, cap)[0]
    every_mlp = near_ints[:, :, 3:5].reshape(-1, 2, count)
    mlp_slots = one_hot_slots(every_mlp, mlp_expert[None], cap)[:, 0]
    other_expert = jnp.sum(every_mlp, 1) - mlp_expert
    row_other = jnp.sum(jnp.where(mlp_slots, other_expert[:, None, :], 0), -1).reshape(-1, 1)

    def by_choice(home, routes, ids):
        named = routes[:, None, :] == ids[None, :, None]
        picks = home[None] & named[:, :, None, :]
        return picks.astype(BF16).reshape(2, -1, count)

    pick_att = by_choice(home_att, ints[1:3], att_ids)
    pick_mlp = by_choice(home_mlp, ints[3:5], mlp_ids)
    flat_mlp = home_mlp.astype(BF16).reshape(n_mlp * cap, count)
    spread = att_slots.astype(BF16)
    row_pos = jnp.sum(
        jnp.where(att_slots, near_pos[:, None, None, :], 0), -1
    ).transpose(1, 0, 2).reshape(-1)
    row_seg = jnp.sum(
        jnp.where(att_slots, seq_ints[:, 0][:, None, None, :], 0), -1
    ).transpose(1, 0, 2).reshape(-1)
    seq_seg = absolute(seq_ints[:, 0]).reshape(seq)
    att_rows = planes * local_att * cap

    def to_expert(rows_half):
        held = shift(list(rows_half.reshape(planes, local_mlp, cap, width)), -1)
        held = jnp.stack(held, 1)
        sent = [held[k % local_mlp].reshape(planes * cap, width) for k in range(columns)]
        own = jnp.concatenate(cross(sent), 0)
        return own, swap(own)

    g_own, g_other = to_expert(dot(flat_mlp, cotangent).astype(BF16))
    raw = hidden_raw(core_at, g_own, g_other, w_dn)

    def gates_of(half_rows, router, routes):
        part = lax.dynamic_slice_in_dim(router, core * width, width, 0).astype(BF16)
        logits = core_sum(ein("de,td->et", part, half_rows))
        experts = router.shape[1]
        named = (
            routes[:, None, :] == jnp.arange(experts, dtype=jnp.int32)[None, :, None]
        ).astype(F32)
        chosen = jnp.sum(named * logits[None], 1)
        return jax.nn.softmax(chosen, axis=0), named, part

    gates_a, named_a, router_a = gates_of(rows_a_half, router_attn, ints[1:3])
    held_a = ein("slct,std->lscd", spread, seq_a.reshape(planes, count, full_width)).astype(BF16)
    held_a = held_a.reshape(local_att, planes * cap, full_width)
    cos_rows, sin_rows = angles_of(row_pos)
    query_raw = ein("lrd,ldf->lrf", held_a, whole_query).reshape(att_rows, feats)
    before = None
    order = [0, planes // 2] + [j for j in range(1, planes) if j != planes // 2]
    for j in order:
        before = att_forward(
            source_planes, query_raw, kv_near[j][None], cos_rows, sin_rows,
            row_pos[:, None], row_seg[:, None], seq_seg[None], j, before,
        )
    mixed_rows, query_rows = before
    mixed_owner = mixed_rows.reshape(local_att, planes * cap, feats)

    def halves(values, axis):
        mine = lax.dynamic_slice_in_dim(values, core * width, width, axis)
        theirs = lax.dynamic_slice_in_dim(values, (1 - core) * width, width, axis)
        return mine, theirs

    out_mine, out_theirs = halves(whole_output, 2)
    given = swap(ein("lrf,lfd->lrd", mixed_owner, out_theirs).astype(BF16))
    branch_a = ein("lrf,lfd->lrd", mixed_owner, out_mine) + given.astype(F32)
    branch_a = branch_a.astype(BF16).reshape(local_att, planes, cap, width)
    home_a = jnp.concatenate(
        shift([branch_a[:, j].reshape(local_att * cap, width) for j in range(planes)], 1), 0
    )
    taken_a = ein("jst,sd->jtd", pick_att, home_a)
    middle = residual + jnp.sum(gates_a[:, :, None] * taken_a, 0)

    scale_b = rms_scale(middle)
    rows_b_half = (middle * scale_b * norm_mlp).astype(BF16)
    gates_b, named_b, router_b = gates_of(rows_b_half, router_mlp, ints[3:5])
    x_own, x_other = to_expert(dot(flat_mlp, rows_b_half).astype(BF16))
    router_wide = jnp.pad(router_mlp.astype(BF16), ((0, 0), (0, HD - n_mlp)))
    place = jnp.stack([core, mlp_expert]).astype(jnp.int32)
    hidden, hidden_gated, grad_both, row_dgate = feed_forward(
        place, x_own, x_other, w_gu, raw, router_wide, row_other
    )

    def mlp_home(rows):
        tail = rows.shape[1:]
        got = cross(list(rows.reshape((columns, planes, cap) + tail)))
        sums = []
        for near in range(local_mlp):
            parts = [got[k].astype(F32) for k in range(near, columns, local_mlp)]
            sums.append(functools.reduce(jnp.add, parts).astype(rows.dtype))
        back = shift(
            [jnp.concatenate([part[j] for part in sums], 0) for j in range(planes)], 1
        )
        return jnp.concatenate(back, 0)

    dgate_home = mlp_home(core_sum(row_dgate[:, 0]))
    given = swap(rows_half(other_at, grad_both, w_gu, width))
    home_db = mlp_home(rows_half(core_at, grad_both, w_gu, width, given))

    def gates_back(gates, grad_gates, named):
        chosen = gates * (grad_gates - jnp.sum(gates * grad_gates, 0, keepdims=True))
        return jnp.sum(chosen[:, None, :] * named, 0).astype(BF16)

    grad_gates_b = jnp.sum(pick_mlp.astype(F32) * dgate_home[None, :, None], 1)
    grad_logit_b = gates_back(gates_b, grad_gates_b, named_b)
    grad_normed_b = ein("st,sd->td", flat_mlp, home_db) + ein("et,de->td", grad_logit_b, router_b)
    grad_router_b = ein("et,td->ed", grad_logit_b, rows_b_half)

    def normalize_back(values, gain, row_scale, grad_normed):
        inner = core_sum(jnp.sum(grad_normed * gain * values, 1, keepdims=True))
        grad_values = (
            row_scale * gain * grad_normed
            - values * (row_scale * row_scale * row_scale) * inner / full_width
        )
        return grad_values, jnp.sum(grad_normed * values * row_scale, 0)

    grad_out = cotangent.astype(F32)
    grad_mid_norm, grad_gain_b = normalize_back(middle, norm_mlp, scale_b, grad_normed_b)
    grad_middle = grad_out + grad_mid_norm

    grad_gates_a = core_sum(jnp.sum(grad_middle[None] * taken_a, 2))
    grad_logit_a = gates_back(gates_a, grad_gates_a, named_a)
    grad_taken_a = (gates_a[:, :, None] * grad_middle[None]).astype(BF16)
    sent_a = ein("jst,jtd->sd", pick_att, grad_taken_a).astype(BF16)
    got_a = shift(list(sent_a.reshape(planes, local_att, cap, width)), -1)
    held_grad_a = both_halves(
        jnp.stack(got_a, 1).reshape(local_att, planes * cap, width), core
    )
    grad_mixed = ein("lrd,lfd->lrf", held_grad_a, whole_output).astype(BF16)
    grad_query, grad_kv_seq = att_backward(
        source_planes, query_rows, grad_mixed.reshape(att_rows, feats),
        jnp.stack(kv_near, 0), cos_rows, sin_rows, cos_seq, sin_seq,
        row_pos[None], row_seg[None], seq_seg[:, None],
    )
    grad_query = grad_query.reshape(local_att, planes * cap, feats)
    grad_kv = lax.psum_scatter(grad_kv_seq, "expert", scatter_dimension=0, tiled=True)
    grad_kv = relative(grad_kv.reshape(planes, count, 2 * kv_part)).reshape(seq, 2 * kv_part)
    query_mine, query_theirs = halves(whole_query, 1)
    kvw_mine, kvw_theirs = halves(w_kv_part, 0)

    def grad_seq(query_half, kv_half):
        rows = ein("lrf,ldf->lrd", grad_query, query_half).astype(BF16)
        rows = ein("slct,lscd->std", spread, rows.reshape(local_att, planes, cap, width))
        return rows.reshape(seq, width) + ein("tf,df->td", grad_kv, kv_half)

    given = swap(grad_seq(query_theirs, kvw_theirs).astype(BF16))
    grad_seq_a = (grad_seq(query_mine, kvw_mine) + given.astype(F32)).astype(BF16)
    back_a = shift(list(grad_seq_a.reshape(planes, count, width)), 1)
    grad_rows_a = functools.reduce(jnp.add, [part.astype(F32) for part in back_a])
    grad_normed_a = grad_rows_a + ein("et,de->td", grad_logit_a, router_a)
    grad_router_a = ein("et,td->ed", grad_logit_a, rows_a_half)
    grad_in_norm, grad_gain_a = normalize_back(residual, norm_attn, scale_a, grad_normed_a)
    grad_tokens = grad_middle + grad_in_norm

    def absolute_halves(own, other):
        first = jnp.where(core == 0, own, other)
        second = jnp.where(core == 0, other, own)
        return jnp.concatenate([first, second], -1)

    x_rows = absolute_halves(x_own, x_other)
    g_rows = absolute_halves(g_own, g_other)
    grad_gu = ein("rd,rf->df", x_rows, grad_both).astype(BF16)
    got_gu = a2a(grad_gu.reshape(columns, depth, 2 * ff), "dp")
    grad_wgateup = unpack_gateup(got_gu.reshape(ff_parts, local_mlp, depth, 2 * ff), ff_parts)
    grad_dn = ein("rf,rsd->sfd", hidden_gated, g_rows.reshape(-1, columns, depth)).astype(BF16)
    got_dn = a2a(grad_dn, "dp")
    grad_wdown = unpack_down(got_dn.reshape(ff_parts, local_mlp, ff, depth))
    grad_woutput = lax.psum_scatter(
        ein("lrf,lrd->lfd", mixed_owner, held_grad_a).astype(BF16),
        "dp",
        scatter_dimension=2,
        tiled=True,
    ).astype(F32)
    grad_wquery = lax.psum_scatter(
        ein("lrd,lrf->ldf", held_a, grad_query).astype(BF16),
        "dp",
        scatter_dimension=1,
        tiled=True,
    ).astype(F32)
    grad_kv_w = lax.psum_scatter(
        ein("td,tf->df", seq_a, grad_kv).astype(BF16), "dp", scatter_dimension=0, tiled=True
    )
    grad_kv_w = a2a(
        grad_kv_w.reshape(planes, w_kv.shape[0], part_heads, 2, HD), "expert"
    )
    grad_wkv = grad_kv_w.transpose(1, 3, 0, 2, 4).astype(F32).reshape(w_kv.shape)

    given = swap(rows_half(other_at, hidden, w_dn, width))
    home_b = mlp_home(rows_half(core_at, hidden, w_dn, width, given))
    taken_b = ein("jst,sd->jtd", pick_mlp, home_b)
    output = middle + jnp.sum(gates_b[:, :, None] * taken_b, 0)

    small = jnp.concatenate(
        [grad_router_a, grad_router_b, grad_gain_a[None], grad_gain_b[None]], 0
    )
    small = total_over(total_over(small, "dp"), "expert")
    routers = both_halves(small[: n_att + n_mlp], core)
    return (
        output.astype(BF16),
        grad_tokens,
        small[n_att + n_mlp],
        small[n_att + n_mlp + 1],
        grad_wkv,
        routers[:n_att].T,
        routers[n_att:].T,
        grad_wquery,
        grad_woutput,
        grad_wgateup,
        grad_wdown,
    )


def solution(mesh):
    in_specs = (
        P(("dp", "expert"), "tensor"),
        P("tensor"),
        P("tensor"),
        P(("dp", "expert"), None, "tensor"),
        P(),
        P(),
        P("expert", "dp", "tensor"),
        P("expert", "tensor", "dp"),
        P("expert", "dp", None, "tensor"),
        P("expert", "tensor", "dp"),
        P(("dp", "expert")),
        P(("dp", "expert"), None),
        P(("dp", "expert"), None),
        P(("dp", "expert"), "tensor"),
    )
    out_specs = (
        P(("dp", "expert"), "tensor"),
        P(("dp", "expert"), "tensor"),
        P("tensor"),
        P("tensor"),
        P(("dp", "expert"), None, "tensor"),
        P(),
        P(),
        P("expert", "dp", "tensor"),
        P("expert", "tensor", "dp"),
        P("expert", "dp", None, "tensor"),
        P("expert", "tensor", "dp"),
    )
    return jax.shard_map(shards, mesh=mesh, in_specs=in_specs, out_specs=out_specs, check_vma=False)
```

```python
import functools
import math

import jax
import jax.numpy as jnp
from jax import lax
from jax.experimental import pallas as pl
from jax.experimental.pallas import tpu as pltpu
from jax.sharding import PartitionSpec as P

HD = 128
EPSILON = 1e-06
MASKED = -1000000000.0
F32 = jnp.float32
BF16 = jnp.bfloat16
LIMIT = 60 << 20
WEIGHT = 0.01
NT = (((1,), (1,)), ((), ()))
TN = (((0,), (0,)), ((), ()))


def dot(lhs, rhs):
    return jnp.dot(lhs, rhs, preferred_element_type=F32)


def ein(spec, lhs, rhs):
    return jnp.einsum(spec, lhs, rhs, preferred_element_type=F32)


def gdot(lhs, rhs, dims):
    return lax.dot_general(lhs, rhs, dims, preferred_element_type=F32)


def swap(values):
    return lax.ppermute(values, "tensor", [(0, 1), (1, 0)])


def a2a(values, axis):
    return lax.all_to_all(values, axis, split_axis=0, concat_axis=0, tiled=True)


def total_over(values, axis):
    count = lax.axis_size(axis)
    step = 1
    while step < count:
        values = values + lax.ppermute(values, axis, [(i, i ^ step) for i in range(count)])
        step *= 2
    return values


def core_sum(values):
    return values + swap(values)


def after(value, *done):
    return lax.optimization_barrier((value,) + done)[0]


def near_planes(values):
    count = lax.axis_size("expert")
    return [values] + [
        lax.ppermute(values, "expert", [(i, (i - j) % count) for i in range(count)])
        for j in range(1, count)
    ]


def relay(values, axis, *done):
    count = lax.axis_size(axis)
    up, down = [values], [values]
    for step in range(count - 1):
        if done and step == count - 2:
            up[-1] = after(up[-1], *done)
        up.append(lax.ppermute(up[-1], axis, [(i, i + 1) for i in range(count - 1)]))
        down.append(lax.ppermute(down[-1], axis, [(i + 1, i) for i in range(count - 1)]))
    return [values] + [down[j] + up[count - j] for j in range(1, count)]


def shift(blocks, sign):
    count = lax.axis_size("expert")
    return [blocks[0]] + [
        lax.ppermute(blocks[j], "expert", [(i, (i + sign * j) % count) for i in range(count)])
        for j in range(1, count)
    ]


def cross(blocks):
    count = lax.axis_size("dp")
    return [blocks[0]] + [
        lax.ppermute(blocks[k], "dp", [(i, i ^ k) for i in range(count)]) for k in range(1, count)
    ]


def both_halves(values, core):
    other = swap(values)
    first = jnp.where(core == 0, values, other)
    second = jnp.where(core == 0, other, values)
    return jnp.concatenate([first, second], -1)


def one_hot_slots(routes, experts, capacity):
    token_count = routes.shape[2]
    member = (routes[:, None, 0] == experts[None, :, None]) | (
        routes[:, None, 1] == experts[None, :, None]
    )
    tokens = jnp.arange(token_count, dtype=jnp.int32)
    upper = (tokens[:, None] < tokens[None, :]).astype(BF16)
    rank = dot(member.astype(BF16), upper).astype(jnp.int32)
    slots = jnp.arange(capacity, dtype=jnp.int32)
    return member[:, :, None, :] & (rank[:, :, None, :] == slots[None, None, :, None])


def params(*kinds):
    return pltpu.CompilerParams(dimension_semantics=kinds, vmem_limit_bytes=LIMIT)


def cost(flops, moved):
    return pl.CostEstimate(
        flops=int(flops * WEIGHT), bytes_accessed=int(moved * WEIGHT), transcendentals=0
    )


def pack_kernel(ff, parts, src, *outs):
    for half in range(2):
        for part in range(parts):
            outs[half][part, 0] = src[0, :, half, part * ff : (part + 1) * ff].astype(BF16)


def pack_gateup(weights, parts):
    local, depth, _, ff_core = weights.shape
    ff = ff_core // parts
    if ff % 128:
        moved = weights.reshape(local, depth, 2, parts, ff).transpose(2, 3, 0, 1, 4).astype(BF16)
        return moved[0], moved[1]
    rows = min(depth, 128)
    return pl.pallas_call(
        functools.partial(pack_kernel, ff, parts),
        grid=(local, depth // rows),
        in_specs=[pl.BlockSpec((1, rows, 2, ff_core), lambda l, r: (l, r, 0, 0))],
        out_specs=[pl.BlockSpec((parts, 1, rows, ff), lambda l, r: (0, l, r, 0))] * 2,
        out_shape=[jax.ShapeDtypeStruct((parts, local, depth, ff), BF16)] * 2,
        compiler_params=params("parallel", "parallel"),
        cost_estimate=cost(0, weights.size * 6),
        name="pack_gateup",
    )(weights)


def unpack_kernel(ff, parts, gate, up, out):
    for half, src in enumerate((gate, up)):
        for part in range(parts):
            out[0, :, half, part * ff : (part + 1) * ff] = src[part, 0].astype(F32)


def unpack_gateup(gate, up):
    parts, local, depth, ff = gate.shape
    if ff % 128:
        moved = jnp.stack([gate, up], 0).transpose(2, 3, 0, 1, 4)
        return moved.astype(F32).reshape(local, depth, 2, parts * ff)
    rows = min(depth, 128)
    return pl.pallas_call(
        functools.partial(unpack_kernel, ff, parts),
        grid=(local, depth // rows),
        in_specs=[pl.BlockSpec((parts, 1, rows, ff), lambda l, r: (0, l, r, 0))] * 2,
        out_specs=pl.BlockSpec((1, rows, 2, parts * ff), lambda l, r: (l, r, 0, 0)),
        out_shape=jax.ShapeDtypeStruct((local, depth, 2, parts * ff), F32),
        compiler_params=params("parallel", "parallel"),
        cost_estimate=cost(0, gate.size * 12),
        name="unpack_gateup",
    )(gate, up)


def cast_kernel(src, out):
    out[...] = src[...].reshape(out.shape).astype(out.dtype)


def pack_down(weights, parts):
    local, ff_core, depth = weights.shape
    ff = ff_core // parts
    return pl.pallas_call(
        cast_kernel,
        grid=(parts, local),
        in_specs=[pl.BlockSpec((1, ff, depth), lambda p, l: (l, p, 0))],
        out_specs=pl.BlockSpec((1, 1, ff, depth), lambda p, l: (p, l, 0, 0)),
        out_shape=jax.ShapeDtypeStruct((parts, local, ff, depth), BF16),
        compiler_params=params("parallel", "parallel"),
        cost_estimate=cost(0, weights.size * 6),
        name="pack_down",
    )(weights)


def unpack_down(grads):
    parts, local, ff, depth = grads.shape
    return pl.pallas_call(
        cast_kernel,
        grid=(parts, local),
        in_specs=[pl.BlockSpec((1, 1, ff, depth), lambda p, l: (p, l, 0, 0))],
        out_specs=pl.BlockSpec((1, ff, depth), lambda p, l: (l, p, 0)),
        out_shape=jax.ShapeDtypeStruct((local, parts * ff, depth), F32),
        compiler_params=params("parallel", "parallel"),
        cost_estimate=cost(0, grads.size * 6),
        name="unpack_down",
    )(grads)


def turn(values, cosine, sine):
    return values * cosine + pltpu.roll(values, HD // 2, 1) * sine


def att_fwd_kernel(
    place, q_in, kv, cos, sin, row_pos, row_seg, key_seg, *rest
):
    o_out, q_out = rest[-2:]
    query = turn(q_in[...], cos[...], sin[...]).astype(BF16)
    q_out[...] = query
    scores = gdot(query, kv[0, :, :HD], NT) * (1.0 / math.sqrt(HD))
    key_pos = lax.broadcasted_iota(jnp.int32, scores.shape, 1)
    allowed = (row_seg[...] == key_seg[...]) & (row_pos[...] >= key_pos)
    scores = jnp.where(allowed, scores, MASKED)
    peak = jnp.max(scores, 1, keepdims=True)
    weight = jnp.exp(scores - peak)
    mass = jnp.sum(weight, 1, keepdims=True)
    soft = (weight * (1.0 / mass)).astype(BF16)
    o_out[...] = dot(soft, kv[0, :, HD:]).astype(BF16)


def att_forward(place, q_raw, kv, cos, sin, row_pos, row_seg, key_seg, group, before):
    rows, feats = q_raw.shape
    seq, wide = kv.shape[1:]
    group_heads = wide // (2 * HD)
    block = min(256, rows)
    head = lambda h, i, place: (i, place[group] * group_heads + h)
    row = lambda h, i, place: (i, 0)
    in_specs = [
        pl.BlockSpec((block, HD), head),
        pl.BlockSpec((1, seq, 2 * HD), lambda h, i, place: (0, 0, h)),
        pl.BlockSpec((block, HD), row),
        pl.BlockSpec((block, HD), row),
        pl.BlockSpec((block, 1), row),
        pl.BlockSpec((block, 1), row),
        pl.BlockSpec((1, seq), lambda h, i, place: (0, 0)),
    ]
    operands = [place, q_raw, kv, cos, sin, row_pos, row_seg, key_seg]
    aliases = {}
    if before is not None:
        in_specs += [pl.BlockSpec(memory_space=pl.ANY)] * 2
        operands += list(before)
        aliases = {8: 0, 9: 1}
    return pl.pallas_call(
        att_fwd_kernel,
        grid_spec=pltpu.PrefetchScalarGridSpec(
            num_scalar_prefetch=1,
            grid=(group_heads, rows // block),
            in_specs=in_specs,
            out_specs=[pl.BlockSpec((block, HD), head)] * 2,
        ),
        out_shape=[jax.ShapeDtypeStruct((rows, feats), BF16)] * 2,
        input_output_aliases=aliases,
        compiler_params=params("arbitrary", "arbitrary"),
        cost_estimate=cost(40 * rows * seq * HD * group_heads, rows * feats * 4),
        name="attention_fwd",
    )(*operands)


def att_bwd_kernel(
    place, q_in, do_in, kv, cos, sin, key_cos, key_sin, row_pos, row_seg, key_seg, *rest
):
    dq_out, dkv_out, dk_sum, dv_sum = rest[-4:]
    step = pl.program_id(1)
    scale = 1.0 / math.sqrt(HD)
    query, grad_out = q_in[...], do_in[...]
    keys, values = kv[0, :, :HD], kv[0, :, HD:]
    scores = gdot(keys, query, NT) * scale
    key_pos = lax.broadcasted_iota(jnp.int32, scores.shape, 0)
    allowed = (row_seg[...] == key_seg[...]) & (row_pos[...] >= key_pos)
    scores = jnp.where(allowed, scores, MASKED)
    peak = jnp.max(scores, 0, keepdims=True)
    weight = jnp.exp(scores - peak)
    soft = weight * (1.0 / jnp.sum(weight, 0, keepdims=True))
    grad_soft = gdot(values, grad_out, NT)
    inner = jnp.sum(soft * grad_soft, 0, keepdims=True)
    grad_scores = (soft * (grad_soft - inner)).astype(BF16)
    grad_query = gdot(grad_scores, keys, TN) * scale
    dq_out[...] = turn(grad_query, cos[...], -sin[...]).astype(BF16)

    @pl.when(step == 0)
    def _():
        dk_sum[...] = jnp.zeros_like(dk_sum)
        dv_sum[...] = jnp.zeros_like(dv_sum)

    dk_sum[...] += dot(grad_scores, query)
    dv_sum[...] += dot(soft.astype(BF16), grad_out)

    @pl.when(step == pl.num_programs(1) - 1)
    def _():
        grad_keys = turn(dk_sum[...] * scale, key_cos[...], -key_sin[...])
        dkv_out[0, :, :HD] = grad_keys.astype(BF16)
        dkv_out[0, :, HD:] = dv_sum[...].astype(BF16)


def att_backward(
    place, query, grad_mixed, kv, cos, sin, key_cos, key_sin, row_pos, row_seg, key_seg,
    group, before,
):
    rows, feats = query.shape
    _, seq, wide = kv.shape
    group_heads = wide // (2 * HD)
    block = min(256, rows)
    head = lambda h, i, place: (i, place[group] * group_heads + h)
    row = lambda h, i, place: (i, 0)
    lane = lambda h, i, place: (0, i)
    whole = lambda h, i, place: (0, 0)
    pair = lambda h, i, place: (0, 0, h)
    in_specs = [
        pl.BlockSpec((block, HD), head),
        pl.BlockSpec((block, HD), head),
        pl.BlockSpec((1, seq, 2 * HD), pair),
        pl.BlockSpec((block, HD), row),
        pl.BlockSpec((block, HD), row),
        pl.BlockSpec((seq, HD), whole),
        pl.BlockSpec((seq, HD), whole),
        pl.BlockSpec((1, block), lane),
        pl.BlockSpec((1, block), lane),
        pl.BlockSpec((seq, 1), whole),
    ]
    operands = [
        place, query, grad_mixed, kv, cos, sin, key_cos, key_sin, row_pos, row_seg, key_seg
    ]
    aliases = {}
    if before is not None:
        in_specs.append(pl.BlockSpec(memory_space=pl.ANY))
        operands.append(before)
        aliases = {11: 0}
    return pl.pallas_call(
        att_bwd_kernel,
        grid_spec=pltpu.PrefetchScalarGridSpec(
            num_scalar_prefetch=1,
            grid=(group_heads, rows // block),
            in_specs=in_specs,
            out_specs=[
                pl.BlockSpec((block, HD), head),
                pl.BlockSpec((1, seq, 2 * HD), pair),
            ],
            scratch_shapes=[pltpu.VMEM((seq, HD), F32)] * 2,
        ),
        out_shape=[
            jax.ShapeDtypeStruct((rows, feats), BF16),
            jax.ShapeDtypeStruct((1, seq, wide), BF16),
        ],
        input_output_aliases=aliases,
        compiler_params=params("arbitrary", "arbitrary"),
        cost_estimate=cost(60 * rows * seq * HD * group_heads, rows * feats * 4),
        name="attention_bwd",
    )(*operands)


def raw_kernel(core, g_own, g_other, w_dn, out):
    columns = w_dn.shape[0]
    half, depth = columns // 2, w_dn.shape[2]
    total = jnp.zeros(out.shape, F32)
    for i in range(half):
        part = slice(i * depth, (i + 1) * depth)
        total += gdot(g_own[:, part], w_dn[core[0] * half + i], NT)
        total += gdot(g_other[:, part], w_dn[(1 - core[0]) * half + i], NT)
    out[...] = total


def hidden_raw(core, g_own, g_other, w_dn):
    rows, width = g_own.shape
    columns, ff, depth = w_dn.shape
    block = 256
    return pl.pallas_call(
        raw_kernel,
        grid_spec=pltpu.PrefetchScalarGridSpec(
            num_scalar_prefetch=1,
            grid=(rows // block,),
            in_specs=[
                pl.BlockSpec((block, width), lambda i, c: (i, 0)),
                pl.BlockSpec((block, width), lambda i, c: (i, 0)),
                pl.BlockSpec(
                    (columns, ff, depth), lambda i, c: (0, 0, 0), pipeline_mode=pl.Buffered(1)
                ),
            ],
            out_specs=pl.BlockSpec((block, ff), lambda i, c: (i, 0)),
        ),
        out_shape=jax.ShapeDtypeStruct((rows, ff), F32),
        compiler_params=params("arbitrary"),
        cost_estimate=cost(2 * w_dn.size * rows, w_dn.size * 2 + rows * ff * 4),
        name="hidden_raw",
    )(core, g_own, g_other, w_dn)


def ff_kernel(
    place, x_own, x_other, w_gate, w_up, raw, router, other, hid, hid_gated, du, dw, dgate
):
    core, expert = place[0], place[1]
    width = x_own.shape[1]
    mine = pl.ds(pl.multiple_of(core * width, width), width)
    theirs = pl.ds(pl.multiple_of((1 - core) * width, width), width)

    def product(weights):
        return dot(x_own[...], weights[mine, :]) + dot(x_other[...], weights[theirs, :])

    logits = product(router)
    lanes = lax.broadcasted_iota(jnp.int32, logits.shape, 1)
    own_logit = jnp.sum(jnp.where(lanes == expert, logits, 0.0), 1, keepdims=True)
    other_logit = jnp.sum(jnp.where(lanes == other[...], logits, 0.0), 1, keepdims=True)
    gate = jax.nn.sigmoid(own_logit - other_logit)
    gate_part, up_part = product(w_gate), product(w_up)
    sig = 1.0 / (1.0 + jnp.exp(-gate_part))
    silu = gate_part * sig
    hidden = silu * up_part
    hid[...] = hidden.astype(BF16)
    hid_gated[...] = (hidden * gate).astype(BF16)
    dgate[...] = jnp.sum(hidden * raw[...], 1, keepdims=True)
    grad_hidden = raw[...] * gate
    du[...] = (grad_hidden * up_part * (sig * (1.0 + gate_part * (1.0 - sig)))).astype(BF16)
    dw[...] = (grad_hidden * silu).astype(BF16)


def feed_forward(place, x_own, x_other, w_gate, w_up, raw, router, other):
    rows, width = x_own.shape
    ff = raw.shape[1]
    block = 256
    row = lambda i, c: (i, 0)
    whole = lambda i, c: (0, 0)
    fixed = lambda array: pl.BlockSpec(array.shape, whole, pipeline_mode=pl.Buffered(1))
    return pl.pallas_call(
        ff_kernel,
        grid_spec=pltpu.PrefetchScalarGridSpec(
            num_scalar_prefetch=1,
            grid=(rows // block,),
            in_specs=[
                pl.BlockSpec((block, width), row),
                pl.BlockSpec((block, width), row),
                fixed(w_gate),
                fixed(w_up),
                pl.BlockSpec((block, ff), row),
                fixed(router),
                pl.BlockSpec((block, 1), row),
            ],
            out_specs=[pl.BlockSpec((block, ff), row)] * 4 + [pl.BlockSpec((block, 1), row)],
        ),
        out_shape=[jax.ShapeDtypeStruct((rows, ff), BF16)] * 4
        + [jax.ShapeDtypeStruct((rows, 1), F32)],
        compiler_params=params("arbitrary"),
        cost_estimate=cost(5 * w_gate.size * rows, w_gate.size * 4 + rows * ff * 12),
        name="feed_forward",
    )(place, x_own, x_other, w_gate, w_up, raw, router, other)


def rows_kernel(count, which, *refs):
    out = refs[-1]
    total = None
    for lhs, weights in zip(refs[:count], refs[count : 2 * count]):
        if len(weights.shape) == 2:
            part = gdot(lhs[...], weights[...], NT)
        else:
            part = jnp.concatenate(
                [dot(lhs[...], weights[i]) for i in range(weights.shape[0])], 1
            )
        total = part if total is None else total + part
    if len(refs) > 2 * count + 1:
        total = total + refs[2 * count][...].astype(F32)
    out[...] = total.astype(BF16)


def rows_half(which, lhs, weights, width, add=None):
    rows = lhs[0].shape[0]
    block = 256
    row = lambda i, c: (i, 0)
    in_specs = [pl.BlockSpec((block, array.shape[1]), row) for array in lhs]
    for array in weights:
        if array.ndim == 2:
            shape, index = (width, array.shape[1]), lambda i, c: (c[0], 0)
        else:
            shape = (array.shape[0] // 2,) + array.shape[1:]
            index = lambda i, c: (c[0], 0, 0)
        in_specs.append(pl.BlockSpec(shape, index, pipeline_mode=pl.Buffered(1)))
    operands = [which, *lhs, *weights]
    if add is not None:
        in_specs.append(pl.BlockSpec((block, width), row))
        operands.append(add)
    return pl.pallas_call(
        functools.partial(rows_kernel, len(lhs)),
        grid_spec=pltpu.PrefetchScalarGridSpec(
            num_scalar_prefetch=1,
            grid=(rows // block,),
            in_specs=in_specs,
            out_specs=pl.BlockSpec((block, width), row),
        ),
        out_shape=jax.ShapeDtypeStruct((rows, width), BF16),
        compiler_params=params("arbitrary"),
        cost_estimate=cost(sum(array.size for array in weights) * rows, rows * width * 4),
        name="rows_half",
    )(*operands)


def gu_outer_kernel(core, x_own, x_other, duw, out):
    half = pl.num_programs(0) // 2
    mine = (pl.program_id(0) // half) == core[0]

    @pl.when(mine)
    def _():
        out[0] = gdot(x_own[...], duw[...], TN).astype(BF16)

    @pl.when(jnp.logical_not(mine))
    def _():
        out[0] = gdot(x_other[...], duw[...], TN).astype(BF16)


def gu_outer(core, x_own, x_other, duw, columns):
    rows, width = x_own.shape
    half = columns // 2
    depth = width // half
    part = lambda s, c: (0, lax.rem(s, half))
    return pl.pallas_call(
        gu_outer_kernel,
        grid_spec=pltpu.PrefetchScalarGridSpec(
            num_scalar_prefetch=1,
            grid=(columns,),
            in_specs=[
                pl.BlockSpec((rows, depth), part),
                pl.BlockSpec((rows, depth), part),
                pl.BlockSpec(duw.shape, lambda s, c: (0, 0), pipeline_mode=pl.Buffered(1)),
            ],
            out_specs=pl.BlockSpec((1, depth, duw.shape[1]), lambda s, c: (s, 0, 0)),
        ),
        out_shape=jax.ShapeDtypeStruct((columns, depth, duw.shape[1]), BF16),
        compiler_params=params("arbitrary"),
        cost_estimate=cost(2 * rows * 2 * width * duw.shape[1], rows * width * 8),
        name="grad_gateup",
    )(core, x_own, x_other, duw)


def dn_outer_kernel(core, hid, g_own, g_other, out):
    half = pl.num_programs(0) // 2
    mine = (pl.program_id(0) // half) == core[0]

    @pl.when(mine)
    def _():
        out[0] = gdot(hid[...], g_own[...], TN).astype(BF16)

    @pl.when(jnp.logical_not(mine))
    def _():
        out[0] = gdot(hid[...], g_other[...], TN).astype(BF16)


def dn_outer(core, hid, g_own, g_other, columns):
    rows, width = g_own.shape
    half = columns // 2
    depth = width // half
    ff = hid.shape[1]
    part = lambda s, c: (0, lax.rem(s, half))
    return pl.pallas_call(
        dn_outer_kernel,
        grid_spec=pltpu.PrefetchScalarGridSpec(
            num_scalar_prefetch=1,
            grid=(columns,),
            in_specs=[
                pl.BlockSpec(hid.shape, lambda s, c: (0, 0), pipeline_mode=pl.Buffered(1)),
                pl.BlockSpec((rows, depth), part),
                pl.BlockSpec((rows, depth), part),
            ],
            out_specs=pl.BlockSpec((1, ff, depth), lambda s, c: (s, 0, 0)),
        ),
        out_shape=jax.ShapeDtypeStruct((columns, ff, depth), BF16),
        compiler_params=params("arbitrary"),
        cost_estimate=cost(2 * rows * 2 * width * ff, rows * width * 8),
        name="grad_down",
    )(core, hid, g_own, g_other)


def shards(
    tokens,
    norm_attn,
    norm_mlp,
    w_kv,
    router_attn,
    router_mlp,
    w_query,
    w_output,
    w_gateup,
    w_down,
    segments,
    att_routes,
    mlp_routes,
    cotangent,
):
    count, width = tokens.shape
    full_width = 2 * width
    planes = lax.axis_size("expert")
    columns = lax.axis_size("dp")
    plane = lax.axis_index("expert")
    column = lax.axis_index("dp")
    core = lax.axis_index("tensor")
    n_att = router_attn.shape[1]
    n_mlp = router_mlp.shape[1]
    local_att = w_query.shape[0]
    local_mlp = w_gateup.shape[0]
    ff_parts = columns // local_mlp
    depth = w_gateup.shape[1]
    ff = w_gateup.shape[3] // ff_parts
    cap = 3 * count // 8
    seq = planes * count
    feats = w_query.shape[2]
    kv_part = feats // planes
    part_heads = kv_part // HD
    own_local = column % local_mlp
    mlp_expert = plane * local_mlp + own_local
    steps = jnp.arange(planes, dtype=jnp.int32)
    source_planes = (plane + steps) % planes
    target_planes = (plane - steps + planes) % planes
    near_local = own_local ^ jnp.arange(local_mlp, dtype=jnp.int32)
    core_at = core.astype(jnp.int32)[None]
    other_at = 1 - core_at

    def absolute(blocks):
        twice = jnp.concatenate([blocks, blocks], 0)
        return lax.dynamic_slice_in_dim(twice, (planes - plane) % planes, planes, 0)

    def relative(blocks):
        twice = jnp.concatenate([blocks, blocks], 0)
        return lax.dynamic_slice_in_dim(twice, plane, planes, 0)

    def relative_down(blocks):
        twice = jnp.concatenate([blocks[::-1], blocks[::-1]], 0)
        return lax.dynamic_slice_in_dim(twice, planes - 1 - plane, planes, 0)

    kv_send = w_kv.astype(BF16).reshape(w_kv.shape[0], 2, planes, part_heads, HD)
    near_tokens = near_planes(tokens)
    kv_send = absolute(jnp.stack(shift(list(relative_down(kv_send.transpose(2, 0, 3, 1, 4))), -1), 0))
    w_kv_part = lax.all_gather(kv_send, "dp", axis=0, tiled=True).reshape(
        full_width, 2 * kv_part
    )
    whole_query = lax.all_gather(
        after(w_query.astype(BF16), kv_send), "dp", axis=1, tiled=True
    )
    whole_output = lax.all_gather(w_output.astype(BF16), "dp", axis=2, tiled=True)
    down_send = pack_down(w_down, ff_parts).reshape(columns, ff, depth)
    gate_send, up_send = pack_gateup(w_gateup, ff_parts)
    w_dn = a2a(down_send, "dp")
    w_gate = a2a(gate_send.reshape(columns, depth, ff), "dp").reshape(full_width, ff)
    w_up = a2a(up_send.reshape(columns, depth, ff), "dp").reshape(full_width, ff)

    ints = jnp.concatenate(
        [
            segments[None],
            att_routes.T,
            mlp_routes.T,
            jnp.zeros((3, count), jnp.int32),
        ],
        0,
    )
    near_ints = jnp.stack(near_planes(ints), 0)[None]
    step = 1
    while step < columns:
        pairs = [(i, i ^ step) for i in range(columns)]
        near_ints = jnp.concatenate([near_ints, lax.ppermute(near_ints, "dp", pairs)], 0)
        step *= 2

    residual = tokens.astype(F32)
    near_tokens[-1] = after(near_tokens[-1], down_send, gate_send, up_send)
    seq_res = jnp.concatenate(near_tokens, 0).astype(F32)

    def rms_scale(values):
        return lax.rsqrt(
            core_sum(jnp.sum(values * values, 1, keepdims=True)) / full_width + EPSILON
        )

    seq_scale = rms_scale(seq_res)
    seq_a_half = (seq_res * seq_scale * norm_attn).astype(BF16)
    scale_a = seq_scale[:count]
    rows_a_half = seq_a_half[:count]
    seq_a = both_halves(seq_a_half, core)

    def angles_of(positions):
        frequency = jnp.exp(
            jnp.arange(HD // 2, dtype=F32) * (-2.0 * math.log(10000.0) / HD)
        )
        angle = positions.astype(F32)[:, None] * frequency[None, :]
        cosine, sine = jnp.cos(angle), jnp.sin(angle)
        return jnp.concatenate([cosine, cosine], 1), jnp.concatenate([-sine, sine], 1)

    seq_pos = jnp.arange(seq, dtype=jnp.int32)
    cos_seq, sin_seq = angles_of(seq_pos)
    near_pos = source_planes[:, None] * count + jnp.arange(count, dtype=jnp.int32)[None]
    cos_near, sin_near = angles_of(near_pos.reshape(-1))
    kv_raw = dot(seq_a, w_kv_part).reshape(seq, part_heads, 2, HD)
    keys = kv_raw[:, :, 0]
    turned = jnp.concatenate([keys[..., HD // 2 :], keys[..., : HD // 2]], -1)
    keys = keys * cos_near[:, None] + turned * sin_near[:, None]
    kv_mine = jnp.stack([keys.astype(BF16), kv_raw[:, :, 1].astype(BF16)], 2)
    kv_mine = absolute(kv_mine.reshape(planes, count, 2 * kv_part)).reshape(seq, 2 * kv_part)
    kv_near = relay(kv_mine, "expert", w_dn)

    seq_ints = near_ints[0]
    own_att = jnp.arange(local_att, dtype=jnp.int32) + plane * local_att
    att_ids = (target_planes[:, None] * local_att + jnp.arange(local_att)[None]).reshape(-1)
    mlp_ids = (target_planes[:, None] * local_mlp + near_local[None]).reshape(-1)
    att_slots = one_hot_slots(seq_ints[:, 1:3], own_att, cap)
    home_att = one_hot_slots(ints[None, 1:3], att_ids, cap)[0]
    home_mlp = one_hot_slots(ints[None, 3:5], mlp_ids, cap)[0]
    every_mlp = near_ints[:, :, 3:5].reshape(-1, 2, count)
    mlp_slots = one_hot_slots(every_mlp, mlp_expert[None], cap)[:, 0]
    other_expert = jnp.sum(every_mlp, 1) - mlp_expert
    row_other = jnp.sum(jnp.where(mlp_slots, other_expert[:, None, :], 0), -1).reshape(-1, 1)

    def by_choice(home, routes, ids):
        named = routes[:, None, :] == ids[None, :, None]
        picks = home[None] & named[:, :, None, :]
        return picks.astype(BF16).reshape(2, -1, count)

    pick_att = by_choice(home_att, ints[1:3], att_ids)
    pick_mlp = by_choice(home_mlp, ints[3:5], mlp_ids)
    flat_mlp = home_mlp.astype(BF16).reshape(n_mlp * cap, count)
    spread = att_slots.astype(BF16)
    row_pos = jnp.sum(
        jnp.where(att_slots, near_pos[:, None, None, :], 0), -1
    ).transpose(1, 0, 2).reshape(-1)
    row_seg = jnp.sum(
        jnp.where(att_slots, seq_ints[:, 0][:, None, None, :], 0), -1
    ).transpose(1, 0, 2).reshape(-1)
    seq_seg = absolute(seq_ints[:, 0]).reshape(seq)
    att_rows = planes * local_att * cap

    def to_plane(rows_half):
        return shift(list(rows_half.reshape(planes, local_mlp, cap, width)), -1)

    def to_expert(held, early=(), late=()):
        held[-1] = after(held[-1], *early)
        held = jnp.stack(held, 1)
        sent = [held[k % local_mlp].reshape(planes * cap, width) for k in range(columns)]
        got = cross(sent)
        got[-1] = after(got[-1], *late)
        own = jnp.concatenate(got, 0)
        return own, swap(own)

    g_held = to_plane(dot(flat_mlp, after(cotangent, kv_near[1], kv_near[-1])).astype(BF16))

    def gates_of(half_rows, router, routes):
        part = lax.dynamic_slice_in_dim(router, core * width, width, 0).astype(BF16)
        logits = core_sum(ein("de,td->et", part, half_rows))
        experts = router.shape[1]
        named = (
            routes[:, None, :] == jnp.arange(experts, dtype=jnp.int32)[None, :, None]
        ).astype(F32)
        chosen = jnp.sum(named * logits[None], 1)
        return jax.nn.softmax(chosen, axis=0), named, part

    gates_a, named_a, router_a = gates_of(rows_a_half, router_attn, ints[1:3])
    held_a = ein("slct,std->lscd", spread, seq_a.reshape(planes, count, full_width)).astype(BF16)
    held_a = held_a.reshape(local_att, planes * cap, full_width)
    cos_rows, sin_rows = angles_of(row_pos)
    query_raw = ein("lrd,ldf->lrf", held_a, whole_query).reshape(att_rows, feats)
    before = None
    order = [0, planes // 2] + [j for j in range(1, planes) if j != planes // 2]
    for j in order:
        before = att_forward(
            source_planes, query_raw, kv_near[j][None], cos_rows, sin_rows,
            row_pos[:, None], row_seg[:, None], seq_seg[None], j, before,
        )
    mixed_rows, query_rows = before
    mixed_rows = after(mixed_rows, w_gate)
    mixed_owner = mixed_rows.reshape(local_att, planes * cap, feats)

    def halves(values, axis):
        mine = lax.dynamic_slice_in_dim(values, core * width, width, axis)
        theirs = lax.dynamic_slice_in_dim(values, (1 - core) * width, width, axis)
        return mine, theirs

    out_mine, out_theirs = halves(whole_output, 2)
    given = swap(ein("lrf,lfd->lrd", mixed_owner, out_theirs).astype(BF16))
    g_own, g_other = to_expert(g_held, (), (given,))
    raw = hidden_raw(core_at, g_own, g_other, w_dn)
    branch_a = ein("lrf,lfd->lrd", mixed_owner, out_mine) + given.astype(F32)
    branch_a = branch_a.astype(BF16).reshape(local_att, planes, cap, width)
    home_a = jnp.concatenate(
        shift([branch_a[:, j].reshape(local_att * cap, width) for j in range(planes)], 1), 0
    )
    taken_a = ein("jst,sd->jtd", pick_att, home_a)
    middle = residual + jnp.sum(gates_a[:, :, None] * taken_a, 0)

    scale_b = rms_scale(middle)
    rows_b_half = (middle * scale_b * norm_mlp).astype(BF16)
    gates_b, named_b, router_b = gates_of(rows_b_half, router_mlp, ints[3:5])
    x_own, x_other = to_expert(
        to_plane(dot(flat_mlp, rows_b_half).astype(BF16)), (raw,), (w_up,)
    )
    router_wide = jnp.pad(router_mlp.astype(BF16), ((0, 0), (0, HD - n_mlp)))
    place = jnp.stack([core, mlp_expert]).astype(jnp.int32)
    hidden, hidden_gated, grad_gate, grad_up, row_dgate = feed_forward(
        place, x_own, x_other, w_gate, w_up, raw, router_wide, row_other
    )

    def over_parts(rows, *done):
        tail = rows.shape[1:]
        got = cross(list(rows.reshape((columns, planes, cap) + tail)))
        there = got[1:]
        got[-1] = after(got[-1], *done)
        sums = []
        for near in range(local_mlp):
            parts = [got[k].astype(F32) for k in range(near, columns, local_mlp)]
            sums.append(functools.reduce(jnp.add, parts).astype(rows.dtype))
        return [jnp.concatenate([part[j] for part in sums], 0) for j in range(planes)], there

    def mlp_home(blocks, *done):
        back = shift(blocks, 1)
        there = back[1:]
        back[-1] = after(back[-1], *done)
        return jnp.concatenate(back, 0), there

    dgate_blocks, dgate_there = over_parts(core_sum(row_dgate[:, 0]))
    dgate_home, dgate_back = mlp_home(dgate_blocks)
    branch_theirs = rows_half(other_at, (hidden,), (w_dn,), width)
    given = swap(branch_theirs)
    grad_wgate = gu_outer(core_at, x_own, x_other, after(grad_gate, branch_theirs), columns)
    branch_b = rows_half(core_at, (after(hidden, grad_wgate),), (w_dn,), width, given)
    branch_blocks, branch_there = over_parts(after(branch_b, *dgate_there))
    home_b, branch_back = mlp_home(branch_blocks)
    grad_pair = (after(grad_gate, branch_b), grad_up)
    given = swap(rows_half(other_at, grad_pair, (w_gate, w_up), width))
    db_rows = rows_half(core_at, grad_pair, (w_gate, w_up), width, given)
    grad_wup = gu_outer(core_at, x_own, x_other, after(grad_up, db_rows, *dgate_back), columns)
    grad_wdn = dn_outer(core_at, after(hidden_gated, grad_wup), g_own, g_other, columns)
    db_blocks, db_there = over_parts(
        after(db_rows, *branch_there), grad_wdn, *branch_back
    )
    home_db, _ = mlp_home(db_blocks)
    got_gate = a2a(after(grad_wgate, *db_there), "dp")
    got_up = a2a(grad_wup, "dp")
    got_dn = a2a(grad_wdn, "dp")

    def gates_back(gates, grad_gates, named):
        chosen = gates * (grad_gates - jnp.sum(gates * grad_gates, 0, keepdims=True))
        return jnp.sum(chosen[:, None, :] * named, 0).astype(BF16)

    grad_gates_b = jnp.sum(pick_mlp.astype(F32) * dgate_home[None, :, None], 1)
    grad_logit_b = gates_back(gates_b, grad_gates_b, named_b)
    grad_normed_b = ein("st,sd->td", flat_mlp, home_db) + ein("et,de->td", grad_logit_b, router_b)
    grad_router_b = ein("et,td->ed", grad_logit_b, rows_b_half)

    def normalize_back(values, gain, row_scale, grad_normed):
        inner = core_sum(jnp.sum(grad_normed * gain * values, 1, keepdims=True))
        grad_values = (
            row_scale * gain * grad_normed
            - values * (row_scale * row_scale * row_scale) * inner / full_width
        )
        return grad_values, jnp.sum(grad_normed * values * row_scale, 0)

    grad_out = cotangent.astype(F32)
    grad_mid_norm, grad_gain_b = normalize_back(middle, norm_mlp, scale_b, grad_normed_b)
    grad_middle = grad_out + grad_mid_norm

    grad_gates_a = core_sum(jnp.sum(grad_middle[None] * taken_a, 2))
    grad_logit_a = gates_back(gates_a, grad_gates_a, named_a)
    grad_taken_a = (gates_a[:, :, None] * grad_middle[None]).astype(BF16)
    sent_a = ein("jst,jtd->sd", pick_att, grad_taken_a).astype(BF16)
    sent_a = after(sent_a, got_gate)
    got_a = shift(list(sent_a.reshape(planes, local_att, cap, width)), -1)
    got_a[-1] = after(got_a[-1], got_up)
    held_grad_a = both_halves(
        jnp.stack(got_a, 1).reshape(local_att, planes * cap, width), core
    )
    grad_mixed = ein("lrd,lfd->lrf", held_grad_a, whole_output).astype(BF16)
    grad_wo = ein("lrf,lrd->lfd", mixed_owner, held_grad_a).astype(BF16)
    grad_woutput = lax.psum_scatter(grad_wo, "dp", scatter_dimension=2, tiled=True).astype(F32)
    grad_query = None
    sent_kv = [None] * planes
    for j in [planes // 2] + [j for j in range(1, planes) if j != planes // 2] + [0]:
        if j == 1:
            grad_query = after(grad_query, grad_wo)
        grad_query, grad_kv_group = att_backward(
            source_planes, query_rows, grad_mixed.reshape(att_rows, feats), kv_near[j][None],
            cos_rows, sin_rows, cos_seq, sin_seq, row_pos[None], row_seg[None],
            seq_seg[:, None], j, grad_query,
        )
        sent_kv[j] = grad_kv_group[0]
    grad_query = grad_query.reshape(local_att, planes * cap, feats)
    got_kv = shift(sent_kv, 1)
    grad_wq = ein(
        "lrd,lrf->ldf", after(held_a, got_kv[planes // 2], got_dn), grad_query
    ).astype(BF16)
    taken_b = ein("jst,sd->jtd", pick_mlp, home_b)
    output = (middle + jnp.sum(gates_b[:, :, None] * taken_b, 0)).astype(BF16)
    got_kv[0] = after(got_kv[0], grad_wq, grad_woutput)
    grad_kv = functools.reduce(jnp.add, [part.astype(F32) for part in got_kv]).astype(BF16)
    grad_kv = relative(grad_kv.reshape(planes, count, 2 * kv_part)).reshape(seq, 2 * kv_part)
    grad_wquery = lax.psum_scatter(
        after(grad_wq, grad_kv), "dp", scatter_dimension=1, tiled=True
    ).astype(F32)
    query_mine, query_theirs = halves(whole_query, 1)
    kvw_mine, kvw_theirs = halves(w_kv_part, 0)

    def grad_seq(query_half, kv_half, done):
        rows = ein("lrf,ldf->lrd", after(grad_query, done), query_half).astype(BF16)
        rows = ein("slct,lscd->std", spread, rows.reshape(local_att, planes, cap, width))
        return rows.reshape(seq, width) + ein("tf,df->td", grad_kv, kv_half)

    given = swap(grad_seq(query_theirs, kvw_theirs, got_kv[1]).astype(BF16))
    grad_seq_a = (grad_seq(query_mine, kvw_mine, got_kv[-1]) + given.astype(F32)).astype(BF16)
    grad_wgateup = unpack_gateup(
        after(got_gate, grad_kv).reshape(ff_parts, local_mlp, depth, ff),
        got_up.reshape(ff_parts, local_mlp, depth, ff),
    )
    grad_wdown = unpack_down(got_dn.reshape(ff_parts, local_mlp, ff, depth))
    grad_kv_w = lax.psum_scatter(
        ein("td,tf->df", seq_a, grad_kv).astype(BF16), "dp", scatter_dimension=0, tiled=True
    )
    grad_kv_w = a2a(
        grad_kv_w.reshape(planes, w_kv.shape[0], part_heads, 2, HD), "expert"
    )
    grad_wkv = grad_kv_w.transpose(1, 3, 0, 2, 4).astype(F32).reshape(w_kv.shape)
    back_a = shift(list(grad_seq_a.reshape(planes, count, width)), 1)
    back_a[0] = after(back_a[0], grad_wgateup, grad_wdown)
    grad_rows_a = functools.reduce(jnp.add, [part.astype(F32) for part in back_a])
    grad_normed_a = grad_rows_a + ein("et,de->td", grad_logit_a, router_a)
    grad_router_a = ein("et,td->ed", grad_logit_a, rows_a_half)
    grad_in_norm, grad_gain_a = normalize_back(residual, norm_attn, scale_a, grad_normed_a)
    grad_tokens = grad_middle + grad_in_norm

    small = jnp.concatenate(
        [grad_router_a, grad_router_b, grad_gain_a[None], grad_gain_b[None]], 0
    )
    small = total_over(total_over(small, "dp"), "expert")
    routers = both_halves(small[: n_att + n_mlp], core)
    return (
        output,
        grad_tokens,
        small[n_att + n_mlp],
        small[n_att + n_mlp + 1],
        grad_wkv,
        routers[:n_att].T,
        routers[n_att:].T,
        grad_wquery,
        grad_woutput,
        grad_wgateup,
        grad_wdown,
    )


def solution(mesh):
    in_specs = (
        P(("dp", "expert"), "tensor"),
        P("tensor"),
        P("tensor"),
        P(("dp", "expert"), None, "tensor"),
        P(),
        P(),
        P("expert", "dp", "tensor"),
        P("expert", "tensor", "dp"),
        P("expert", "dp", None, "tensor"),
        P("expert", "tensor", "dp"),
        P(("dp", "expert")),
        P(("dp", "expert"), None),
        P(("dp", "expert"), None),
        P(("dp", "expert"), "tensor"),
    )
    out_specs = (
        P(("dp", "expert"), "tensor"),
        P(("dp", "expert"), "tensor"),
        P("tensor"),
        P("tensor"),
        P(("dp", "expert"), None, "tensor"),
        P(),
        P(),
        P("expert", "dp", "tensor"),
        P("expert", "tensor", "dp"),
        P("expert", "dp", None, "tensor"),
        P("expert", "tensor", "dp"),
    )
    return jax.shard_map(shards, mesh=mesh, in_specs=in_specs, out_specs=out_specs, check_vma=False)
```

```python
import functools
import math

import jax
import jax.numpy as jnp
from jax import lax
from jax.experimental import pallas as pl
from jax.experimental.pallas import tpu as pltpu
from jax.sharding import PartitionSpec as P

HD = 128
EPSILON = 1e-06
MASKED = -1000000000.0
F32 = jnp.float32
BF16 = jnp.bfloat16
LIMIT = 60 << 20
WEIGHT = 0.01
NT = (((1,), (1,)), ((), ()))
TN = (((0,), (0,)), ((), ()))


def dot(lhs, rhs):
    return jnp.dot(lhs, rhs, preferred_element_type=F32)


def ein(spec, lhs, rhs):
    return jnp.einsum(spec, lhs, rhs, preferred_element_type=F32)


def gdot(lhs, rhs, dims):
    return lax.dot_general(lhs, rhs, dims, preferred_element_type=F32)


def swap(values):
    return lax.ppermute(values, "tensor", [(0, 1), (1, 0)])


def a2a(values, axis):
    return lax.all_to_all(values, axis, split_axis=0, concat_axis=0, tiled=True)


def total_over(values, axis):
    count = lax.axis_size(axis)
    step = 1
    while step < count:
        values = values + lax.ppermute(values, axis, [(i, i ^ step) for i in range(count)])
        step *= 2
    return values


def core_sum(values):
    return values + swap(values)


def after(value, *done):
    return lax.optimization_barrier((value,) + done)[0]


def near_planes(values):
    count = lax.axis_size("expert")
    return [values] + [
        lax.ppermute(values, "expert", [(i, (i - j) % count) for i in range(count)])
        for j in range(1, count)
    ]


def relay(values, axis, *done):
    count = lax.axis_size(axis)
    up, down = [values], [values]
    for step in range(count - 1):
        if done and step == count - 2:
            up[-1] = after(up[-1], *done)
        up.append(lax.ppermute(up[-1], axis, [(i, i + 1) for i in range(count - 1)]))
        down.append(lax.ppermute(down[-1], axis, [(i + 1, i) for i in range(count - 1)]))
    return [values] + [down[j] + up[count - j] for j in range(1, count)]


def shift(blocks, sign):
    count = lax.axis_size("expert")
    return [blocks[0]] + [
        lax.ppermute(blocks[j], "expert", [(i, (i + sign * j) % count) for i in range(count)])
        for j in range(1, count)
    ]


def cross(blocks):
    count = lax.axis_size("dp")
    return [blocks[0]] + [
        lax.ppermute(blocks[k], "dp", [(i, i ^ k) for i in range(count)]) for k in range(1, count)
    ]


def both_halves(values, core):
    other = swap(values)
    first = jnp.where(core == 0, values, other)
    second = jnp.where(core == 0, other, values)
    return jnp.concatenate([first, second], -1)


def one_hot_slots(routes, experts, capacity):
    token_count = routes.shape[2]
    member = (routes[:, None, 0] == experts[None, :, None]) | (
        routes[:, None, 1] == experts[None, :, None]
    )
    tokens = jnp.arange(token_count, dtype=jnp.int32)
    upper = (tokens[:, None] < tokens[None, :]).astype(BF16)
    rank = dot(member.astype(BF16), upper).astype(jnp.int32)
    slots = jnp.arange(capacity, dtype=jnp.int32)
    return member[:, :, None, :] & (rank[:, :, None, :] == slots[None, None, :, None])


def params(*kinds):
    return pltpu.CompilerParams(dimension_semantics=kinds, vmem_limit_bytes=LIMIT)


def cost(flops, moved):
    return pl.CostEstimate(
        flops=int(flops * WEIGHT), bytes_accessed=int(moved * WEIGHT), transcendentals=0
    )


def pack_kernel(ff, parts, src, *outs):
    for half in range(2):
        for part in range(parts):
            outs[half][part, 0] = src[0, :, half, part * ff : (part + 1) * ff].astype(BF16)


def pack_gateup(weights, parts):
    local, depth, _, ff_core = weights.shape
    ff = ff_core // parts
    if ff % 128:
        moved = weights.reshape(local, depth, 2, parts, ff).transpose(2, 3, 0, 1, 4).astype(BF16)
        return moved[0], moved[1]
    rows = min(depth, 128)
    return pl.pallas_call(
        functools.partial(pack_kernel, ff, parts),
        grid=(local, depth // rows),
        in_specs=[pl.BlockSpec((1, rows, 2, ff_core), lambda l, r: (l, r, 0, 0))],
        out_specs=[pl.BlockSpec((parts, 1, rows, ff), lambda l, r: (0, l, r, 0))] * 2,
        out_shape=[jax.ShapeDtypeStruct((parts, local, depth, ff), BF16)] * 2,
        compiler_params=params("parallel", "parallel"),
        cost_estimate=cost(0, weights.size * 6),
        name="pack_gateup",
    )(weights)


def unpack_kernel(ff, parts, gate, up, out):
    for half, src in enumerate((gate, up)):
        for part in range(parts):
            out[0, :, half, part * ff : (part + 1) * ff] = src[part, 0].astype(F32)


def unpack_gateup(gate, up):
    parts, local, depth, ff = gate.shape
    if ff % 128:
        moved = jnp.stack([gate, up], 0).transpose(2, 3, 0, 1, 4)
        return moved.astype(F32).reshape(local, depth, 2, parts * ff)
    rows = min(depth, 128)
    return pl.pallas_call(
        functools.partial(unpack_kernel, ff, parts),
        grid=(local, depth // rows),
        in_specs=[pl.BlockSpec((parts, 1, rows, ff), lambda l, r: (0, l, r, 0))] * 2,
        out_specs=pl.BlockSpec((1, rows, 2, parts * ff), lambda l, r: (l, r, 0, 0)),
        out_shape=jax.ShapeDtypeStruct((local, depth, 2, parts * ff), F32),
        compiler_params=params("parallel", "parallel"),
        cost_estimate=cost(0, gate.size * 12),
        name="unpack_gateup",
    )(gate, up)


def cast_kernel(src, out):
    out[...] = src[...].reshape(out.shape).astype(out.dtype)


def pack_down(weights, parts):
    local, ff_core, depth = weights.shape
    ff = ff_core // parts
    return pl.pallas_call(
        cast_kernel,
        grid=(parts, local),
        in_specs=[pl.BlockSpec((1, ff, depth), lambda p, l: (l, p, 0))],
        out_specs=pl.BlockSpec((1, 1, ff, depth), lambda p, l: (p, l, 0, 0)),
        out_shape=jax.ShapeDtypeStruct((parts, local, ff, depth), BF16),
        compiler_params=params("parallel", "parallel"),
        cost_estimate=cost(0, weights.size * 6),
        name="pack_down",
    )(weights)


def unpack_down(grads):
    parts, local, ff, depth = grads.shape
    return pl.pallas_call(
        cast_kernel,
        grid=(parts, local),
        in_specs=[pl.BlockSpec((1, 1, ff, depth), lambda p, l: (p, l, 0, 0))],
        out_specs=pl.BlockSpec((1, ff, depth), lambda p, l: (l, p, 0)),
        out_shape=jax.ShapeDtypeStruct((local, parts * ff, depth), F32),
        compiler_params=params("parallel", "parallel"),
        cost_estimate=cost(0, grads.size * 6),
        name="unpack_down",
    )(grads)


def turn(values, cosine, sine):
    return values * cosine + pltpu.roll(values, HD // 2, 1) * sine


def att_fwd_kernel(
    place, q_in, kv, cos, sin, row_pos, row_seg, key_seg, *rest
):
    o_out, q_out = rest[-2:]
    query = turn(q_in[...], cos[...], sin[...]).astype(BF16)
    q_out[...] = query
    scores = gdot(query, kv[0, :, :HD], NT) * (1.0 / math.sqrt(HD))
    key_pos = lax.broadcasted_iota(jnp.int32, scores.shape, 1)
    allowed = (row_seg[...] == key_seg[...]) & (row_pos[...] >= key_pos)
    scores = jnp.where(allowed, scores, MASKED)
    peak = jnp.max(scores, 1, keepdims=True)
    weight = jnp.exp(scores - peak)
    mass = jnp.sum(weight, 1, keepdims=True)
    soft = (weight * (1.0 / mass)).astype(BF16)
    o_out[...] = dot(soft, kv[0, :, HD:]).astype(BF16)


def att_forward(place, q_raw, kv, cos, sin, row_pos, row_seg, key_seg, group, before):
    rows, feats = q_raw.shape
    seq, wide = kv.shape[1:]
    group_heads = wide // (2 * HD)
    block = min(256, rows)
    head = lambda h, i, place: (i, place[group] * group_heads + h)
    row = lambda h, i, place: (i, 0)
    in_specs = [
        pl.BlockSpec((block, HD), head),
        pl.BlockSpec((1, seq, 2 * HD), lambda h, i, place: (0, 0, h)),
        pl.BlockSpec((block, HD), row),
        pl.BlockSpec((block, HD), row),
        pl.BlockSpec((block, 1), row),
        pl.BlockSpec((block, 1), row),
        pl.BlockSpec((1, seq), lambda h, i, place: (0, 0)),
    ]
    operands = [place, q_raw, kv, cos, sin, row_pos, row_seg, key_seg]
    aliases = {}
    if before is not None:
        in_specs += [pl.BlockSpec(memory_space=pl.ANY)] * 2
        operands += list(before)
        aliases = {8: 0, 9: 1}
    return pl.pallas_call(
        att_fwd_kernel,
        grid_spec=pltpu.PrefetchScalarGridSpec(
            num_scalar_prefetch=1,
            grid=(group_heads, rows // block),
            in_specs=in_specs,
            out_specs=[pl.BlockSpec((block, HD), head)] * 2,
        ),
        out_shape=[jax.ShapeDtypeStruct((rows, feats), BF16)] * 2,
        input_output_aliases=aliases,
        compiler_params=params("arbitrary", "arbitrary"),
        cost_estimate=cost(40 * rows * seq * HD * group_heads, rows * feats * 4),
        name="attention_fwd",
    )(*operands)


def att_bwd_kernel(
    place, q_in, do_in, kv, cos, sin, key_cos, key_sin, row_pos, row_seg, key_seg, *rest
):
    dq_out, dkv_out, dk_sum, dv_sum = rest[-4:]
    step = pl.program_id(1)
    scale = 1.0 / math.sqrt(HD)
    query, grad_out = q_in[...], do_in[...]
    keys, values = kv[0, :, :HD], kv[0, :, HD:]
    scores = gdot(keys, query, NT) * scale
    key_pos = lax.broadcasted_iota(jnp.int32, scores.shape, 0)
    allowed = (row_seg[...] == key_seg[...]) & (row_pos[...] >= key_pos)
    scores = jnp.where(allowed, scores, MASKED)
    peak = jnp.max(scores, 0, keepdims=True)
    weight = jnp.exp(scores - peak)
    soft = weight * (1.0 / jnp.sum(weight, 0, keepdims=True))
    grad_soft = gdot(values, grad_out, NT)
    inner = jnp.sum(soft * grad_soft, 0, keepdims=True)
    grad_scores = (soft * (grad_soft - inner)).astype(BF16)
    grad_query = gdot(grad_scores, keys, TN) * scale
    dq_out[...] = turn(grad_query, cos[...], -sin[...]).astype(BF16)

    @pl.when(step == 0)
    def _():
        dk_sum[...] = jnp.zeros_like(dk_sum)
        dv_sum[...] = jnp.zeros_like(dv_sum)

    dk_sum[...] += dot(grad_scores, query)
    dv_sum[...] += dot(soft.astype(BF16), grad_out)

    @pl.when(step == pl.num_programs(1) - 1)
    def _():
        grad_keys = turn(dk_sum[...] * scale, key_cos[...], -key_sin[...])
        dkv_out[0, :, :HD] = grad_keys.astype(BF16)
        dkv_out[0, :, HD:] = dv_sum[...].astype(BF16)


def att_backward(
    place, query, grad_mixed, kv, cos, sin, key_cos, key_sin, row_pos, row_seg, key_seg,
    group, before,
):
    rows, feats = query.shape
    _, seq, wide = kv.shape
    group_heads = wide // (2 * HD)
    block = min(256, rows)
    head = lambda h, i, place: (i, place[group] * group_heads + h)
    row = lambda h, i, place: (i, 0)
    lane = lambda h, i, place: (0, i)
    whole = lambda h, i, place: (0, 0)
    pair = lambda h, i, place: (0, 0, h)
    in_specs = [
        pl.BlockSpec((block, HD), head),
        pl.BlockSpec((block, HD), head),
        pl.BlockSpec((1, seq, 2 * HD), pair),
        pl.BlockSpec((block, HD), row),
        pl.BlockSpec((block, HD), row),
        pl.BlockSpec((seq, HD), whole),
        pl.BlockSpec((seq, HD), whole),
        pl.BlockSpec((1, block), lane),
        pl.BlockSpec((1, block), lane),
        pl.BlockSpec((seq, 1), whole),
    ]
    operands = [
        place, query, grad_mixed, kv, cos, sin, key_cos, key_sin, row_pos, row_seg, key_seg
    ]
    aliases = {}
    if before is not None:
        in_specs.append(pl.BlockSpec(memory_space=pl.ANY))
        operands.append(before)
        aliases = {11: 0}
    return pl.pallas_call(
        att_bwd_kernel,
        grid_spec=pltpu.PrefetchScalarGridSpec(
            num_scalar_prefetch=1,
            grid=(group_heads, rows // block),
            in_specs=in_specs,
            out_specs=[
                pl.BlockSpec((block, HD), head),
                pl.BlockSpec((1, seq, 2 * HD), pair),
            ],
            scratch_shapes=[pltpu.VMEM((seq, HD), F32)] * 2,
        ),
        out_shape=[
            jax.ShapeDtypeStruct((rows, feats), BF16),
            jax.ShapeDtypeStruct((1, seq, wide), BF16),
        ],
        input_output_aliases=aliases,
        compiler_params=params("arbitrary", "arbitrary"),
        cost_estimate=cost(60 * rows * seq * HD * group_heads, rows * feats * 4),
        name="attention_bwd",
    )(*operands)


def raw_kernel(core, g_own, g_other, w_dn, out):
    columns = w_dn.shape[0]
    half, depth = columns // 2, w_dn.shape[2]
    total = jnp.zeros(out.shape, F32)
    for i in range(half):
        part = slice(i * depth, (i + 1) * depth)
        total += gdot(g_own[:, part], w_dn[core[0] * half + i], NT)
        total += gdot(g_other[:, part], w_dn[(1 - core[0]) * half + i], NT)
    out[...] = total


def hidden_raw(core, g_own, g_other, w_dn):
    rows, width = g_own.shape
    columns, ff, depth = w_dn.shape
    block = 256
    return pl.pallas_call(
        raw_kernel,
        grid_spec=pltpu.PrefetchScalarGridSpec(
            num_scalar_prefetch=1,
            grid=(rows // block,),
            in_specs=[
                pl.BlockSpec((block, width), lambda i, c: (i, 0)),
                pl.BlockSpec((block, width), lambda i, c: (i, 0)),
                pl.BlockSpec(
                    (columns, ff, depth), lambda i, c: (0, 0, 0), pipeline_mode=pl.Buffered(1)
                ),
            ],
            out_specs=pl.BlockSpec((block, ff), lambda i, c: (i, 0)),
        ),
        out_shape=jax.ShapeDtypeStruct((rows, ff), F32),
        compiler_params=params("arbitrary"),
        cost_estimate=cost(2 * w_dn.size * rows, w_dn.size * 2 + rows * ff * 4),
        name="hidden_raw",
    )(core, g_own, g_other, w_dn)


def ff_kernel(
    place, x_own, x_other, w_gate, w_up, raw, router, other, hid, hid_gated, du, dw, dgate
):
    core, expert = place[0], place[1]
    width = x_own.shape[1]
    mine = pl.ds(pl.multiple_of(core * width, width), width)
    theirs = pl.ds(pl.multiple_of((1 - core) * width, width), width)

    def product(weights):
        return dot(x_own[...], weights[mine, :]) + dot(x_other[...], weights[theirs, :])

    logits = product(router)
    lanes = lax.broadcasted_iota(jnp.int32, logits.shape, 1)
    own_logit = jnp.sum(jnp.where(lanes == expert, logits, 0.0), 1, keepdims=True)
    other_logit = jnp.sum(jnp.where(lanes == other[...], logits, 0.0), 1, keepdims=True)
    gate = jax.nn.sigmoid(own_logit - other_logit)
    gate_part, up_part = product(w_gate), product(w_up)
    sig = 1.0 / (1.0 + jnp.exp(-gate_part))
    silu = gate_part * sig
    hidden = silu * up_part
    hid[...] = hidden.astype(BF16)
    hid_gated[...] = (hidden * gate).astype(BF16)
    dgate[...] = jnp.sum(hidden * raw[...], 1, keepdims=True)
    grad_hidden = raw[...] * gate
    du[...] = (grad_hidden * up_part * (sig * (1.0 + gate_part * (1.0 - sig)))).astype(BF16)
    dw[...] = (grad_hidden * silu).astype(BF16)


def feed_forward(place, x_own, x_other, w_gate, w_up, raw, router, other):
    rows, width = x_own.shape
    ff = raw.shape[1]
    block = 256
    row = lambda i, c: (i, 0)
    whole = lambda i, c: (0, 0)
    fixed = lambda array: pl.BlockSpec(array.shape, whole, pipeline_mode=pl.Buffered(1))
    return pl.pallas_call(
        ff_kernel,
        grid_spec=pltpu.PrefetchScalarGridSpec(
            num_scalar_prefetch=1,
            grid=(rows // block,),
            in_specs=[
                pl.BlockSpec((block, width), row),
                pl.BlockSpec((block, width), row),
                fixed(w_gate),
                fixed(w_up),
                pl.BlockSpec((block, ff), row),
                fixed(router),
                pl.BlockSpec((block, 1), row),
            ],
            out_specs=[pl.BlockSpec((block, ff), row)] * 4 + [pl.BlockSpec((block, 1), row)],
        ),
        out_shape=[jax.ShapeDtypeStruct((rows, ff), BF16)] * 4
        + [jax.ShapeDtypeStruct((rows, 1), F32)],
        compiler_params=params("arbitrary"),
        cost_estimate=cost(5 * w_gate.size * rows, w_gate.size * 4 + rows * ff * 12),
        name="feed_forward",
    )(place, x_own, x_other, w_gate, w_up, raw, router, other)


def rows_kernel(count, which, *refs):
    out = refs[-1]
    total = None
    for lhs, weights in zip(refs[:count], refs[count : 2 * count]):
        if len(weights.shape) == 2:
            part = gdot(lhs[...], weights[...], NT)
        else:
            part = jnp.concatenate(
                [dot(lhs[...], weights[i]) for i in range(weights.shape[0])], 1
            )
        total = part if total is None else total + part
    if len(refs) > 2 * count + 1:
        total = total + refs[2 * count][...].astype(F32)
    out[...] = total.astype(BF16)


def rows_half(which, lhs, weights, width, add=None):
    rows = lhs[0].shape[0]
    block = 256
    row = lambda i, c: (i, 0)
    in_specs = [pl.BlockSpec((block, array.shape[1]), row) for array in lhs]
    for array in weights:
        if array.ndim == 2:
            shape, index = (width, array.shape[1]), lambda i, c: (c[0], 0)
        else:
            shape = (array.shape[0] // 2,) + array.shape[1:]
            index = lambda i, c: (c[0], 0, 0)
        in_specs.append(pl.BlockSpec(shape, index, pipeline_mode=pl.Buffered(1)))
    operands = [which, *lhs, *weights]
    if add is not None:
        in_specs.append(pl.BlockSpec((block, width), row))
        operands.append(add)
    return pl.pallas_call(
        functools.partial(rows_kernel, len(lhs)),
        grid_spec=pltpu.PrefetchScalarGridSpec(
            num_scalar_prefetch=1,
            grid=(rows // block,),
            in_specs=in_specs,
            out_specs=pl.BlockSpec((block, width), row),
        ),
        out_shape=jax.ShapeDtypeStruct((rows, width), BF16),
        compiler_params=params("arbitrary"),
        cost_estimate=cost(sum(array.size for array in weights) * rows, rows * width * 4),
        name="rows_half",
    )(*operands)


def gu_outer_kernel(core, x_own, x_other, duw, out):
    half = pl.num_programs(0) // 2
    mine = (pl.program_id(0) // half) == core[0]

    @pl.when(mine)
    def _():
        out[0] = gdot(x_own[...], duw[...], TN).astype(BF16)

    @pl.when(jnp.logical_not(mine))
    def _():
        out[0] = gdot(x_other[...], duw[...], TN).astype(BF16)


def gu_outer(core, x_own, x_other, duw, columns):
    rows, width = x_own.shape
    half = columns // 2
    depth = width // half
    part = lambda s, c: (0, lax.rem(s, half))
    return pl.pallas_call(
        gu_outer_kernel,
        grid_spec=pltpu.PrefetchScalarGridSpec(
            num_scalar_prefetch=1,
            grid=(columns,),
            in_specs=[
                pl.BlockSpec((rows, depth), part),
                pl.BlockSpec((rows, depth), part),
                pl.BlockSpec(duw.shape, lambda s, c: (0, 0), pipeline_mode=pl.Buffered(1)),
            ],
            out_specs=pl.BlockSpec((1, depth, duw.shape[1]), lambda s, c: (s, 0, 0)),
        ),
        out_shape=jax.ShapeDtypeStruct((columns, depth, duw.shape[1]), BF16),
        compiler_params=params("arbitrary"),
        cost_estimate=cost(2 * rows * 2 * width * duw.shape[1], rows * width * 8),
        name="grad_gateup",
    )(core, x_own, x_other, duw)


def dn_outer_kernel(core, hid, g_own, g_other, out):
    half = pl.num_programs(0) // 2
    mine = (pl.program_id(0) // half) == core[0]

    @pl.when(mine)
    def _():
        out[0] = gdot(hid[...], g_own[...], TN).astype(BF16)

    @pl.when(jnp.logical_not(mine))
    def _():
        out[0] = gdot(hid[...], g_other[...], TN).astype(BF16)


def dn_outer(core, hid, g_own, g_other, columns):
    rows, width = g_own.shape
    half = columns // 2
    depth = width // half
    ff = hid.shape[1]
    part = lambda s, c: (0, lax.rem(s, half))
    return pl.pallas_call(
        dn_outer_kernel,
        grid_spec=pltpu.PrefetchScalarGridSpec(
            num_scalar_prefetch=1,
            grid=(columns,),
            in_specs=[
                pl.BlockSpec(hid.shape, lambda s, c: (0, 0), pipeline_mode=pl.Buffered(1)),
                pl.BlockSpec((rows, depth), part),
                pl.BlockSpec((rows, depth), part),
            ],
            out_specs=pl.BlockSpec((1, ff, depth), lambda s, c: (s, 0, 0)),
        ),
        out_shape=jax.ShapeDtypeStruct((columns, ff, depth), BF16),
        compiler_params=params("arbitrary"),
        cost_estimate=cost(2 * rows * 2 * width * ff, rows * width * 8),
        name="grad_down",
    )(core, hid, g_own, g_other)


def shards(
    tokens,
    norm_attn,
    norm_mlp,
    w_kv,
    router_attn,
    router_mlp,
    w_query,
    w_output,
    w_gateup,
    w_down,
    segments,
    att_routes,
    mlp_routes,
    cotangent,
):
    count, width = tokens.shape
    full_width = 2 * width
    planes = lax.axis_size("expert")
    columns = lax.axis_size("dp")
    plane = lax.axis_index("expert")
    column = lax.axis_index("dp")
    core = lax.axis_index("tensor")
    n_att = router_attn.shape[1]
    n_mlp = router_mlp.shape[1]
    local_att = w_query.shape[0]
    local_mlp = w_gateup.shape[0]
    ff_parts = columns // local_mlp
    depth = w_gateup.shape[1]
    ff = w_gateup.shape[3] // ff_parts
    cap = 3 * count // 8
    seq = planes * count
    feats = w_query.shape[2]
    kv_part = feats // planes
    part_heads = kv_part // HD
    own_local = column % local_mlp
    mlp_expert = plane * local_mlp + own_local
    steps = jnp.arange(planes, dtype=jnp.int32)
    source_planes = (plane + steps) % planes
    target_planes = (plane - steps + planes) % planes
    near_local = own_local ^ jnp.arange(local_mlp, dtype=jnp.int32)
    core_at = core.astype(jnp.int32)[None]
    other_at = 1 - core_at

    def absolute(blocks):
        twice = jnp.concatenate([blocks, blocks], 0)
        return lax.dynamic_slice_in_dim(twice, (planes - plane) % planes, planes, 0)

    def relative(blocks):
        twice = jnp.concatenate([blocks, blocks], 0)
        return lax.dynamic_slice_in_dim(twice, plane, planes, 0)

    def relative_down(blocks):
        twice = jnp.concatenate([blocks[::-1], blocks[::-1]], 0)
        return lax.dynamic_slice_in_dim(twice, planes - 1 - plane, planes, 0)

    kv_send = w_kv.astype(BF16).reshape(w_kv.shape[0], 2, planes, part_heads, HD)
    near_tokens = near_planes(tokens)
    kv_send = absolute(jnp.stack(shift(list(relative_down(kv_send.transpose(2, 0, 3, 1, 4))), -1), 0))
    w_kv_part = lax.all_gather(kv_send, "dp", axis=0, tiled=True).reshape(
        full_width, 2 * kv_part
    )
    whole_query = lax.all_gather(
        after(w_query.astype(BF16), kv_send), "dp", axis=1, tiled=True
    )
    whole_output = lax.all_gather(w_output.astype(BF16), "dp", axis=2, tiled=True)
    down_send = pack_down(w_down, ff_parts).reshape(columns, ff, depth)
    gate_send, up_send = pack_gateup(w_gateup, ff_parts)
    w_dn = a2a(down_send, "dp")
    w_gate = a2a(gate_send.reshape(columns, depth, ff), "dp").reshape(full_width, ff)
    w_up = a2a(up_send.reshape(columns, depth, ff), "dp").reshape(full_width, ff)

    ints = jnp.concatenate(
        [
            segments[None],
            att_routes.T,
            mlp_routes.T,
            jnp.zeros((3, count), jnp.int32),
        ],
        0,
    )
    near_ints = jnp.stack(near_planes(ints), 0)[None]
    step = 1
    while step < columns:
        pairs = [(i, i ^ step) for i in range(columns)]
        near_ints = jnp.concatenate([near_ints, lax.ppermute(near_ints, "dp", pairs)], 0)
        step *= 2

    residual = tokens.astype(F32)
    near_tokens[-1] = after(near_tokens[-1], down_send, gate_send, up_send)
    seq_res = jnp.concatenate(near_tokens, 0).astype(F32)

    def rms_scale(values):
        return lax.rsqrt(
            core_sum(jnp.sum(values * values, 1, keepdims=True)) / full_width + EPSILON
        )

    seq_scale = rms_scale(seq_res)
    seq_a_half = (seq_res * seq_scale * norm_attn).astype(BF16)
    scale_a = seq_scale[:count]
    rows_a_half = seq_a_half[:count]
    seq_a = both_halves(seq_a_half, core)

    def angles_of(positions):
        frequency = jnp.exp(
            jnp.arange(HD // 2, dtype=F32) * (-2.0 * math.log(10000.0) / HD)
        )
        angle = positions.astype(F32)[:, None] * frequency[None, :]
        cosine, sine = jnp.cos(angle), jnp.sin(angle)
        return jnp.concatenate([cosine, cosine], 1), jnp.concatenate([-sine, sine], 1)

    seq_pos = jnp.arange(seq, dtype=jnp.int32)
    cos_seq, sin_seq = angles_of(seq_pos)
    near_pos = source_planes[:, None] * count + jnp.arange(count, dtype=jnp.int32)[None]
    cos_near, sin_near = angles_of(near_pos.reshape(-1))
    kv_raw = dot(seq_a, w_kv_part).reshape(seq, part_heads, 2, HD)
    keys = kv_raw[:, :, 0]
    turned = jnp.concatenate([keys[..., HD // 2 :], keys[..., : HD // 2]], -1)
    keys = keys * cos_near[:, None] + turned * sin_near[:, None]
    kv_mine = jnp.stack([keys.astype(BF16), kv_raw[:, :, 1].astype(BF16)], 2)
    kv_mine = absolute(kv_mine.reshape(planes, count, 2 * kv_part)).reshape(seq, 2 * kv_part)
    kv_near = relay(kv_mine, "expert", w_dn)

    seq_ints = near_ints[0]
    own_att = jnp.arange(local_att, dtype=jnp.int32) + plane * local_att
    att_ids = (target_planes[:, None] * local_att + jnp.arange(local_att)[None]).reshape(-1)
    mlp_ids = (target_planes[:, None] * local_mlp + near_local[None]).reshape(-1)
    att_slots = one_hot_slots(seq_ints[:, 1:3], own_att, cap)
    home_att = one_hot_slots(ints[None, 1:3], att_ids, cap)[0]
    home_mlp = one_hot_slots(ints[None, 3:5], mlp_ids, cap)[0]
    every_mlp = near_ints[:, :, 3:5].reshape(-1, 2, count)
    mlp_slots = one_hot_slots(every_mlp, mlp_expert[None], cap)[:, 0]
    other_expert = jnp.sum(every_mlp, 1) - mlp_expert
    row_other = jnp.sum(jnp.where(mlp_slots, other_expert[:, None, :], 0), -1).reshape(-1, 1)

    def by_choice(home, routes, ids):
        named = routes[:, None, :] == ids[None, :, None]
        picks = home[None] & named[:, :, None, :]
        return picks.astype(BF16).reshape(2, -1, count)

    pick_att = by_choice(home_att, ints[1:3], att_ids)
    pick_mlp = by_choice(home_mlp, ints[3:5], mlp_ids)
    flat_mlp = home_mlp.astype(BF16).reshape(n_mlp * cap, count)
    spread = att_slots.astype(BF16)
    row_pos = jnp.sum(
        jnp.where(att_slots, near_pos[:, None, None, :], 0), -1
    ).transpose(1, 0, 2).reshape(-1)
    row_seg = jnp.sum(
        jnp.where(att_slots, seq_ints[:, 0][:, None, None, :], 0), -1
    ).transpose(1, 0, 2).reshape(-1)
    seq_seg = absolute(seq_ints[:, 0]).reshape(seq)
    att_rows = planes * local_att * cap

    def to_plane(rows_half):
        return shift(list(rows_half.reshape(planes, local_mlp, cap, width)), -1)

    def to_expert(held, early=(), late=()):
        held[-1] = after(held[-1], *early)
        held = jnp.stack(held, 1)
        sent = [held[k % local_mlp].reshape(planes * cap, width) for k in range(columns)]
        got = cross(sent)
        got[-1] = after(got[-1], *late)
        own = jnp.concatenate(got, 0)
        return own, swap(own)

    g_held = to_plane(dot(flat_mlp, after(cotangent, kv_near[1], kv_near[-1])).astype(BF16))

    def gates_of(half_rows, router, routes):
        part = lax.dynamic_slice_in_dim(router, core * width, width, 0).astype(BF16)
        logits = core_sum(ein("de,td->et", part, half_rows))
        experts = router.shape[1]
        named = (
            routes[:, None, :] == jnp.arange(experts, dtype=jnp.int32)[None, :, None]
        ).astype(F32)
        chosen = jnp.sum(named * logits[None], 1)
        return jax.nn.softmax(chosen, axis=0), named, part

    gates_a, named_a, router_a = gates_of(rows_a_half, router_attn, ints[1:3])
    held_a = ein("slct,std->lscd", spread, seq_a.reshape(planes, count, full_width)).astype(BF16)
    held_a = held_a.reshape(local_att, planes * cap, full_width)
    cos_rows, sin_rows = angles_of(row_pos)
    query_raw = ein("lrd,ldf->lrf", held_a, whole_query).reshape(att_rows, feats)
    before = None
    order = [0, planes // 2] + [j for j in range(1, planes) if j != planes // 2]
    for j in order:
        if j == order[-2]:
            kv_near[j] = after(kv_near[j], *g_held[1:])
        before = att_forward(
            source_planes, query_raw, kv_near[j][None], cos_rows, sin_rows,
            row_pos[:, None], row_seg[:, None], seq_seg[None], j, before,
        )
    mixed_rows, query_rows = before
    mixed_rows = after(mixed_rows, w_gate)
    mixed_owner = mixed_rows.reshape(local_att, planes * cap, feats)

    def halves(values, axis):
        mine = lax.dynamic_slice_in_dim(values, core * width, width, axis)
        theirs = lax.dynamic_slice_in_dim(values, (1 - core) * width, width, axis)
        return mine, theirs

    out_mine, out_theirs = halves(whole_output, 2)
    given = swap(ein("lrf,lfd->lrd", mixed_owner, out_theirs).astype(BF16))
    branch_a = ein("lrf,lfd->lrd", mixed_owner, out_mine) + given.astype(F32)
    branch_a = branch_a.astype(BF16).reshape(local_att, planes, cap, width)
    home_a = shift([branch_a[:, j].reshape(local_att * cap, width) for j in range(planes)], 1)
    g_own, g_other = to_expert(g_held, (), tuple(home_a[1:]))
    raw = hidden_raw(core_at, g_own, g_other, w_dn)
    home_a = jnp.concatenate(home_a, 0)
    taken_a = ein("jst,sd->jtd", pick_att, home_a)
    middle = residual + jnp.sum(gates_a[:, :, None] * taken_a, 0)

    scale_b = rms_scale(middle)
    rows_b_half = (middle * scale_b * norm_mlp).astype(BF16)
    gates_b, named_b, router_b = gates_of(rows_b_half, router_mlp, ints[3:5])
    x_own, x_other = to_expert(
        to_plane(dot(flat_mlp, rows_b_half).astype(BF16)), (raw,), (w_up,)
    )
    router_wide = jnp.pad(router_mlp.astype(BF16), ((0, 0), (0, HD - n_mlp)))
    place = jnp.stack([core, mlp_expert]).astype(jnp.int32)
    hidden, hidden_gated, grad_gate, grad_up, row_dgate = feed_forward(
        place, x_own, x_other, w_gate, w_up, raw, router_wide, row_other
    )

    def over_parts(rows, *done):
        tail = rows.shape[1:]
        got = cross(list(rows.reshape((columns, planes, cap) + tail)))
        if done:
            got = list(lax.optimization_barrier(tuple(got) + done)[:columns])
        there = got[1:]
        sums = []
        for near in range(local_mlp):
            parts = [got[k].astype(F32) for k in range(near, columns, local_mlp)]
            sums.append(functools.reduce(jnp.add, parts).astype(rows.dtype))
        return [jnp.concatenate([part[j] for part in sums], 0) for j in range(planes)], there

    def mlp_home(blocks, *done):
        back = shift(blocks, 1)
        there = back[1:]
        back[-1] = after(back[-1], *done)
        return jnp.concatenate(back, 0), there

    dgate_blocks, dgate_there = over_parts(core_sum(row_dgate[:, 0]))
    dgate_home, dgate_back = mlp_home(dgate_blocks)
    branch_theirs = rows_half(other_at, (hidden,), (w_dn,), width)
    given = swap(branch_theirs)
    grad_wgate = gu_outer(core_at, x_own, x_other, after(grad_gate, branch_theirs), columns)
    branch_b = rows_half(core_at, (after(hidden, grad_wgate, *dgate_there),), (w_dn,), width, given)
    grad_pair = (after(grad_gate, branch_b, *dgate_back), grad_up)
    given = swap(rows_half(other_at, grad_pair, (w_gate, w_up), width))
    db_rows = rows_half(core_at, grad_pair, (w_gate, w_up), width, given)
    grad_wup = gu_outer(core_at, x_own, x_other, after(grad_up, db_rows), columns)
    branch_blocks, _ = over_parts(branch_b, grad_wup)
    home_b, branch_back = mlp_home(branch_blocks)
    grad_wdn = dn_outer(core_at, after(hidden_gated, grad_wup), g_own, g_other, columns)
    db_blocks, db_there = over_parts(db_rows, grad_wdn, *branch_back)
    home_db, _ = mlp_home(db_blocks)
    got_gate = a2a(after(grad_wgate, *db_there), "dp")
    got_up = a2a(grad_wup, "dp")
    got_dn = a2a(grad_wdn, "dp")

    def gates_back(gates, grad_gates, named):
        chosen = gates * (grad_gates - jnp.sum(gates * grad_gates, 0, keepdims=True))
        return jnp.sum(chosen[:, None, :] * named, 0).astype(BF16)

    grad_gates_b = jnp.sum(pick_mlp.astype(F32) * dgate_home[None, :, None], 1)
    grad_logit_b = gates_back(gates_b, grad_gates_b, named_b)
    grad_normed_b = ein("st,sd->td", flat_mlp, home_db) + ein("et,de->td", grad_logit_b, router_b)
    grad_router_b = ein("et,td->ed", grad_logit_b, rows_b_half)

    def normalize_back(values, gain, row_scale, grad_normed):
        inner = core_sum(jnp.sum(grad_normed * gain * values, 1, keepdims=True))
        grad_values = (
            row_scale * gain * grad_normed
            - values * (row_scale * row_scale * row_scale) * inner / full_width
        )
        return grad_values, jnp.sum(grad_normed * values * row_scale, 0)

    grad_out = cotangent.astype(F32)
    grad_mid_norm, grad_gain_b = normalize_back(middle, norm_mlp, scale_b, grad_normed_b)
    grad_middle = grad_out + grad_mid_norm

    grad_gates_a = core_sum(jnp.sum(grad_middle[None] * taken_a, 2))
    grad_logit_a = gates_back(gates_a, grad_gates_a, named_a)
    grad_taken_a = (gates_a[:, :, None] * grad_middle[None]).astype(BF16)
    sent_a = ein("jst,jtd->sd", pick_att, grad_taken_a).astype(BF16)
    got_a = shift(list(sent_a.reshape(planes, local_att, cap, width)), -1)
    got_a[-1] = after(got_a[-1], got_gate)
    held_grad_a = both_halves(
        jnp.stack(got_a, 1).reshape(local_att, planes * cap, width), core
    )
    grad_mixed = ein("lrd,lfd->lrf", held_grad_a, whole_output).astype(BF16)
    grad_wo = ein("lrf,lrd->lfd", mixed_owner, held_grad_a).astype(BF16)
    grad_woutput = lax.psum_scatter(grad_wo, "dp", scatter_dimension=2, tiled=True).astype(F32)
    grad_query = None
    sent_kv = [None] * planes
    for j in [planes // 2] + [j for j in range(1, planes) if j != planes // 2] + [0]:
        if j == 1:
            grad_query = after(grad_query, grad_wo)
        grad_query, grad_kv_group = att_backward(
            source_planes, query_rows, grad_mixed.reshape(att_rows, feats), kv_near[j][None],
            cos_rows, sin_rows, cos_seq, sin_seq, row_pos[None], row_seg[None],
            seq_seg[:, None], j, grad_query,
        )
        sent_kv[j] = grad_kv_group[0]
    grad_query = grad_query.reshape(local_att, planes * cap, feats)
    got_kv = shift(sent_kv, 1)
    grad_wq = ein(
        "lrd,lrf->ldf", after(held_a, got_kv[planes // 2], got_up), grad_query
    ).astype(BF16)
    taken_b = ein("jst,sd->jtd", pick_mlp, home_b)
    output = (middle + jnp.sum(gates_b[:, :, None] * taken_b, 0)).astype(BF16)
    got_kv[0] = after(got_kv[0], grad_wq, grad_woutput)
    grad_kv = functools.reduce(jnp.add, [part.astype(F32) for part in got_kv]).astype(BF16)
    grad_kv = relative(grad_kv.reshape(planes, count, 2 * kv_part)).reshape(seq, 2 * kv_part)
    grad_wquery = lax.psum_scatter(
        grad_wq, "dp", scatter_dimension=1, tiled=True
    ).astype(F32)
    query_mine, query_theirs = halves(whole_query, 1)
    kvw_mine, kvw_theirs = halves(w_kv_part, 0)

    def grad_seq(query_half, kv_half, done):
        rows = ein("lrf,ldf->lrd", after(grad_query, done), query_half).astype(BF16)
        rows = ein("slct,lscd->std", spread, rows.reshape(local_att, planes, cap, width))
        return rows.reshape(seq, width) + ein("tf,df->td", grad_kv, kv_half)

    given = swap(grad_seq(query_theirs, kvw_theirs, got_kv[1]).astype(BF16))
    grad_seq_a = (grad_seq(query_mine, kvw_mine, got_kv[-1]) + given.astype(F32)).astype(BF16)
    grad_wgateup = unpack_gateup(
        after(got_gate, grad_kv).reshape(ff_parts, local_mlp, depth, ff),
        got_up.reshape(ff_parts, local_mlp, depth, ff),
    )
    grad_wdown = unpack_down(got_dn.reshape(ff_parts, local_mlp, ff, depth))
    grad_kv_w = a2a(ein("td,tf->df", seq_a, grad_kv).astype(BF16), "dp")
    grad_kv_w = jnp.sum(
        grad_kv_w.reshape(columns, full_width // columns, 2 * kv_part).astype(F32), 0
    ).astype(BF16)
    grad_kv_w = a2a(
        grad_kv_w.reshape(planes, w_kv.shape[0], part_heads, 2, HD), "expert"
    )
    grad_wkv = grad_kv_w.transpose(1, 3, 0, 2, 4).astype(F32).reshape(w_kv.shape)
    back_a = shift(list(grad_seq_a.reshape(planes, count, width)), 1)
    back_a[0] = after(back_a[0], grad_wgateup, grad_wdown)
    grad_rows_a = functools.reduce(jnp.add, [part.astype(F32) for part in back_a])
    grad_normed_a = grad_rows_a + ein("et,de->td", grad_logit_a, router_a)
    grad_router_a = ein("et,td->ed", grad_logit_a, rows_a_half)
    grad_in_norm, grad_gain_a = normalize_back(residual, norm_attn, scale_a, grad_normed_a)
    grad_tokens = grad_middle + grad_in_norm

    small = jnp.concatenate(
        [grad_router_a, grad_router_b, grad_gain_a[None], grad_gain_b[None]], 0
    )
    small = total_over(total_over(small, "dp"), "expert")
    routers = both_halves(small[: n_att + n_mlp], core)
    return (
        output,
        grad_tokens,
        small[n_att + n_mlp],
        small[n_att + n_mlp + 1],
        grad_wkv,
        routers[:n_att].T,
        routers[n_att:].T,
        grad_wquery,
        grad_woutput,
        grad_wgateup,
        grad_wdown,
    )


def solution(mesh):
    in_specs = (
        P(("dp", "expert"), "tensor"),
        P("tensor"),
        P("tensor"),
        P(("dp", "expert"), None, "tensor"),
        P(),
        P(),
        P("expert", "dp", "tensor"),
        P("expert", "tensor", "dp"),
        P("expert", "dp", None, "tensor"),
        P("expert", "tensor", "dp"),
        P(("dp", "expert")),
        P(("dp", "expert"), None),
        P(("dp", "expert"), None),
        P(("dp", "expert"), "tensor"),
    )
    out_specs = (
        P(("dp", "expert"), "tensor"),
        P(("dp", "expert"), "tensor"),
        P("tensor"),
        P("tensor"),
        P(("dp", "expert"), None, "tensor"),
        P(),
        P(),
        P("expert", "dp", "tensor"),
        P("expert", "tensor", "dp"),
        P("expert", "dp", None, "tensor"),
        P("expert", "tensor", "dp"),
    )
    return jax.shard_map(shards, mesh=mesh, in_specs=in_specs, out_specs=out_specs, check_vma=False)
```

```python
import functools
import math

import jax
import jax.numpy as jnp
from jax import lax
from jax.experimental import pallas as pl
from jax.experimental.pallas import tpu as pltpu
from jax.sharding import PartitionSpec as P

HD = 128
EPSILON = 1e-06
MASKED = -1000000000.0
F32 = jnp.float32
BF16 = jnp.bfloat16
LIMIT = 60 << 20
WEIGHT = 0.01
NT = (((1,), (1,)), ((), ()))
TN = (((0,), (0,)), ((), ()))


def dot(lhs, rhs):
    return jnp.dot(lhs, rhs, preferred_element_type=F32)


def ein(spec, lhs, rhs):
    return jnp.einsum(spec, lhs, rhs, preferred_element_type=F32)


def gdot(lhs, rhs, dims):
    return lax.dot_general(lhs, rhs, dims, preferred_element_type=F32)


def swap(values):
    return lax.ppermute(values, "tensor", [(0, 1), (1, 0)])


def a2a(values, axis):
    return lax.all_to_all(values, axis, split_axis=0, concat_axis=0, tiled=True)


def total_over(values, axis):
    count = lax.axis_size(axis)
    step = 1
    while step < count:
        values = values + lax.ppermute(values, axis, [(i, i ^ step) for i in range(count)])
        step *= 2
    return values


def core_sum(values):
    return values + swap(values)


def after(value, *done):
    return lax.optimization_barrier((value,) + done)[0]


def near_planes(values):
    count = lax.axis_size("expert")
    return [values] + [
        lax.ppermute(values, "expert", [(i, (i - j) % count) for i in range(count)])
        for j in range(1, count)
    ]


def relay(values, axis, *done):
    count = lax.axis_size(axis)
    up, down = [values], [values]
    for step in range(count - 1):
        if done and step == count - 2:
            up[-1] = after(up[-1], *done)
        up.append(lax.ppermute(up[-1], axis, [(i, i + 1) for i in range(count - 1)]))
        down.append(lax.ppermute(down[-1], axis, [(i + 1, i) for i in range(count - 1)]))
    return [values] + [down[j] + up[count - j] for j in range(1, count)]


def shift(blocks, sign):
    count = lax.axis_size("expert")
    return [blocks[0]] + [
        lax.ppermute(blocks[j], "expert", [(i, (i + sign * j) % count) for i in range(count)])
        for j in range(1, count)
    ]


def cross(blocks):
    count = lax.axis_size("dp")
    return [blocks[0]] + [
        lax.ppermute(blocks[k], "dp", [(i, i ^ k) for i in range(count)]) for k in range(1, count)
    ]


def both_halves(values, core):
    other = swap(values)
    first = jnp.where(core == 0, values, other)
    second = jnp.where(core == 0, other, values)
    return jnp.concatenate([first, second], -1)


def one_hot_slots(routes, experts, capacity):
    token_count = routes.shape[2]
    member = (routes[:, None, 0] == experts[None, :, None]) | (
        routes[:, None, 1] == experts[None, :, None]
    )
    tokens = jnp.arange(token_count, dtype=jnp.int32)
    upper = (tokens[:, None] < tokens[None, :]).astype(BF16)
    rank = dot(member.astype(BF16), upper).astype(jnp.int32)
    slots = jnp.arange(capacity, dtype=jnp.int32)
    return member[:, :, None, :] & (rank[:, :, None, :] == slots[None, None, :, None])


def params(*kinds):
    return pltpu.CompilerParams(dimension_semantics=kinds, vmem_limit_bytes=LIMIT)


def cost(flops, moved):
    return pl.CostEstimate(
        flops=int(flops * WEIGHT), bytes_accessed=int(moved * WEIGHT), transcendentals=0
    )


def pack_kernel(ff, parts, src, *outs):
    for half in range(2):
        for part in range(parts):
            outs[half][part, 0] = src[0, :, half, part * ff : (part + 1) * ff].astype(BF16)


def pack_gateup(weights, parts):
    local, depth, _, ff_core = weights.shape
    ff = ff_core // parts
    if ff % 128:
        moved = weights.reshape(local, depth, 2, parts, ff).transpose(2, 3, 0, 1, 4).astype(BF16)
        return moved[0], moved[1]
    rows = min(depth, 128)
    return pl.pallas_call(
        functools.partial(pack_kernel, ff, parts),
        grid=(local, depth // rows),
        in_specs=[pl.BlockSpec((1, rows, 2, ff_core), lambda l, r: (l, r, 0, 0))],
        out_specs=[pl.BlockSpec((parts, 1, rows, ff), lambda l, r: (0, l, r, 0))] * 2,
        out_shape=[jax.ShapeDtypeStruct((parts, local, depth, ff), BF16)] * 2,
        compiler_params=params("parallel", "parallel"),
        cost_estimate=cost(0, weights.size * 6),
        name="pack_gateup",
    )(weights)


def unpack_kernel(ff, parts, early, gate, up_early, up_late, out):
    first = pl.program_id(1) < early
    for part in range(parts):
        where = slice(part * ff, (part + 1) * ff)
        out[0, :, 0, where] = gate[part, 0].astype(F32)

        @pl.when(first)
        def _():
            out[0, :, 1, where] = up_early[part, 0].astype(F32)

        @pl.when(jnp.logical_not(first))
        def _():
            out[0, :, 1, where] = up_late[part, 0].astype(F32)


def unpack_gateup(sooner, later):
    parts, local, half, ff = later.shape
    depth = 2 * half
    if ff % 128:
        both = jnp.concatenate([sooner, later], 2).reshape(parts, local, 2, depth, ff)
        return both.transpose(1, 3, 2, 0, 4).astype(F32).reshape(local, depth, 2, parts * ff)
    rows = min(half, 128)
    early = half // rows
    block = (parts, 1, rows, ff)
    return pl.pallas_call(
        functools.partial(unpack_kernel, ff, parts, early),
        grid=(local, 2 * early),
        in_specs=[
            pl.BlockSpec(block, lambda l, r: (0, l, r, 0)),
            pl.BlockSpec(block, lambda l, r: (0, l, 2 * early + jnp.minimum(r, early - 1), 0)),
            pl.BlockSpec(block, lambda l, r: (0, l, jnp.maximum(r - early, 0), 0)),
        ],
        out_specs=pl.BlockSpec((1, rows, 2, parts * ff), lambda l, r: (l, r, 0, 0)),
        out_shape=jax.ShapeDtypeStruct((local, depth, 2, parts * ff), F32),
        compiler_params=params("parallel", "parallel"),
        cost_estimate=cost(0, later.size * 48),
        name="unpack_gateup",
    )(sooner, sooner, later)


def cast_kernel(src, out):
    out[...] = src[...].reshape(out.shape).astype(out.dtype)


def pack_down(weights, parts):
    local, ff_core, depth = weights.shape
    ff = ff_core // parts
    return pl.pallas_call(
        cast_kernel,
        grid=(parts, local),
        in_specs=[pl.BlockSpec((1, ff, depth), lambda p, l: (l, p, 0))],
        out_specs=pl.BlockSpec((1, 1, ff, depth), lambda p, l: (p, l, 0, 0)),
        out_shape=jax.ShapeDtypeStruct((parts, local, ff, depth), BF16),
        compiler_params=params("parallel", "parallel"),
        cost_estimate=cost(0, weights.size * 6),
        name="pack_down",
    )(weights)


def unpack_down(grads):
    parts, local, ff, depth = grads.shape
    return pl.pallas_call(
        cast_kernel,
        grid=(parts, local),
        in_specs=[pl.BlockSpec((1, 1, ff, depth), lambda p, l: (p, l, 0, 0))],
        out_specs=pl.BlockSpec((1, ff, depth), lambda p, l: (l, p, 0)),
        out_shape=jax.ShapeDtypeStruct((local, parts * ff, depth), F32),
        compiler_params=params("parallel", "parallel"),
        cost_estimate=cost(0, grads.size * 6),
        name="unpack_down",
    )(grads)


def turn(values, cosine, sine):
    return values * cosine + pltpu.roll(values, HD // 2, 1) * sine


def att_fwd_kernel(
    place, q_in, kv, cos, sin, row_pos, row_seg, key_seg, *rest
):
    o_out, q_out = rest[-2:]
    query = turn(q_in[...], cos[...], sin[...]).astype(BF16)
    q_out[...] = query
    scores = gdot(query, kv[0, :, :HD], NT) * (1.0 / math.sqrt(HD))
    key_pos = lax.broadcasted_iota(jnp.int32, scores.shape, 1)
    allowed = (row_seg[...] == key_seg[...]) & (row_pos[...] >= key_pos)
    scores = jnp.where(allowed, scores, MASKED)
    peak = jnp.max(scores, 1, keepdims=True)
    weight = jnp.exp(scores - peak)
    mass = jnp.sum(weight, 1, keepdims=True)
    soft = (weight * (1.0 / mass)).astype(BF16)
    o_out[...] = dot(soft, kv[0, :, HD:]).astype(BF16)


def att_forward(place, q_raw, kv, cos, sin, row_pos, row_seg, key_seg, group, before):
    rows, feats = q_raw.shape
    seq, wide = kv.shape[1:]
    group_heads = wide // (2 * HD)
    block = min(256, rows)
    head = lambda h, i, place: (i, place[group] * group_heads + h)
    row = lambda h, i, place: (i, 0)
    in_specs = [
        pl.BlockSpec((block, HD), head),
        pl.BlockSpec((1, seq, 2 * HD), lambda h, i, place: (0, 0, h)),
        pl.BlockSpec((block, HD), row),
        pl.BlockSpec((block, HD), row),
        pl.BlockSpec((block, 1), row),
        pl.BlockSpec((block, 1), row),
        pl.BlockSpec((1, seq), lambda h, i, place: (0, 0)),
    ]
    operands = [place, q_raw, kv, cos, sin, row_pos, row_seg, key_seg]
    aliases = {}
    if before is not None:
        in_specs += [pl.BlockSpec(memory_space=pl.ANY)] * 2
        operands += list(before)
        aliases = {8: 0, 9: 1}
    return pl.pallas_call(
        att_fwd_kernel,
        grid_spec=pltpu.PrefetchScalarGridSpec(
            num_scalar_prefetch=1,
            grid=(group_heads, rows // block),
            in_specs=in_specs,
            out_specs=[pl.BlockSpec((block, HD), head)] * 2,
        ),
        out_shape=[jax.ShapeDtypeStruct((rows, feats), BF16)] * 2,
        input_output_aliases=aliases,
        compiler_params=params("arbitrary", "arbitrary"),
        cost_estimate=cost(40 * rows * seq * HD * group_heads, rows * feats * 4),
        name="attention_fwd",
    )(*operands)


def att_bwd_kernel(
    place, q_in, do_in, kv, cos, sin, key_cos, key_sin, row_pos, row_seg, key_seg, *rest
):
    dq_out, dkv_out, dk_sum, dv_sum = rest[-4:]
    step = pl.program_id(1)
    scale = 1.0 / math.sqrt(HD)
    query, grad_out = q_in[...], do_in[...]
    keys, values = kv[0, :, :HD], kv[0, :, HD:]
    scores = gdot(keys, query, NT) * scale
    key_pos = lax.broadcasted_iota(jnp.int32, scores.shape, 0)
    allowed = (row_seg[...] == key_seg[...]) & (row_pos[...] >= key_pos)
    scores = jnp.where(allowed, scores, MASKED)
    peak = jnp.max(scores, 0, keepdims=True)
    weight = jnp.exp(scores - peak)
    soft = weight * (1.0 / jnp.sum(weight, 0, keepdims=True))
    grad_soft = gdot(values, grad_out, NT)
    inner = jnp.sum(soft * grad_soft, 0, keepdims=True)
    grad_scores = (soft * (grad_soft - inner)).astype(BF16)
    grad_query = gdot(grad_scores, keys, TN) * scale
    dq_out[...] = turn(grad_query, cos[...], -sin[...]).astype(BF16)

    @pl.when(step == 0)
    def _():
        dk_sum[...] = jnp.zeros_like(dk_sum)
        dv_sum[...] = jnp.zeros_like(dv_sum)

    dk_sum[...] += dot(grad_scores, query)
    dv_sum[...] += dot(soft.astype(BF16), grad_out)

    @pl.when(step == pl.num_programs(1) - 1)
    def _():
        grad_keys = turn(dk_sum[...] * scale, key_cos[...], -key_sin[...])
        dkv_out[0, :, :HD] = grad_keys.astype(BF16)
        dkv_out[0, :, HD:] = dv_sum[...].astype(BF16)


def att_backward(
    place, query, grad_mixed, kv, cos, sin, key_cos, key_sin, row_pos, row_seg, key_seg,
    group, before,
):
    rows, feats = query.shape
    _, seq, wide = kv.shape
    group_heads = wide // (2 * HD)
    block = min(256, rows)
    head = lambda h, i, place: (i, place[group] * group_heads + h)
    row = lambda h, i, place: (i, 0)
    lane = lambda h, i, place: (0, i)
    whole = lambda h, i, place: (0, 0)
    pair = lambda h, i, place: (0, 0, h)
    in_specs = [
        pl.BlockSpec((block, HD), head),
        pl.BlockSpec((block, HD), head),
        pl.BlockSpec((1, seq, 2 * HD), pair),
        pl.BlockSpec((block, HD), row),
        pl.BlockSpec((block, HD), row),
        pl.BlockSpec((seq, HD), whole),
        pl.BlockSpec((seq, HD), whole),
        pl.BlockSpec((1, block), lane),
        pl.BlockSpec((1, block), lane),
        pl.BlockSpec((seq, 1), whole),
    ]
    operands = [
        place, query, grad_mixed, kv, cos, sin, key_cos, key_sin, row_pos, row_seg, key_seg
    ]
    aliases = {}
    if before is not None:
        in_specs.append(pl.BlockSpec(memory_space=pl.ANY))
        operands.append(before)
        aliases = {11: 0}
    return pl.pallas_call(
        att_bwd_kernel,
        grid_spec=pltpu.PrefetchScalarGridSpec(
            num_scalar_prefetch=1,
            grid=(group_heads, rows // block),
            in_specs=in_specs,
            out_specs=[
                pl.BlockSpec((block, HD), head),
                pl.BlockSpec((1, seq, 2 * HD), pair),
            ],
            scratch_shapes=[pltpu.VMEM((seq, HD), F32)] * 2,
        ),
        out_shape=[
            jax.ShapeDtypeStruct((rows, feats), BF16),
            jax.ShapeDtypeStruct((1, seq, wide), BF16),
        ],
        input_output_aliases=aliases,
        compiler_params=params("arbitrary", "arbitrary"),
        cost_estimate=cost(60 * rows * seq * HD * group_heads, rows * feats * 4),
        name="attention_bwd",
    )(*operands)


def raw_kernel(core, g_own, g_other, w_dn, out):
    columns = w_dn.shape[0]
    half, depth = columns // 2, w_dn.shape[2]
    total = jnp.zeros(out.shape, F32)
    for i in range(half):
        part = slice(i * depth, (i + 1) * depth)
        total += gdot(g_own[:, part], w_dn[core[0] * half + i], NT)
        total += gdot(g_other[:, part], w_dn[(1 - core[0]) * half + i], NT)
    out[...] = total


def hidden_raw(core, g_own, g_other, w_dn):
    rows, width = g_own.shape
    columns, ff, depth = w_dn.shape
    block = 256
    return pl.pallas_call(
        raw_kernel,
        grid_spec=pltpu.PrefetchScalarGridSpec(
            num_scalar_prefetch=1,
            grid=(rows // block,),
            in_specs=[
                pl.BlockSpec((block, width), lambda i, c: (i, 0)),
                pl.BlockSpec((block, width), lambda i, c: (i, 0)),
                pl.BlockSpec(
                    (columns, ff, depth), lambda i, c: (0, 0, 0), pipeline_mode=pl.Buffered(1)
                ),
            ],
            out_specs=pl.BlockSpec((block, ff), lambda i, c: (i, 0)),
        ),
        out_shape=jax.ShapeDtypeStruct((rows, ff), F32),
        compiler_params=params("arbitrary"),
        cost_estimate=cost(2 * w_dn.size * rows, w_dn.size * 2 + rows * ff * 4),
        name="hidden_raw",
    )(core, g_own, g_other, w_dn)


def ff_kernel(
    place, x_own, x_other, w_gate, w_up, raw, router, other, hid, hid_gated, du, dw, dgate
):
    core, expert = place[0], place[1]
    width = x_own.shape[1]
    mine = pl.ds(pl.multiple_of(core * width, width), width)
    theirs = pl.ds(pl.multiple_of((1 - core) * width, width), width)

    def product(weights):
        return dot(x_own[...], weights[mine, :]) + dot(x_other[...], weights[theirs, :])

    logits = product(router)
    lanes = lax.broadcasted_iota(jnp.int32, logits.shape, 1)
    own_logit = jnp.sum(jnp.where(lanes == expert, logits, 0.0), 1, keepdims=True)
    other_logit = jnp.sum(jnp.where(lanes == other[...], logits, 0.0), 1, keepdims=True)
    gate = jax.nn.sigmoid(own_logit - other_logit)
    gate_part, up_part = product(w_gate), product(w_up)
    sig = 1.0 / (1.0 + jnp.exp(-gate_part))
    silu = gate_part * sig
    hidden = silu * up_part
    hid[...] = hidden.astype(BF16)
    hid_gated[...] = (hidden * gate).astype(BF16)
    dgate[...] = jnp.sum(hidden * raw[...], 1, keepdims=True)
    grad_hidden = raw[...] * gate
    du[...] = (grad_hidden * up_part * (sig * (1.0 + gate_part * (1.0 - sig)))).astype(BF16)
    dw[...] = (grad_hidden * silu).astype(BF16)


def feed_forward(place, x_own, x_other, w_gate, w_up, raw, router, other):
    rows, width = x_own.shape
    ff = raw.shape[1]
    block = 256
    row = lambda i, c: (i, 0)
    whole = lambda i, c: (0, 0)
    fixed = lambda array: pl.BlockSpec(array.shape, whole, pipeline_mode=pl.Buffered(1))
    return pl.pallas_call(
        ff_kernel,
        grid_spec=pltpu.PrefetchScalarGridSpec(
            num_scalar_prefetch=1,
            grid=(rows // block,),
            in_specs=[
                pl.BlockSpec((block, width), row),
                pl.BlockSpec((block, width), row),
                fixed(w_gate),
                fixed(w_up),
                pl.BlockSpec((block, ff), row),
                fixed(router),
                pl.BlockSpec((block, 1), row),
            ],
            out_specs=[pl.BlockSpec((block, ff), row)] * 4 + [pl.BlockSpec((block, 1), row)],
        ),
        out_shape=[jax.ShapeDtypeStruct((rows, ff), BF16)] * 4
        + [jax.ShapeDtypeStruct((rows, 1), F32)],
        compiler_params=params("arbitrary"),
        cost_estimate=cost(5 * w_gate.size * rows, w_gate.size * 4 + rows * ff * 12),
        name="feed_forward",
    )(place, x_own, x_other, w_gate, w_up, raw, router, other)


def rows_kernel(count, which, *refs):
    out = refs[-1]
    total = None
    for lhs, weights in zip(refs[:count], refs[count : 2 * count]):
        if len(weights.shape) == 2:
            part = gdot(lhs[...], weights[...], NT)
        else:
            part = jnp.concatenate(
                [dot(lhs[...], weights[i]) for i in range(weights.shape[0])], 1
            )
        total = part if total is None else total + part
    if len(refs) > 2 * count + 1:
        total = total + refs[2 * count][...].astype(F32)
    out[...] = total.astype(BF16)


def rows_half(which, lhs, weights, width, add=None):
    rows = lhs[0].shape[0]
    block = 256
    row = lambda i, c: (i, 0)
    in_specs = [pl.BlockSpec((block, array.shape[1]), row) for array in lhs]
    for array in weights:
        if array.ndim == 2:
            shape, index = (width, array.shape[1]), lambda i, c: (c[0], 0)
        else:
            shape = (array.shape[0] // 2,) + array.shape[1:]
            index = lambda i, c: (c[0], 0, 0)
        in_specs.append(pl.BlockSpec(shape, index, pipeline_mode=pl.Buffered(1)))
    operands = [which, *lhs, *weights]
    if add is not None:
        in_specs.append(pl.BlockSpec((block, width), row))
        operands.append(add)
    return pl.pallas_call(
        functools.partial(rows_kernel, len(lhs)),
        grid_spec=pltpu.PrefetchScalarGridSpec(
            num_scalar_prefetch=1,
            grid=(rows // block,),
            in_specs=in_specs,
            out_specs=pl.BlockSpec((block, width), row),
        ),
        out_shape=jax.ShapeDtypeStruct((rows, width), BF16),
        compiler_params=params("arbitrary"),
        cost_estimate=cost(sum(array.size for array in weights) * rows, rows * width * 4),
        name="rows_half",
    )(*operands)


def gu_outer_kernel(sooner, core, x_own, x_other, *refs):
    out = refs[-1]
    half = pl.num_programs(0) // 2
    depth = x_own.shape[1]
    mine = (pl.program_id(0) // half) == core[0]

    def fill(rows):
        if sooner:
            du, dw = refs[0], refs[1]
            out[0, :depth] = gdot(rows[...], du[...], TN).astype(BF16)
            out[0, depth:] = gdot(rows[:, : depth // 2], dw[...], TN).astype(BF16)
        else:
            out[0] = gdot(rows[:, depth // 2 :], refs[0][...], TN).astype(BF16)

    @pl.when(mine)
    def _():
        fill(x_own)

    @pl.when(jnp.logical_not(mine))
    def _():
        fill(x_other)


def gu_outer(core, x_own, x_other, hidden_grads, columns):
    rows, width = x_own.shape
    half = columns // 2
    depth = width // half
    ff = hidden_grads[0].shape[1]
    sooner = len(hidden_grads) == 2
    height = 3 * depth // 2 if sooner else depth // 2
    part = lambda s, c: (0, lax.rem(s, half))
    fixed = pl.BlockSpec((rows, ff), lambda s, c: (0, 0), pipeline_mode=pl.Buffered(1))
    return pl.pallas_call(
        functools.partial(gu_outer_kernel, sooner),
        grid_spec=pltpu.PrefetchScalarGridSpec(
            num_scalar_prefetch=1,
            grid=(columns,),
            in_specs=[pl.BlockSpec((rows, depth), part)] * 2 + [fixed] * len(hidden_grads),
            out_specs=pl.BlockSpec((1, height, ff), lambda s, c: (s, 0, 0)),
        ),
        out_shape=jax.ShapeDtypeStruct((columns, height, ff), BF16),
        compiler_params=params("arbitrary"),
        cost_estimate=cost(2 * rows * columns * height * ff, rows * width * 8),
        name="grad_gateup",
    )(core, x_own, x_other, *hidden_grads)


def dn_outer_kernel(core, hid, g_own, g_other, out):
    half = pl.num_programs(0) // 2
    mine = (pl.program_id(0) // half) == core[0]

    @pl.when(mine)
    def _():
        out[0] = gdot(hid[...], g_own[...], TN).astype(BF16)

    @pl.when(jnp.logical_not(mine))
    def _():
        out[0] = gdot(hid[...], g_other[...], TN).astype(BF16)


def dn_outer(core, hid, g_own, g_other, columns):
    rows, width = g_own.shape
    half = columns // 2
    depth = width // half
    ff = hid.shape[1]
    part = lambda s, c: (0, lax.rem(s, half))
    return pl.pallas_call(
        dn_outer_kernel,
        grid_spec=pltpu.PrefetchScalarGridSpec(
            num_scalar_prefetch=1,
            grid=(columns,),
            in_specs=[
                pl.BlockSpec(hid.shape, lambda s, c: (0, 0), pipeline_mode=pl.Buffered(1)),
                pl.BlockSpec((rows, depth), part),
                pl.BlockSpec((rows, depth), part),
            ],
            out_specs=pl.BlockSpec((1, ff, depth), lambda s, c: (s, 0, 0)),
        ),
        out_shape=jax.ShapeDtypeStruct((columns, ff, depth), BF16),
        compiler_params=params("arbitrary"),
        cost_estimate=cost(2 * rows * 2 * width * ff, rows * width * 8),
        name="grad_down",
    )(core, hid, g_own, g_other)


def shards(
    tokens,
    norm_attn,
    norm_mlp,
    w_kv,
    router_attn,
    router_mlp,
    w_query,
    w_output,
    w_gateup,
    w_down,
    segments,
    att_routes,
    mlp_routes,
    cotangent,
):
    count, width = tokens.shape
    full_width = 2 * width
    planes = lax.axis_size("expert")
    columns = lax.axis_size("dp")
    plane = lax.axis_index("expert")
    column = lax.axis_index("dp")
    core = lax.axis_index("tensor")
    n_att = router_attn.shape[1]
    n_mlp = router_mlp.shape[1]
    local_att = w_query.shape[0]
    local_mlp = w_gateup.shape[0]
    ff_parts = columns // local_mlp
    depth = w_gateup.shape[1]
    ff = w_gateup.shape[3] // ff_parts
    cap = 3 * count // 8
    seq = planes * count
    feats = w_query.shape[2]
    kv_part = feats // planes
    part_heads = kv_part // HD
    own_local = column % local_mlp
    mlp_expert = plane * local_mlp + own_local
    steps = jnp.arange(planes, dtype=jnp.int32)
    source_planes = (plane + steps) % planes
    target_planes = (plane - steps + planes) % planes
    near_local = own_local ^ jnp.arange(local_mlp, dtype=jnp.int32)
    core_at = core.astype(jnp.int32)[None]
    other_at = 1 - core_at

    def absolute(blocks):
        twice = jnp.concatenate([blocks, blocks], 0)
        return lax.dynamic_slice_in_dim(twice, (planes - plane) % planes, planes, 0)

    def relative(blocks):
        twice = jnp.concatenate([blocks, blocks], 0)
        return lax.dynamic_slice_in_dim(twice, plane, planes, 0)

    def relative_down(blocks):
        twice = jnp.concatenate([blocks[::-1], blocks[::-1]], 0)
        return lax.dynamic_slice_in_dim(twice, planes - 1 - plane, planes, 0)

    kv_send = w_kv.astype(BF16).reshape(w_kv.shape[0], 2, planes, part_heads, HD)
    near_tokens = near_planes(tokens)
    kv_send = absolute(jnp.stack(shift(list(relative_down(kv_send.transpose(2, 0, 3, 1, 4))), -1), 0))
    w_kv_part = lax.all_gather(kv_send, "dp", axis=0, tiled=True).reshape(
        full_width, 2 * kv_part
    )
    whole_query = lax.all_gather(
        after(w_query.astype(BF16), kv_send), "dp", axis=1, tiled=True
    )
    whole_output = lax.all_gather(w_output.astype(BF16), "dp", axis=2, tiled=True)
    down_send = pack_down(w_down, ff_parts).reshape(columns, ff, depth)
    gate_send, up_send = pack_gateup(w_gateup, ff_parts)
    w_dn = a2a(down_send, "dp")
    w_gate = a2a(gate_send.reshape(columns, depth, ff), "dp").reshape(full_width, ff)
    w_up = a2a(up_send.reshape(columns, depth, ff), "dp").reshape(full_width, ff)

    ints = jnp.concatenate(
        [
            segments[None],
            att_routes.T,
            mlp_routes.T,
            jnp.zeros((3, count), jnp.int32),
        ],
        0,
    )
    near_ints = jnp.stack(near_planes(ints), 0)[None]
    step = 1
    while step < columns:
        pairs = [(i, i ^ step) for i in range(columns)]
        near_ints = jnp.concatenate([near_ints, lax.ppermute(near_ints, "dp", pairs)], 0)
        step *= 2

    residual = tokens.astype(F32)
    near_tokens[-1] = after(near_tokens[-1], down_send, gate_send, up_send)
    seq_res = jnp.concatenate(near_tokens, 0).astype(F32)

    def rms_scale(values):
        return lax.rsqrt(
            core_sum(jnp.sum(values * values, 1, keepdims=True)) / full_width + EPSILON
        )

    seq_scale = rms_scale(seq_res)
    seq_a_half = (seq_res * seq_scale * norm_attn).astype(BF16)
    scale_a = seq_scale[:count]
    rows_a_half = seq_a_half[:count]
    seq_a = both_halves(seq_a_half, core)

    def angles_of(positions):
        frequency = jnp.exp(
            jnp.arange(HD // 2, dtype=F32) * (-2.0 * math.log(10000.0) / HD)
        )
        angle = positions.astype(F32)[:, None] * frequency[None, :]
        cosine, sine = jnp.cos(angle), jnp.sin(angle)
        return jnp.concatenate([cosine, cosine], 1), jnp.concatenate([-sine, sine], 1)

    seq_pos = jnp.arange(seq, dtype=jnp.int32)
    cos_seq, sin_seq = angles_of(seq_pos)
    near_pos = source_planes[:, None] * count + jnp.arange(count, dtype=jnp.int32)[None]
    cos_near, sin_near = angles_of(near_pos.reshape(-1))
    kv_raw = dot(seq_a, w_kv_part).reshape(seq, part_heads, 2, HD)
    keys = kv_raw[:, :, 0]
    turned = jnp.concatenate([keys[..., HD // 2 :], keys[..., : HD // 2]], -1)
    keys = keys * cos_near[:, None] + turned * sin_near[:, None]
    kv_mine = jnp.stack([keys.astype(BF16), kv_raw[:, :, 1].astype(BF16)], 2)
    kv_mine = absolute(kv_mine.reshape(planes, count, 2 * kv_part)).reshape(seq, 2 * kv_part)
    kv_near = relay(kv_mine, "expert", w_dn)

    seq_ints = near_ints[0]
    own_att = jnp.arange(local_att, dtype=jnp.int32) + plane * local_att
    att_ids = (target_planes[:, None] * local_att + jnp.arange(local_att)[None]).reshape(-1)
    mlp_ids = (target_planes[:, None] * local_mlp + near_local[None]).reshape(-1)
    att_slots = one_hot_slots(seq_ints[:, 1:3], own_att, cap)
    home_att = one_hot_slots(ints[None, 1:3], att_ids, cap)[0]
    home_mlp = one_hot_slots(ints[None, 3:5], mlp_ids, cap)[0]
    every_mlp = near_ints[:, :, 3:5].reshape(-1, 2, count)
    mlp_slots = one_hot_slots(every_mlp, mlp_expert[None], cap)[:, 0]
    other_expert = jnp.sum(every_mlp, 1) - mlp_expert
    row_other = jnp.sum(jnp.where(mlp_slots, other_expert[:, None, :], 0), -1).reshape(-1, 1)

    def by_choice(home, routes, ids):
        named = routes[:, None, :] == ids[None, :, None]
        picks = home[None] & named[:, :, None, :]
        return picks.astype(BF16).reshape(2, -1, count)

    pick_att = by_choice(home_att, ints[1:3], att_ids)
    pick_mlp = by_choice(home_mlp, ints[3:5], mlp_ids)
    flat_mlp = home_mlp.astype(BF16).reshape(n_mlp * cap, count)
    spread = att_slots.astype(BF16)
    row_pos = jnp.sum(
        jnp.where(att_slots, near_pos[:, None, None, :], 0), -1
    ).transpose(1, 0, 2).reshape(-1)
    row_seg = jnp.sum(
        jnp.where(att_slots, seq_ints[:, 0][:, None, None, :], 0), -1
    ).transpose(1, 0, 2).reshape(-1)
    seq_seg = absolute(seq_ints[:, 0]).reshape(seq)
    att_rows = planes * local_att * cap

    def to_plane(rows_half):
        return shift(list(rows_half.reshape(planes, local_mlp, cap, width)), -1)

    def to_expert(held, early=(), late=()):
        held[-1] = after(held[-1], *early)
        held = jnp.stack(held, 1)
        sent = [held[k % local_mlp].reshape(planes * cap, width) for k in range(columns)]
        got = cross(sent)
        got[-1] = after(got[-1], *late)
        own = jnp.concatenate(got, 0)
        return own, swap(own)

    g_held = to_plane(dot(flat_mlp, after(cotangent, kv_near[1], kv_near[-1])).astype(BF16))

    def gates_of(half_rows, router, routes):
        part = lax.dynamic_slice_in_dim(router, core * width, width, 0).astype(BF16)
        logits = core_sum(ein("de,td->et", part, half_rows))
        experts = router.shape[1]
        named = (
            routes[:, None, :] == jnp.arange(experts, dtype=jnp.int32)[None, :, None]
        ).astype(F32)
        chosen = jnp.sum(named * logits[None], 1)
        return jax.nn.softmax(chosen, axis=0), named, part

    gates_a, named_a, router_a = gates_of(rows_a_half, router_attn, ints[1:3])
    held_a = ein("slct,std->lscd", spread, seq_a.reshape(planes, count, full_width)).astype(BF16)
    held_a = held_a.reshape(local_att, planes * cap, full_width)
    cos_rows, sin_rows = angles_of(row_pos)
    query_raw = ein("lrd,ldf->lrf", held_a, whole_query).reshape(att_rows, feats)
    before = None
    order = [0, planes // 2] + [j for j in range(1, planes) if j != planes // 2]
    for j in order:
        if j == order[-2]:
            kv_near[j] = after(kv_near[j], *g_held[1:])
        before = att_forward(
            source_planes, query_raw, kv_near[j][None], cos_rows, sin_rows,
            row_pos[:, None], row_seg[:, None], seq_seg[None], j, before,
        )
    mixed_rows, query_rows = before
    mixed_rows = after(mixed_rows, w_gate)
    mixed_owner = mixed_rows.reshape(local_att, planes * cap, feats)

    def halves(values, axis):
        mine = lax.dynamic_slice_in_dim(values, core * width, width, axis)
        theirs = lax.dynamic_slice_in_dim(values, (1 - core) * width, width, axis)
        return mine, theirs

    out_mine, out_theirs = halves(whole_output, 2)
    given = swap(ein("lrf,lfd->lrd", mixed_owner, out_theirs).astype(BF16))
    branch_a = ein("lrf,lfd->lrd", mixed_owner, out_mine) + given.astype(F32)
    branch_a = branch_a.astype(BF16).reshape(local_att, planes, cap, width)
    home_a = shift([branch_a[:, j].reshape(local_att * cap, width) for j in range(planes)], 1)
    home_a = jnp.concatenate(home_a, 0)
    taken_a = ein("jst,sd->jtd", pick_att, home_a)
    middle = residual + jnp.sum(gates_a[:, :, None] * taken_a, 0)

    scale_b = rms_scale(middle)
    rows_b_half = (middle * scale_b * norm_mlp).astype(BF16)
    gates_b, named_b, router_b = gates_of(rows_b_half, router_mlp, ints[3:5])
    x_held = to_plane(dot(flat_mlp, rows_b_half).astype(BF16))
    g_own, g_other = to_expert(g_held, (), tuple(x_held[1:]))
    raw = hidden_raw(core_at, g_own, g_other, w_dn)
    x_own, x_other = to_expert(x_held, (w_up,), (raw,))
    router_wide = jnp.pad(router_mlp.astype(BF16), ((0, 0), (0, HD - n_mlp)))
    place = jnp.stack([core, mlp_expert]).astype(jnp.int32)
    hidden, hidden_gated, grad_gate, grad_up, row_dgate = feed_forward(
        place, x_own, x_other, w_gate, w_up, raw, router_wide, row_other
    )

    def over_parts(rows, *done):
        tail = rows.shape[1:]
        got = cross(list(rows.reshape((columns, planes, cap) + tail)))
        if done:
            got = list(lax.optimization_barrier(tuple(got) + done)[:columns])
        there = got[1:]
        sums = []
        for near in range(local_mlp):
            parts = [got[k].astype(F32) for k in range(near, columns, local_mlp)]
            sums.append(functools.reduce(jnp.add, parts).astype(rows.dtype))
        return [jnp.concatenate([part[j] for part in sums], 0) for j in range(planes)], there

    def mlp_home(blocks, *done):
        back = shift(blocks, 1)
        there = back[1:]
        back[-1] = after(back[-1], *done)
        return jnp.concatenate(back, 0), there

    dgate_blocks, dgate_there = over_parts(core_sum(row_dgate[:, 0]))
    dgate_home, dgate_back = mlp_home(dgate_blocks)
    branch_theirs = rows_half(other_at, (hidden,), (w_dn,), width)
    given = swap(branch_theirs)
    grad_wgate = gu_outer(
        core_at, x_own, x_other, (after(grad_gate, branch_theirs), grad_up), columns
    )
    branch_b = rows_half(core_at, (after(hidden, grad_wgate, *dgate_there),), (w_dn,), width, given)
    grad_pair = (after(grad_gate, branch_b, *dgate_back), grad_up)
    given = swap(rows_half(other_at, grad_pair, (w_gate, w_up), width))
    db_rows = rows_half(core_at, grad_pair, (w_gate, w_up), width, given)
    grad_wup = gu_outer(core_at, x_own, x_other, (after(grad_up, db_rows),), columns)
    branch_blocks, _ = over_parts(branch_b, grad_wup)
    home_b, branch_back = mlp_home(branch_blocks)
    grad_wdn = dn_outer(core_at, after(hidden_gated, grad_wup), g_own, g_other, columns)
    db_blocks, db_there = over_parts(db_rows, grad_wdn, *branch_back)
    home_db, _ = mlp_home(db_blocks)
    got_gate = a2a(after(grad_wgate, *db_there), "dp")
    got_up = a2a(grad_wup, "dp")
    got_dn = a2a(grad_wdn, "dp")

    def gates_back(gates, grad_gates, named):
        chosen = gates * (grad_gates - jnp.sum(gates * grad_gates, 0, keepdims=True))
        return jnp.sum(chosen[:, None, :] * named, 0).astype(BF16)

    grad_gates_b = jnp.sum(pick_mlp.astype(F32) * dgate_home[None, :, None], 1)
    grad_logit_b = gates_back(gates_b, grad_gates_b, named_b)
    grad_normed_b = ein("st,sd->td", flat_mlp, home_db) + ein("et,de->td", grad_logit_b, router_b)
    grad_router_b = ein("et,td->ed", grad_logit_b, rows_b_half)

    def normalize_back(values, gain, row_scale, grad_normed):
        inner = core_sum(jnp.sum(grad_normed * gain * values, 1, keepdims=True))
        grad_values = (
            row_scale * gain * grad_normed
            - values * (row_scale * row_scale * row_scale) * inner / full_width
        )
        return grad_values, jnp.sum(grad_normed * values * row_scale, 0)

    grad_out = cotangent.astype(F32)
    grad_mid_norm, grad_gain_b = normalize_back(middle, norm_mlp, scale_b, grad_normed_b)
    grad_middle = grad_out + grad_mid_norm

    grad_gates_a = core_sum(jnp.sum(grad_middle[None] * taken_a, 2))
    grad_logit_a = gates_back(gates_a, grad_gates_a, named_a)
    grad_taken_a = (gates_a[:, :, None] * grad_middle[None]).astype(BF16)
    sent_a = ein("jst,jtd->sd", pick_att, grad_taken_a).astype(BF16)
    got_a = shift(list(sent_a.reshape(planes, local_att, cap, width)), -1)
    got_a[-1] = after(got_a[-1], got_gate)
    held_grad_a = both_halves(
        jnp.stack(got_a, 1).reshape(local_att, planes * cap, width), core
    )
    grad_mixed = ein("lrd,lfd->lrf", held_grad_a, whole_output).astype(BF16)
    grad_wo = ein("lrf,lrd->lfd", mixed_owner, held_grad_a).astype(BF16)
    grad_woutput = lax.psum_scatter(grad_wo, "dp", scatter_dimension=2, tiled=True).astype(F32)
    grad_query = None
    sent_kv = [None] * planes
    for j in [planes // 2] + [j for j in range(1, planes) if j != planes // 2] + [0]:
        if j == 1:
            grad_query = after(grad_query, grad_wo)
        grad_query, grad_kv_group = att_backward(
            source_planes, query_rows, grad_mixed.reshape(att_rows, feats), kv_near[j][None],
            cos_rows, sin_rows, cos_seq, sin_seq, row_pos[None], row_seg[None],
            seq_seg[:, None], j, grad_query,
        )
        sent_kv[j] = grad_kv_group[0]
    grad_query = grad_query.reshape(local_att, planes * cap, feats)
    got_kv = shift(sent_kv, 1)
    grad_wq = ein(
        "lrd,lrf->ldf", after(held_a, got_kv[planes // 2], got_up), grad_query
    ).astype(BF16)
    taken_b = ein("jst,sd->jtd", pick_mlp, home_b)
    output = (middle + jnp.sum(gates_b[:, :, None] * taken_b, 0)).astype(BF16)
    got_kv[0] = after(got_kv[0], grad_wq, grad_woutput)
    grad_kv = functools.reduce(jnp.add, [part.astype(F32) for part in got_kv]).astype(BF16)
    grad_kv = relative(grad_kv.reshape(planes, count, 2 * kv_part)).reshape(seq, 2 * kv_part)
    grad_wquery = lax.psum_scatter(grad_wq, "dp", scatter_dimension=1, tiled=True)
    query_mine, query_theirs = halves(whole_query, 1)
    kvw_mine, kvw_theirs = halves(w_kv_part, 0)

    def grad_seq(query_half, kv_half, done):
        rows = ein("lrf,ldf->lrd", after(grad_query, done), query_half).astype(BF16)
        rows = ein("slct,lscd->std", spread, rows.reshape(local_att, planes, cap, width))
        return rows.reshape(seq, width) + ein("tf,df->td", grad_kv, kv_half)

    given = swap(grad_seq(query_theirs, kvw_theirs, got_kv[1]).astype(BF16))
    grad_seq_a = (grad_seq(query_mine, kvw_mine, got_kv[-1]) + given.astype(F32)).astype(BF16)
    grad_wgateup = unpack_gateup(
        after(got_gate, grad_kv).reshape(ff_parts, local_mlp, 3 * depth // 2, ff),
        got_up.reshape(ff_parts, local_mlp, depth // 2, ff),
    )
    grad_wdown = unpack_down(got_dn.reshape(ff_parts, local_mlp, ff, depth))
    grad_kv_w = a2a(ein("td,tf->df", seq_a, grad_kv).astype(BF16), "dp")
    grad_kv_w = jnp.sum(
        grad_kv_w.reshape(columns, full_width // columns, 2 * kv_part).astype(F32), 0
    ).astype(BF16)
    grad_kv_w = a2a(
        grad_kv_w.reshape(planes, w_kv.shape[0], part_heads, 2, HD), "expert"
    )
    grad_wkv = grad_kv_w.transpose(1, 3, 0, 2, 4).astype(F32).reshape(w_kv.shape)
    back_a = shift(list(grad_seq_a.reshape(planes, count, width)), 1)
    back_a[0] = after(back_a[0], grad_wgateup, grad_wdown)
    grad_rows_a = functools.reduce(jnp.add, [part.astype(F32) for part in back_a])
    grad_normed_a = grad_rows_a + ein("et,de->td", grad_logit_a, router_a)
    grad_router_a = ein("et,td->ed", grad_logit_a, rows_a_half)
    grad_in_norm, grad_gain_a = normalize_back(residual, norm_attn, scale_a, grad_normed_a)
    grad_tokens = grad_middle + grad_in_norm

    small = jnp.concatenate(
        [grad_router_a, grad_router_b, grad_gain_a[None], grad_gain_b[None]], 0
    )
    small = total_over(total_over(small, "dp"), "expert")
    grad_wquery = after(grad_wquery, small).astype(F32)
    routers = both_halves(small[: n_att + n_mlp], core)
    return (
        output,
        grad_tokens,
        small[n_att + n_mlp],
        small[n_att + n_mlp + 1],
        grad_wkv,
        routers[:n_att].T,
        routers[n_att:].T,
        grad_wquery,
        grad_woutput,
        grad_wgateup,
        grad_wdown,
    )


def solution(mesh):
    in_specs = (
        P(("dp", "expert"), "tensor"),
        P("tensor"),
        P("tensor"),
        P(("dp", "expert"), None, "tensor"),
        P(),
        P(),
        P("expert", "dp", "tensor"),
        P("expert", "tensor", "dp"),
        P("expert", "dp", None, "tensor"),
        P("expert", "tensor", "dp"),
        P(("dp", "expert")),
        P(("dp", "expert"), None),
        P(("dp", "expert"), None),
        P(("dp", "expert"), "tensor"),
    )
    out_specs = (
        P(("dp", "expert"), "tensor"),
        P(("dp", "expert"), "tensor"),
        P("tensor"),
        P("tensor"),
        P(("dp", "expert"), None, "tensor"),
        P(),
        P(),
        P("expert", "dp", "tensor"),
        P("expert", "tensor", "dp"),
        P("expert", "dp", None, "tensor"),
        P("expert", "tensor", "dp"),
    )
    return jax.shard_map(shards, mesh=mesh, in_specs=in_specs, out_specs=out_specs, check_vma=False)
```
